128 devices in a mesh: pool: 4 (over x), fib: 32 (over y, z, core).
Axes of the slice: x: 4, y: 4, z: 4, core: 2. Of those that a mesh axis runs over, the one named last changes fastest.
Arguments:
- vm_state: float32 [32768, 1536], P(('pool', 'fib')), may hold values from -4 to 4
- recovery: float32 [32768, 1536], P(('pool', 'fib')), may hold values from -3 to 3
- spike_record_matrix: int32 [256, 4], P(('pool', 'fib')), may hold values 0 or 1
- muscle_cell_owner_number: int32 [32768], P(('pool', 'fib')), may hold values from 0 to 63
- junction: int32 [32768], P(('pool', 'fib')), may hold values from 576 to 959
- column_index: int32 [32768, 12], P(('pool', 'fib')), may hold values from 0 to 255, all different within a row; in each aligned block of 256 rows (0 to 255, 256 to 511, ...) at most 16 rows name the same one
- cable_inverse: float32 [1536, 1536], replicated, may hold values from 0 to 0.6, as said below
- reaction: float32 [128, 8, 1536], P('fib', 'pool'), may hold values from 0.1 to 2
- potential: float32 [128, 8, 1536], P('fib', 'pool'), may hold values from -3 to 3
Outputs:
- membrane: float32 [32768, 1536], P(('pool', 'fib'))
- recovering: float32 [32768, 1536], P(('pool', 'fib'))
- extracell: float32 [128, 8, 1536], P('fib', 'pool')
The draws below stay inside these ranges and needn't reach their ends.
Inputs may be any that keep to these rules, and one draw needn't show every extreme that they name: cable_inverse is symmetric with positive entries. `column_index`: the blocks of one fibre lie in distinct columns of its slab, and among the fibres of one device no column holds more than 16 blocks.
All inputs are finite; a program needn't handle non-finite values. No bound on the sum of `spike_record_matrix` on one device may be relied on, other than what follows from the above.
Results may differ from the reference program's by a relative error of at most 0.0001.
Values sent between devices are 32-bit elements; how exact they have to be, the bound alone decides.
No kernel may reach another device: no remote copies, remote signals or barrier semaphores. Data moves between devices by JAX's collectives and lax.ppermute only.
A program may use at most 128 MiB of HBM per device.

```python
import math
import jax
import jax.numpy as jnp
import numpy as np
from jax import lax

PTS = 1536
NBLK = 12
FIB_DEV = 256
FIBRES = 32768
MU_POOL = 64
MUS = 256
STEPS = 4
SWEEPS = 4
GX = 8
GY = 128
SLAB_COLS = 256
CAP = 16
N_POOL = 4


def draw_cable_inverse(key, part):
    ratio_key = jax.random.fold_in(key, 11)
    share_key = jax.random.fold_in(key, 12)
    entry_key = jax.random.fold_in(key, 13)
    cable_ratio = jnp.exp(jax.random.uniform(ratio_key, (), jnp.float32, jnp.log(0.5), jnp.log(4.0)))
    far_share = jax.random.uniform(share_key, (), jnp.float32, 0.2, 0.3)
    spread_entries = jax.random.uniform(entry_key, (PTS, PTS), jnp.float32, 0.0, 2.0)
    far_part = (spread_entries + spread_entries.T) / (2.0 * PTS)
    half_root = jnp.sqrt(0.25 / cable_ratio)
    decay_rate = 2.0 * jnp.log(half_root + jnp.sqrt(half_root * half_root + 1.0))
    index_row = jnp.arange(PTS, dtype=jnp.float32)[:, None]
    index_col = jnp.arange(PTS, dtype=jnp.float32)[None, :]
    nearer = jnp.minimum(index_row, index_col)
    farther = jnp.maximum(index_row, index_col)
    length = float(PTS)
    numer = jnp.exp(-jnp.abs(index_row - index_col) * decay_rate)
    numer = numer * (1.0 - jnp.exp(-2.0 * (nearer + 1.0) * decay_rate))
    numer = numer * (1.0 - jnp.exp(-2.0 * (length - farther) * decay_rate))
    denom = 2.0 * jnp.sinh(decay_rate) * (1.0 - jnp.exp(-2.0 * (length + 1.0) * decay_rate)) * cable_ratio
    green = numer / denom
    return ((1.0 - far_share) * green + far_share * far_part).astype(jnp.float32)


def with_ends(drawn, key, smallest, largest):
    index_at = [jax.random.randint(jax.random.fold_in(key, axis), (), 0, length) for axis, length in enumerate(drawn.shape)]
    main_axis = drawn.shape.index(max(drawn.shape))
    beside = index_at[:main_axis] + [(index_at[main_axis] + 1) % drawn.shape[main_axis]] + index_at[main_axis + 1:]
    return drawn.at[tuple(index_at)].set(smallest).at[tuple(beside)].set(largest)


def levels(stream_key, shape, shards, low, top_value):
    factor_of, own = 1.0, jax.random.fold_in(stream_key, 6)
    for dim, parts in shards:
        steps = jnp.exp(jax.random.uniform(jax.random.fold_in(own, dim), (parts,), jnp.float32, low / len(shards), top_value / len(shards)))
        factor_of = factor_of * jnp.repeat(steps, shape[dim] // parts).reshape([-1 if axis == dim else 1 for axis in range(len(shape))])
    return factor_of


def rank_bounds(amount, lean):
    weights = [(1 << 20) // math.isqrt(grade ** lean) + 1 for grade in range(1, amount + 1)]
    deviation = 1 + sum(weights) // (1 << 30)
    return np.cumsum(np.array([max(1, weight // deviation) for weight in weights]))


def ranked(stream_key, dims, number_of, slope):
    grid = rank_bounds(number_of, slope)
    lot = jax.random.randint(jax.random.fold_in(stream_key, 1), dims, 0, int(grid[number_of - 1]))
    grade = jnp.searchsorted(jnp.asarray(grid, jnp.int32), lot, side="right")
    return jax.random.permutation(jax.random.fold_in(stream_key, 2), number_of)[grade].astype(jnp.int32)


def assign_block(stream_key, own, number, rows, amount, top, limit, skew):
    ranking = jax.random.permutation(stream_key, amount)
    packed, common = shares(amount, rows * top, limit, skew, True), shares(amount, rows * top, limit, skew, False)
    places = jnp.arange(amount)

    def named(tallies, offset_by):
        used = int((tallies > 0).sum())
        fixed = max(1, used // 4)
        shifted = fixed + (places - fixed + offset_by * (used - fixed)) % max(1, amount - fixed)
        return jnp.zeros((amount,), jnp.int32).at[ranking[jnp.where(places < fixed, places, shifted)]].set(jnp.asarray(tallies, jnp.int32))

    tallies = jnp.where(number % 4 == 0, named(packed, number // 4), named(common, number - number // 4 - 1))
    mixed = jax.random.permutation(jax.random.fold_in(own, 3), amount)
    giver, receiver = mixed[0:amount // 2 * 2:2], mixed[1:amount // 2 * 2:2]
    room = jnp.minimum(tallies[giver] - 1, limit - tallies[receiver]) // 2
    room = jnp.where((giver == ranking[0]) | (receiver == ranking[0]) | (tallies[receiver] == 0), 0, jnp.maximum(room, 0))
    shifted = jax.random.randint(jax.random.fold_in(own, 4), (amount // 2,), 0, 1 << 20) % (room + 1)
    tallies = tallies.at[giver].add(-shifted).at[receiver].add(shifted)
    members = jnp.searchsorted(jnp.cumsum(tallies), jnp.arange(rows * top), side="right").astype(jnp.int32)
    listing = members.reshape(top, rows).T
    listing = listing[jax.random.permutation(jax.random.fold_in(own, 1), rows)]
    offset_by = jax.random.randint(jax.random.fold_in(own, 2), (rows, 1), 0, top)
    return jnp.take_along_axis(listing, (jnp.arange(top)[None, :] + offset_by) % top, axis=1)


def shares(amount, total, most, skew, full):
    portions = [(1 << 20) // math.isqrt(standing ** skew) + 1 for standing in range(1, amount + 1)]
    largest = most if full else min(most, max(-(-total // amount), total * portions[0] // sum(portions)))
    least = 1 if total - largest >= amount - 1 else 0
    given, rest = [largest] + [least] * (amount - 1), total - largest - least * (amount - 1)
    while rest > 0:
        movable = [i for i in range(1, amount) if given[i] < largest] or [i for i in range(1, amount) if given[i] < most]
        pool, left = sum([portions[i] for i in movable]), rest
        for i in movable:
            more = min(most - given[i], max(1, left * portions[i] // pool), rest)
            given[i] = given[i] + more
            rest = rest - more
    return np.array(given)


def noise(stream_key, shape, scale, reach, pieces=(), held_as=jnp.bfloat16):
    values = jax.random.normal(stream_key, shape, jnp.float32) * scale
    if len(pieces) > 0:
        values = levels(stream_key, shape, pieces, -0.22, 0.18) * values
    return jnp.clip(values, min=-reach, max=reach).astype(held_as)


def setup_inputs(seed: int = 0) -> dict:
    key_list = jax.random.split(jax.random.key(seed), 10)
    vm_state = noise(key_list[0], (FIBRES, PTS), 1.0, 4.0, ((0, 128),), jnp.float32)
    recovery = noise(key_list[1], (FIBRES, PTS), 0.5, 3.0, ((0, 128),), jnp.float32)
    spike_record_matrix = with_ends((jax.random.randint(key_list[2], (MUS, STEPS), 0, 4) < 3).astype(jnp.int32), jax.random.fold_in(key_list[2], 1), 0, 1)
    muscle_cell_owner_number = with_ends(ranked(key_list[3], (FIBRES,), MU_POOL, 2), jax.random.fold_in(key_list[3], 3), 0, MU_POOL - 1).astype(jnp.int32)
    junction = with_ends(jax.random.randint(key_list[4], (FIBRES,), PTS // 2 - PTS // 8, PTS // 2 + PTS // 8), jax.random.fold_in(key_list[4], 1), PTS // 2 - PTS // 8, (PTS // 2 + PTS // 8) - 1).astype(jnp.int32)
    column_index_keys = jax.random.split(jax.random.fold_in(key_list[5], 1), FIBRES // FIB_DEV)
    column_index_turns = jax.random.permutation(jax.random.fold_in(key_list[5], 3), FIBRES // FIB_DEV)
    column_index = jax.vmap(lambda own, number: assign_block(jax.random.fold_in(key_list[5], 2), own, number, FIB_DEV, SLAB_COLS, NBLK, CAP, 0))(column_index_keys, column_index_turns).reshape((FIBRES, NBLK))
    cable_inverse = draw_cable_inverse(jax.random.fold_in(key_list[9], 71), 0)
    reaction = jnp.clip(jnp.exp(math.log(2.0) - 2.9957323 * jax.random.uniform(key_list[7], (GY, GX, PTS), jnp.float32) ** levels(key_list[7], (GY, GX, PTS), ((0, 32), (1, 4)), -0.2, 0.2)), 0.1, 2.0)
    potential = noise(key_list[8], (GY, GX, PTS), 0.5, 3.0, ((0, 32), (1, 4)), jnp.float32)
    return dict(vm_state=vm_state, recovery=recovery, spike_record_matrix=spike_record_matrix, muscle_cell_owner_number=muscle_cell_owner_number, junction=junction, column_index=column_index, cable_inverse=cable_inverse, reaction=reaction, potential=potential)


TIME_STEP = 0.05
RECOVERY_RATE = 0.5
RECOVERY_SHIFT = 0.7
RECOVERY_SLOPE = 0.8
STIMULUS_GAIN = 4.0
JUNCTION_SPREAD = 8.0
SOURCE_GAIN = 0.25
RELAX_WEIGHT = 0.8


def stencil(extracell, source, diagonal):
    padded = jnp.pad(extracell, 1)
    neighbours = padded[2:, 1:-1, 1:-1] + padded[:-2, 1:-1, 1:-1]
    neighbours = neighbours + padded[1:-1, 2:, 1:-1] + padded[1:-1, :-2, 1:-1]
    neighbours = neighbours + padded[1:-1, 1:-1, 2:] + padded[1:-1, 1:-1, :-2]
    return (1.0 - RELAX_WEIGHT) * extracell + RELAX_WEIGHT * (source + neighbours) / diagonal


def reference(vm_state, recovery, spike_record_matrix, muscle_cell_owner_number, junction, column_index, cable_inverse, reaction, potential):
    fibres, points = vm_state.shape
    blocks = column_index.shape[1]
    block_len = points // blocks
    grid_first, grid_second = potential.shape[0], potential.shape[1]
    slab_second = grid_second // N_POOL
    per_pool = fibres // N_POOL
    neuron_group_members = spike_record_matrix.shape[0] // N_POOL
    group_member_table = jnp.arange(fibres, dtype=jnp.int32) // per_pool
    spike_sequence = spike_record_matrix[group_member_table * neuron_group_members + muscle_cell_owner_number].astype(jnp.float32)
    position = jnp.arange(points, dtype=jnp.int32).astype(jnp.float32)
    offsets = (position[None, :] - junction[:, None].astype(jnp.float32)) / JUNCTION_SPREAD
    drive_waveform = STIMULUS_GAIN * jnp.exp(-offsets * offsets)
    grid_rows = (column_index // slab_second) * grid_second + group_member_table[:, None] * slab_second + column_index % slab_second
    block_ids = jnp.arange(blocks, dtype=jnp.int32)[None, :]
    diagonal = 6.0 + reaction
    extracell = potential
    membrane = vm_state
    recovering = recovery
    for clock_tick_counter in range(STEPS):
        ionic_term = membrane - membrane * membrane * membrane / 3.0 - recovering
        injected_drive = spike_sequence[:, clock_tick_counter][:, None] * drive_waveform
        current = ionic_term + injected_drive
        sampled = extracell.reshape(grid_first * grid_second, blocks, block_len)
        at_fibre = sampled[grid_rows, block_ids].reshape(fibres, points)
        right_side = membrane + TIME_STEP * (current + at_fibre)
        recovering = recovering + TIME_STEP * RECOVERY_RATE * (membrane + RECOVERY_SHIFT - RECOVERY_SLOPE * recovering)
        membrane = jnp.dot(right_side, cable_inverse, precision=lax.Precision.HIGHEST, preferred_element_type=jnp.float32)
        deposit = jnp.zeros((grid_first * grid_second, blocks, block_len), jnp.float32)
        deposit = deposit.at[grid_rows, block_ids].add(current.reshape(fibres, blocks, block_len))
        source = SOURCE_GAIN * deposit.reshape(grid_first, grid_second, points)
        for sweep_index in range(SWEEPS):
            extracell = stencil(extracell, source, diagonal)
    return membrane, recovering, extracell
```

```python
import functools

import jax
import jax.numpy as jnp
from jax import lax
from jax.experimental import pallas as pl
from jax.experimental.pallas import tpu as pltpu
from jax.sharding import PartitionSpec as P

STEPS = 4
SWEEPS = 4
TIME_STEP = 0.05
RECOVERY_RATE = 0.5
RECOVERY_SHIFT = 0.7
RECOVERY_SLOPE = 0.8
STIMULUS_GAIN = 4.0
JUNCTION_SPREAD = 8.0
SOURCE_GAIN = 0.25
RELAX_WEIGHT = 0.8

PTS = 1536
NBLK = 12
BLK = 128
FIB = 256
COLS = 256
ROWS = 128
CHUNK = 48
HALO = 4
WIN = CHUNK + 2 * HALO
YPART = 4 * CHUNK
CPART = 16 * CHUNK
TILE = 256
F32 = jnp.float32
BF16 = jnp.bfloat16
VMEM = pl.BlockSpec(memory_space=pltpu.VMEM)
SMEM = pl.BlockSpec(memory_space=pltpu.SMEM)


def split(x):
    high = x.astype(BF16)
    return high, (x - high.astype(F32)).astype(BF16)


def dot(a, b, dims=((1,), (0,))):
    return lax.dot_general(a, b, (dims, ((), ())), preferred_element_type=F32)


def one_hot(column):
    lanes = lax.broadcasted_iota(jnp.int32, (FIB, COLS), 1)
    return jnp.where(column == lanes, 1.0, 0.0).astype(BF16)


def current_of(m, r, fire, place, start):
    width = m.shape[1]
    at = lax.broadcasted_iota(jnp.int32, (FIB, width), 1) + start
    offsets = (at.astype(F32) - place) * (1.0 / JUNCTION_SPREAD)
    wave = STIMULUS_GAIN * jnp.exp(-offsets * offsets)
    return m - m * m * m / 3.0 - r + fire * wave


def deposit(current, hot):
    high, low = split(current.T)
    return dot(high, hot) + dot(low, hot)


def put_halves(where_ref, sums_ref, keep_ref, send_ref):
    size = CPART + 2 * HALO
    for core in range(2):

        @pl.when(where_ref[0] == core)
        def _():
            keep_ref[...] = sums_ref[pl.ds(8 - HALO + CPART * core, size), :]
            send_ref[...] = sums_ref[pl.ds(8 - HALO + CPART * (1 - core), size), :]


def clear_ends(sums_ref):
    zero = jnp.zeros((8, COLS), F32)
    sums_ref[pl.ds(0, 8), :] = zero
    sums_ref[pl.ds(8 + PTS, 8), :] = zero


def first_kernel(where_ref, m_ref, r_ref, col_ref, place_ref, fire_ref, keep_ref, send_ref, sums_ref):
    clear_ends(sums_ref)
    place = place_ref[...]
    fire = fire_ref[:, 0:1]
    for b in range(NBLK):
        here = pl.ds(b * BLK, BLK)
        current = current_of(m_ref[:, here], r_ref[:, here], fire, place, b * BLK)
        sums_ref[pl.ds(8 + b * BLK, BLK), :] = deposit(current, one_hot(col_ref[:, b : b + 1]))
    put_halves(where_ref, sums_ref, keep_ref, send_ref)


def step_kernel(step, *refs):
    natural = step == 0
    last = step == STEPS - 1
    refs = list(refs)
    take = lambda k: [refs.pop(0) for _ in range(k)]
    where_ref, own_ref, other_ref, m_ref, r_ref, look_ref, col_ref, place_ref, fire_ref, high_ref, low_ref = take(11)
    m_out, r_out = take(2)
    if not last:
        keep_ref, send_ref = take(2)
    field_ref, rhs_high, rhs_low = take(3)
    if not last:
        hot_ref, sums_ref = take(2)
    tile = pl.program_id(0)
    core, y, z = where_ref[0], where_ref[1], where_ref[2]
    place = place_ref[...]

    @pl.when(tile == 0)
    def _():
        rows = 8 if natural else CHUNK
        for half, ref in ((core, own_ref), (1 - core, other_ref)):
            for yy in range(4):
                for zz in range(4):
                    index = lax.rem(y - yy + 4, 4) * 4 + lax.rem(z - zz + 4, 4)
                    start = pl.multiple_of(half * (16 * rows), 8) + (4 * yy + zz) * rows
                    field_ref[pl.ds(pl.multiple_of(start, 8), rows), :] = ref[index]
        for b in range(NBLK):
            here = pl.ds(b * BLK, BLK)
            hot = one_hot(look_ref[:, b : b + 1])
            if natural:
                high, low = split(field_ref[:, here])
                sampled = dot(hot, high) + dot(hot, low)
            else:
                high, low = split(field_ref[here, :])
                sampled = dot(hot, high, ((1,), (1,))) + dot(hot, low, ((1,), (1,)))
            m = m_ref[:, here]
            current = current_of(m, r_ref[:, here], fire_ref[:, step : step + 1], place, b * BLK)
            high, low = split(m + TIME_STEP * (current + sampled))
            rhs_high[:, here] = high
            rhs_low[:, here] = low
            if not last:
                hot_ref[b] = one_hot(col_ref[:, b : b + 1]) if natural else hot
        if not last:
            clear_ends(sums_ref)

    here = pl.ds(pl.multiple_of(tile * TILE, TILE), TILE)
    m_new = (
        dot(rhs_high[...], high_ref[...])
        + dot(rhs_low[...], high_ref[...])
        + dot(rhs_high[...], low_ref[...])
    )
    m_old, r_old = m_ref[:, here], r_ref[:, here]
    r_new = r_old + TIME_STEP * RECOVERY_RATE * (m_old + RECOVERY_SHIFT - RECOVERY_SLOPE * r_old)
    m_out[...] = m_new
    r_out[...] = r_new
    if not last:
        current = current_of(m_new, r_new, fire_ref[:, step + 1 : step + 2], place, tile * TILE)
        for k in range(TILE // BLK):
            block = tile * (TILE // BLK) + k
            start = pl.multiple_of(8 + block * BLK, 8)
            sums_ref[pl.ds(start, BLK), :] = deposit(current[:, k * BLK : (k + 1) * BLK], hot_ref[block])

        @pl.when(tile == pl.num_programs(0) - 1)
        def _():
            put_halves(where_ref, sums_ref, keep_ref, send_ref)


HALF_SHAPE = jax.ShapeDtypeStruct((CPART + 2 * HALO, COLS), F32)
STATE_SHAPE = jax.ShapeDtypeStruct((FIB, PTS), F32)


def first_call(where, m, r, col, place, fire):
    return pl.pallas_call(
        first_kernel,
        name="first_deposit",
        out_shape=(HALF_SHAPE, HALF_SHAPE),
        in_specs=[SMEM] + [VMEM] * 5,
        out_specs=(VMEM, VMEM),
        scratch_shapes=[pltpu.VMEM((PTS + 16, COLS), F32)],
        cost_estimate=pl.CostEstimate(flops=2 * 2 * FIB * COLS * PTS, bytes_accessed=5 << 20, transcendentals=FIB * PTS),
        compiler_params=pltpu.CompilerParams(vmem_limit_bytes=40 << 20),
    )(where, m, r, col, place, fire)


def step_call(step, where, own, other, m, r, look, col, place, fire, high, low):
    last = step == STEPS - 1
    whole = lambda a: pl.BlockSpec(a.shape, lambda j: (0,) * a.ndim)
    weights = pl.BlockSpec((PTS, TILE), lambda j: (0, j))
    tiles = pl.BlockSpec((FIB, TILE), lambda j: (0, j))
    out_shape, out_specs = [STATE_SHAPE, STATE_SHAPE], [tiles, tiles]
    field = (COLS, PTS) if step == 0 else (PTS, COLS)
    scratch = [pltpu.VMEM(field, F32), pltpu.VMEM((FIB, PTS), BF16), pltpu.VMEM((FIB, PTS), BF16)]
    if not last:
        out_shape += [HALF_SHAPE, HALF_SHAPE]
        out_specs += [pl.BlockSpec(HALF_SHAPE.shape, lambda j: (0, 0))] * 2
        scratch += [pltpu.VMEM((NBLK, FIB, COLS), BF16), pltpu.VMEM((PTS + 16, COLS), F32)]
    operands = (own, other, m, r, look, col, place, fire)
    return pl.pallas_call(
        functools.partial(step_kernel, step),
        name="fibre_step",
        out_shape=out_shape,
        grid=(PTS // TILE,),
        in_specs=[SMEM] + [whole(a) for a in operands] + [weights, weights],
        out_specs=out_specs,
        scratch_shapes=scratch,
        cost_estimate=pl.CostEstimate(flops=2 * 3 * FIB * PTS * PTS, bytes_accessed=18 << 20, transcendentals=2 * FIB * PTS),
        compiler_params=pltpu.CompilerParams(vmem_limit_bytes=48 << 20),
    )(where, *operands, high, low)


def relax_kernel(fresh, where_ref, msg0, msg1, msg2, msg3, state_ref, gain_ref, state_out, own_out, field_a, field_b, msgs, source):
    pool = where_ref[3]
    for k, ref in enumerate((msg0, msg1, msg2, msg3)):
        msgs[k] = ref[...]
    lanes = lax.broadcasted_iota(jnp.int32, (WIN, ROWS), 1)
    zeros = jnp.zeros((WIN + 16, ROWS), F32)
    edge = jnp.zeros((8, ROWS), F32)
    for field in (field_a, field_b):
        field[0] = zeros
        field[9] = zeros
        for x in range(8):
            field[x + 1, pl.ds(0, 8), :] = edge
            field[x + 1, pl.ds(WIN + 8, 8), :] = edge
    for p in range(4):
        near = lax.rem(pool - p + 4, 4)
        for i in range(2):
            x = 2 * p + i
            lane = pl.ds(i * ROWS, ROWS)
            field_a[x + 1, pl.ds(8, WIN), :] = state_ref[near, i]
            if not fresh:
                field_a[x + 1, pl.ds(8, HALO), :] = msgs[near, pl.ds(WIN, HALO), lane]
                field_a[x + 1, pl.ds(8 + HALO + CHUNK, HALO), :] = msgs[near, pl.ds(WIN + HALO, HALO), lane]
            source[x] = SOURCE_GAIN * msgs[near, pl.ds(0, WIN), lane]
    old, new = field_a, field_b
    for _ in range(SWEEPS):
        for p in range(4):
            near = lax.rem(pool - p + 4, 4)
            for i in range(2):
                x = 2 * p + i
                centre = old[x + 1, pl.ds(8, WIN), :]
                total = source[x] + old[x, pl.ds(8, WIN), :] + old[x + 2, pl.ds(8, WIN), :]
                total = total + old[x + 1, pl.ds(7, WIN), :] + old[x + 1, pl.ds(9, WIN), :]
                total = total + jnp.where(lanes == 0, 0.0, pltpu.roll(centre, 1, 1))
                total = total + jnp.where(lanes == ROWS - 1, 0.0, pltpu.roll(centre, ROWS - 1, 1))
                new[x + 1, pl.ds(8, WIN), :] = (1.0 - RELAX_WEIGHT) * centre + gain_ref[near, i] * total
        old, new = new, old
    for p in range(4):
        near = lax.rem(pool - p + 4, 4)
        for i in range(2):
            state_out[near, i] = old[2 * p + i + 1, pl.ds(8, WIN), :]
    for i in range(2):
        own_out[:, i * ROWS : (i + 1) * ROWS] = old[2 * pool + i + 1, pl.ds(8 + HALO, CHUNK), :]


def relax_call(step, where, msgs, state, gain):
    return pl.pallas_call(
        functools.partial(relax_kernel, step == 0),
        name="relax",
        out_shape=(jax.ShapeDtypeStruct((4, 2, WIN, ROWS), F32), jax.ShapeDtypeStruct((CHUNK, COLS), F32)),
        in_specs=[SMEM] + [VMEM] * 6,
        out_specs=(VMEM, VMEM),
        scratch_shapes=[
            pltpu.VMEM((10, WIN + 16, ROWS), F32),
            pltpu.VMEM((10, WIN + 16, ROWS), F32),
            pltpu.VMEM((4, WIN + 2 * HALO, COLS), F32),
            pltpu.VMEM((8, WIN, ROWS), F32),
        ],
        cost_estimate=pl.CostEstimate(flops=SWEEPS * 12 * 8 * WIN * ROWS, bytes_accessed=2 << 20, transcendentals=0),
    )(where, *msgs, state, gain)


def fib_of(y, z, core):
    return (y * 4 + z) * 2 + core


def shift(x, axis, by):
    if axis == "pool":
        return lax.ppermute(x, "pool", [(i, (i + by) % 4) for i in range(4)])
    pairs = []
    for y in range(4):
        for z in range(4):
            for core in range(2):
                to = {
                    "y": ((y + by) % 4, z, core),
                    "z": (y, (z + by) % 4, core),
                    "core": (y, z, 1 - core),
                }[axis]
                pairs.append((fib_of(y, z, core), fib_of(*to)))
    return lax.ppermute(x, "fib", pairs)


def from_three(x, axis):
    got = {k: shift(x, axis, k) for k in (1, 3, 2)}
    return [x, got[1], got[2], got[3]]


def gathered(piece):
    held = jnp.stack(from_three(piece, "z"))
    held = jnp.stack(from_three(held, "y"))
    held = held.reshape((16,) + piece.shape)
    return held, shift(held, "core", 1)


def rows_of(x, start, size):
    return lax.dynamic_slice_in_dim(x, start, size, 0)


def scattered(keep, send, y, z):
    total = keep + shift(send, "core", 1)
    for axis, me, part in (("y", y, YPART), ("z", z, CHUNK)):
        size = part + 2 * HALO
        terms = {k: shift(rows_of(total, part * lax.rem(me + k, 4), size), axis, k) for k in (1, 3, 2)}
        total = rows_of(total, part * me, size) + terms[1] + terms[3] + terms[2]
    return total


def halos(own, other, core, y, z):
    chunk = core * 16 + y * 4 + z

    def rows(which, start):
        held = jnp.clip(which, 0, 31)
        c, yy, zz = held // 16, (held // 4) % 4, held % 4
        index = lax.rem(y - yy + 4, 4) * 4 + lax.rem(z - zz + 4, 4)
        cut = lambda a: lax.dynamic_slice(a, (index, start, 0), (1, HALO, COLS))[0]
        found = jnp.where(c == core, cut(own), cut(other))
        return jnp.where(which == held, found, 0.0)

    return rows(chunk - 1, CHUNK - HALO), rows(chunk + 1, 0)


def opening(reaction, potential, spikes):
    pair = jnp.stack([potential, RELAX_WEIGHT / (6.0 + reaction)]).reshape(16, PTS)
    padded = jnp.pad(pair, ((0, 0), (HALO, CHUNK - HALO))).reshape(16, 33, CHUNK)
    windows = jnp.concatenate([padded[:, :32], padded[:, 1:, : 2 * HALO]], axis=2)
    windows = windows.reshape(16, 2, 4, 4, WIN).transpose(2, 3, 1, 0, 4).reshape(32, 16, WIN)
    flags = jnp.pad(spikes.astype(F32).reshape(1, 1, 8), ((0, 0), (0, 0), (0, WIN - 8)))
    packed = jnp.concatenate([windows, jnp.broadcast_to(flags, (32, 1, WIN))], axis=1)
    packed = lax.all_to_all(packed, "fib", 0, 0, tiled=True)
    trains = packed[:, 16, :8].reshape(64, STEPS)
    slab = packed[:, :16].reshape(32, 2, 4, 2, WIN).transpose(1, 3, 4, 0, 2).reshape(2, 2, WIN, ROWS)
    return trains, slab


def on_device(vm_state, recovery, spikes, owner, junction, column_index, cable_inverse, reaction, potential):
    fib = lax.axis_index("fib")
    pool = lax.axis_index("pool")
    core, z, y = fib % 2, (fib // 2) % 4, fib // 8
    where = jnp.stack([core, y, z, pool]).astype(jnp.int32)

    own, other = gathered(potential.reshape(8, PTS))
    trains, slab = opening(reaction, potential, spikes)
    units = (owner[:, None] == lax.iota(jnp.int32, 64)[None, :]).astype(F32)
    fire = jnp.dot(units, trains, preferred_element_type=F32)
    place = junction.astype(F32)[:, None]
    col = (column_index % 2) * ROWS + column_index // 2
    look = ((column_index // 8) % 2) * 128 + (column_index // 16) * 8 + column_index % 8

    keep, send = first_call(where, vm_state, recovery, col, place, fire)

    slabs = from_three(slab, "pool")
    state = jnp.stack([s[0] for s in slabs])
    gain = jnp.stack([s[1] for s in slabs])
    rounded = lax.reduce_precision(cable_inverse, 8, 7)
    high = rounded.astype(BF16)
    low = (cable_inverse - rounded).astype(BF16)

    membrane, recovering = vm_state, recovery
    edges = jnp.zeros((2 * HALO, COLS), F32)
    for step in range(STEPS):
        if step:
            edges = jnp.concatenate(halos(own, other, core, y, z))
        source = scattered(keep, send, y, z)
        msgs = from_three(jnp.concatenate([source, edges]), "pool")
        out = step_call(
            step, where, own, other, membrane, recovering, col if step else look, col, place, fire, high, low
        )
        membrane, recovering = out[0], out[1]
        state, piece = relax_call(step, where, msgs, state, gain)
        if step < STEPS - 1:
            keep, send = out[2], out[3]
            own, other = gathered(piece)
    sends = piece.T.reshape(2, 32, 4, CHUNK).transpose(1, 2, 0, 3).reshape(32, 8, CHUNK)
    got = lax.all_to_all(sends, "fib", 0, 0, tiled=True)
    extracell = got.reshape(4, 4, 2, 4, 2, CHUNK).transpose(3, 4, 2, 0, 1, 5).reshape(4, 2, PTS)
    return membrane, recovering, extracell


def solution(mesh):
    split_rows = P(("pool", "fib"), None)
    grid = P("fib", "pool", None)
    flat = P(("pool", "fib"))
    in_specs = (split_rows, split_rows, split_rows, flat, flat, split_rows, P(), grid, grid)
    return jax.shard_map(
        on_device, mesh=mesh, in_specs=in_specs, out_specs=(split_rows, split_rows, grid), check_vma=False
    )
```

```python
import functools

import jax
import jax.numpy as jnp
from jax import lax
from jax.experimental import pallas as pl
from jax.experimental.pallas import tpu as pltpu
from jax.sharding import PartitionSpec as P

STEPS = 4
SWEEPS = 4
TIME_STEP = 0.05
RECOVERY_RATE = 0.5
RECOVERY_SHIFT = 0.7
RECOVERY_SLOPE = 0.8
STIMULUS_GAIN = 4.0
JUNCTION_SPREAD = 8.0
SOURCE_GAIN = 0.25
RELAX_WEIGHT = 0.8

PTS = 1536
NBLK = 12
BLK = 128
FIB = 256
COLS = 256
ROWS = 128
CHUNK = 48
HALO = 4
WIN = CHUNK + 2 * HALO
YPART = 4 * CHUNK
CPART = 16 * CHUNK
YWIN = YPART + 2 * HALO
HALF = CPART + 2 * HALO
LOAD = YWIN + CHUNK
TILE = 256
F32 = jnp.float32
BF16 = jnp.bfloat16
VMEM = pl.BlockSpec(memory_space=pltpu.VMEM)
SMEM = pl.BlockSpec(memory_space=pltpu.SMEM)


def shaped(*dims, dtype=F32):
    return jax.ShapeDtypeStruct(dims, dtype)


def run(kernel, name, out_shape, operands, scratch=(), flops=1 << 20, moved=1 << 20, megabytes=4):
    return pl.pallas_call(
        kernel,
        name=name,
        out_shape=out_shape,
        in_specs=[SMEM] + [VMEM] * (len(operands) - 1),
        out_specs=jax.tree.map(lambda _: VMEM, out_shape),
        scratch_shapes=scratch,
        cost_estimate=pl.CostEstimate(flops=flops, bytes_accessed=moved, transcendentals=0),
        compiler_params=pltpu.CompilerParams(vmem_limit_bytes=megabytes << 20),
    )(*operands)


def split(x):
    high = x.astype(BF16)
    return high, (x - high.astype(F32)).astype(BF16)


def dot(a, b, dims=((1,), (0,))):
    return lax.dot_general(a, b, (dims, ((), ())), preferred_element_type=F32)


def one_hot(column, width):
    lanes = lax.broadcasted_iota(jnp.int32, (column.shape[0], width), 1)
    return jnp.where(column == lanes, 1.0, 0.0).astype(BF16)


def advance(m, r, fire, place, start):
    width = m.shape[1]
    at = (lax.broadcasted_iota(jnp.int32, (1, width), 1) + start).astype(F32)
    offsets = (at - place) * (1.0 / JUNCTION_SPREAD)
    wave = jnp.exp(-offsets * offsets)
    current = m - m * m * m * (1.0 / 3.0) - r + (STIMULUS_GAIN * fire) * wave
    base = m + TIME_STEP * current
    following = r + TIME_STEP * RECOVERY_RATE * (m + RECOVERY_SHIFT - RECOVERY_SLOPE * r)
    return current, base, following


def deposit(current, hot):
    high, low = split(current.T)
    return dot(high, hot) + dot(low, hot)


def clear_ends(sums_ref):
    zero = jnp.zeros((8, COLS), F32)
    sums_ref[pl.ds(0, 8), :] = zero
    sums_ref[pl.ds(8 + PTS, 8), :] = zero


def put_halves(where_ref, sums_ref, keep_ref, send_ref):
    for core in range(2):

        @pl.when(where_ref[0] == core)
        def _():
            keep_ref[...] = sums_ref[pl.ds(8 - HALO + CPART * core, HALF), :]
            send_ref[...] = sums_ref[pl.ds(8 - HALO + CPART * (1 - core), HALF), :]


SUMS = pltpu.VMEM((PTS + 16, COLS), F32)


def first_kernel(
    where_ref, m_ref, r_ref, table_ref, near_ref, far_ref,
    base_ref, next_ref, hot_ref, look_ref, fire_ref, keep_ref, send_ref, sums_ref,
):
    clear_ends(sums_ref)
    slot = table_ref[:, NBLK : NBLK + 1]
    place = table_ref[:, NBLK + 1 : NBLK + 2].astype(F32)
    units = one_hot(slot, 64)
    fires = dot(units[:, :32], near_ref[...].astype(BF16)) + dot(units[:, 32:], far_ref[...].astype(BF16))
    fire_ref[...] = fires
    fire = fires[:, 0:1]
    for b in range(NBLK):
        here = pl.ds(b * BLK, BLK)
        current, base, following = advance(m_ref[:, here], r_ref[:, here], fire, place, b * BLK)
        base_ref[:, here] = base
        next_ref[:, here] = following
        index = table_ref[:, b : b + 1]
        hot = one_hot((index & 1) * ROWS + (index >> 1), COLS)
        hot_ref[b] = hot
        look_ref[b] = one_hot(((index >> 3) & 1) * 128 + (index >> 4) * 8 + (index & 7), COLS)
        sums_ref[pl.ds(8 + b * BLK, BLK), :] = deposit(current, hot)
    put_halves(where_ref, sums_ref, keep_ref, send_ref)


def first_call(where, m, r, table, near, far):
    state = shaped(FIB, PTS)
    hots = shaped(NBLK, FIB, COLS, dtype=BF16)
    return run(
        first_kernel,
        "first_deposit",
        (state, state, hots, hots, shaped(FIB, STEPS), shaped(HALF, COLS), shaped(HALF, COLS)),
        (where, m, r, table, near, far),
        [SUMS],
        flops=6 << 30,
        moved=12 << 20,
        megabytes=6,
    )


def step_kernel(step, *refs):
    natural = step == 0
    last = step == STEPS - 1
    where_ref, own_ref, other_ref, base_ref, next_ref, look_ref, hot_ref, table_ref, fire_ref, high_ref, low_ref = refs[:11]
    if last:
        m_out, field_ref, rhs_high, rhs_low = refs[11:]
    else:
        base_out, next_out, keep_ref, send_ref, field_ref, rhs_high, rhs_low, sums_ref, m_out = refs[11:]
    core, y, z = where_ref[0], where_ref[1], where_ref[2]
    for half, ref in ((core, own_ref), (1 - core, other_ref)):
        for yy in range(4):
            for zz in range(4):
                index = lax.rem(z - zz + 4, 4) * 4 + lax.rem(y - yy + 4, 4)
                first = pl.multiple_of(index * CHUNK, 8)
                if natural:
                    start = pl.multiple_of(half * 128 + (4 * yy + zz) * 8, 8)
                    for t in range(PTS // TILE):
                        tile = ref[pl.ds(first + 8 * t, 8), :]
                        field_ref[pl.ds(start, 8), t * TILE : (t + 1) * TILE] = tile
                else:
                    start = pl.multiple_of(half * CPART + (4 * yy + zz) * CHUNK, 8)
                    field_ref[pl.ds(start, CHUNK), :] = ref[pl.ds(first, CHUNK), :]
    for b in range(NBLK):
        here = pl.ds(b * BLK, BLK)
        hot = look_ref[b]
        if natural:
            high, low = split(field_ref[:, here])
            sampled = dot(hot, high) + dot(hot, low)
        else:
            high, low = split(field_ref[here, :])
            sampled = dot(hot, high, ((1,), (1,))) + dot(hot, low, ((1,), (1,)))
        high, low = split(base_ref[:, here] + TIME_STEP * sampled)
        rhs_high[:, here] = high
        rhs_low[:, here] = low
    for t in range(PTS // TILE):
        here = pl.ds(t * TILE, TILE)
        m_out[:, here] = (
            dot(rhs_high[...], high_ref[:, here])
            + dot(rhs_low[...], high_ref[:, here])
            + dot(rhs_high[...], low_ref[:, here])
        )
    if last:
        return
    clear_ends(sums_ref)
    place = table_ref[:, NBLK + 1 : NBLK + 2].astype(F32)
    fire = fire_ref[:, step + 1 : step + 2]
    for b in range(NBLK):
        here = pl.ds(b * BLK, BLK)
        current, base, following = advance(m_out[:, here], next_ref[:, here], fire, place, b * BLK)
        base_out[:, here] = base
        next_out[:, here] = following
        sums_ref[pl.ds(8 + b * BLK, BLK), :] = deposit(current, hot_ref[b])
    put_halves(where_ref, sums_ref, keep_ref, send_ref)


def step_call(step, *operands):
    last = step == STEPS - 1
    state = shaped(FIB, PTS)
    field = (COLS, PTS) if step == 0 else (PTS, COLS)
    scratch = [pltpu.VMEM(field, F32), pltpu.VMEM((FIB, PTS), BF16), pltpu.VMEM((FIB, PTS), BF16)]
    if last:
        out_shape = (state,)
    else:
        out_shape = (state, state, shaped(HALF, COLS), shaped(HALF, COLS))
        scratch += [SUMS, pltpu.VMEM((FIB, PTS), F32)]
    return run(
        functools.partial(step_kernel, step),
        "fibre_step",
        out_shape,
        operands,
        scratch,
        flops=2 * 3 * FIB * PTS * PTS,
        moved=20 << 20,
        megabytes=10,
    )


def y_pack_kernel(where_ref, keep_ref, got_ref, piece_ref, mine_ref, one_ref, two_ref, three_ref):
    y = where_ref[1]
    piece = piece_ref[...]
    for k, out in enumerate((mine_ref, one_ref, two_ref, three_ref)):
        here = pl.ds(pl.multiple_of(lax.rem(y + k, 4) * YPART, 8), YWIN)
        out[pl.ds(0, YWIN), :] = keep_ref[here, :] + got_ref[here, :]
        if k:
            out[pl.ds(YWIN, CHUNK), :] = piece


def y_pack(where, keep, got, piece):
    load = shaped(LOAD, COLS)
    return run(y_pack_kernel, "y_pack", (shaped(YWIN, COLS), load, load, load), (where, keep, got, piece))


def z_pack_kernel(joint, where_ref, mine_ref, piece_ref, got1, got2, got3, own_ref, group_ref, *outs):
    z = where_ref[2]
    group = [piece_ref[...]] + [got[pl.ds(YWIN, CHUNK), :] for got in (got1, got2, got3)]
    for k, part in enumerate(group):
        group_ref[pl.ds(k * CHUNK, CHUNK), :] = part
    for k, out in enumerate((own_ref,) + outs):
        here = pl.ds(pl.multiple_of(lax.rem(z + k, 4) * CHUNK, 8), WIN)
        out[pl.ds(0, WIN), :] = mine_ref[here, :] + got1[here, :] + got3[here, :] + got2[here, :]
        if k and joint:
            for i, part in enumerate(group):
                out[pl.ds(WIN + i * CHUNK, CHUNK), :] = part


def z_pack(joint, where, mine, piece, gots):
    load = shaped(LOAD if joint else WIN, COLS)
    return run(
        functools.partial(z_pack_kernel, joint),
        "z_pack",
        (shaped(WIN, COLS), shaped(YPART, COLS), load, load, load),
        (where, mine, piece, *gots),
    )


def z_join_kernel(where_ref, own_ref, group_ref, got1, got2, got3, source_ref, held_ref):
    here = pl.ds(0, WIN)
    source_ref[...] = own_ref[...] + got1[here, :] + got3[here, :] + got2[here, :]
    held_ref[pl.ds(0, YPART), :] = group_ref[...]
    for k, got in enumerate((got1, got2, got3)):
        held_ref[pl.ds((k + 1) * YPART, YPART), :] = got[pl.ds(WIN, YPART), :]


def z_join(where, own, group, gots):
    return run(z_join_kernel, "z_join", (shaped(WIN, COLS), shaped(CPART, COLS)), (where, own, group, *gots))


def message_kernel(where_ref, source_ref, own_ref, other_ref, out_ref):
    core, y, z = where_ref[0], where_ref[1], where_ref[2]
    chunk = core * 16 + y * 4 + z
    out_ref[pl.ds(0, WIN), :] = source_ref[...]

    def rows(which, start):
        held = jnp.clip(which, 0, 31)
        c, yy, zz = held >> 4, (held >> 2) & 3, held & 3
        index = lax.rem(z - zz + 4, 4) * 4 + lax.rem(y - yy + 4, 4)
        here = pl.ds(pl.multiple_of(index * CHUNK + start, 8), 8)
        found = jnp.where(c == core, own_ref[here, :], other_ref[here, :])
        return pltpu.roll(jnp.where(which == held, found, 0.0), 4, 0)

    below = rows(chunk - 1, CHUNK - 8)
    above = rows(chunk + 1, 0)
    level = lax.broadcasted_iota(jnp.int32, (8, COLS), 0)
    out_ref[pl.ds(WIN, 8), :] = jnp.where(level < HALO, below, above)


def message(where, source, own, other):
    return run(message_kernel, "message", shaped(WIN + 8, COLS), (where, source, own, other))


def relax_kernel(step, *refs):
    fresh = step == 0
    last = step == STEPS - 1
    refs = list(refs)
    where_ref = refs.pop(0)
    pool = where_ref[3]
    message_refs = [refs.pop(0) for _ in range(4)]
    if fresh:
        slab_refs = [refs.pop(0) for _ in range(4)]
    else:
        state_ref, gain_ref = refs.pop(0), refs.pop(0)
    if not last:
        state_out = refs.pop(0)
    own_out = refs.pop(0)
    if fresh:
        gain_ref = refs.pop(0)
    field_a, field_b, msgs, source = refs[:4]
    for k, ref in enumerate(message_refs):
        msgs[k] = ref[...]
    if fresh:
        state_ref = state_out
        for k, ref in enumerate(slab_refs):
            state_ref[k] = ref[0]
            gain_ref[k] = ref[1]
    lanes = lax.broadcasted_iota(jnp.int32, (WIN, ROWS), 1)
    zeros = jnp.zeros((WIN + 16, ROWS), F32)
    edge = jnp.zeros((8, ROWS), F32)
    for field in (field_a, field_b):
        field[0] = zeros
        field[9] = zeros
        for x in range(8):
            field[x + 1, pl.ds(0, 8), :] = edge
            field[x + 1, pl.ds(WIN + 8, 8), :] = edge
    for p in range(4):
        near = lax.rem(pool - p + 4, 4)
        for i in range(2):
            x = 2 * p + i
            lane = pl.ds(i * ROWS, ROWS)
            field_a[x + 1, pl.ds(8, WIN), :] = state_ref[near, i]
            if not fresh:
                field_a[x + 1, pl.ds(8, HALO), :] = msgs[near, pl.ds(WIN, HALO), lane]
                field_a[x + 1, pl.ds(8 + HALO + CHUNK, HALO), :] = msgs[near, pl.ds(WIN + HALO, HALO), lane]
            source[x] = SOURCE_GAIN * msgs[near, pl.ds(0, WIN), lane]
    old, new = field_a, field_b
    for _ in range(SWEEPS):
        for p in range(4):
            near = lax.rem(pool - p + 4, 4)
            for i in range(2):
                x = 2 * p + i
                centre = old[x + 1, pl.ds(8, WIN), :]
                total = source[x] + old[x, pl.ds(8, WIN), :] + old[x + 2, pl.ds(8, WIN), :]
                total = total + old[x + 1, pl.ds(7, WIN), :] + old[x + 1, pl.ds(9, WIN), :]
                total = total + jnp.where(lanes == 0, 0.0, pltpu.roll(centre, 1, 1))
                total = total + jnp.where(lanes == ROWS - 1, 0.0, pltpu.roll(centre, ROWS - 1, 1))
                new[x + 1, pl.ds(8, WIN), :] = (1.0 - RELAX_WEIGHT) * centre + gain_ref[near, i] * total
        old, new = new, old
    if last:
        for i in range(2):
            flat = old[2 * pool + i + 1, pl.ds(8, WIN), :]
            refs[4][...] = jnp.zeros((ROWS, ROWS), F32)
            refs[4][pl.ds(0, WIN), :] = flat
            turned = refs[4][...].T
            for s in range(32):
                own_out[s, pl.ds(4 * i, 4), :] = turned[4 * s : 4 * s + 4, :]
        return
    for p in range(4):
        near = lax.rem(pool - p + 4, 4)
        for i in range(2):
            state_out[near, i] = old[2 * p + i + 1, pl.ds(8, WIN), :]
    for i in range(2):
        own_out[:, i * ROWS : (i + 1) * ROWS] = old[2 * pool + i + 1, pl.ds(8 + HALO, CHUNK), :]


def relax(step, where, msgs, extra):
    state = shaped(4, 2, WIN, ROWS)
    own = shaped(CHUNK, COLS)
    out_shape = (state, own)
    if step == 0:
        out_shape = (state, own, state)
    if step == STEPS - 1:
        out_shape = (shaped(32, 8, ROWS),)
    scratch = [
        pltpu.VMEM((10, WIN + 16, ROWS), F32),
        pltpu.VMEM((10, WIN + 16, ROWS), F32),
        pltpu.VMEM((4, WIN + 8, COLS), F32),
        pltpu.VMEM((8, WIN, ROWS), F32),
        pltpu.VMEM((ROWS, ROWS), F32),
    ]
    return run(functools.partial(relax_kernel, step), "relax", out_shape, (where, *msgs, *extra), scratch)


def chunk_parts(s):
    core, z, y = s % 2, (s // 2) % 4, s // 8
    return core * 16 + y * 4 + z


def open_kernel(where_ref, potential_ref, reaction_ref, out_ref, wide_ref):
    wide_ref[...] = jnp.zeros((16, PTS + 256), F32)
    for row in range(4):
        for x in range(2):
            wide_ref[4 * x + row, pl.ds(128, PTS)] = potential_ref[row, x, :]
            wide_ref[8 + 4 * x + row, pl.ds(128, PTS)] = RELAX_WEIGHT / (6.0 + reaction_ref[row, x, :])
    for s in range(32):
        out_ref[s] = wide_ref[:, pl.ds(128 + CHUNK * chunk_parts(s) - HALO, 128)]


def open_pack(where, potential, reaction):
    return run(
        open_kernel,
        "open_pack",
        shaped(32, 16, 128),
        (where, potential, reaction),
        [pltpu.VMEM((16, PTS + 256), F32)],
    )


def slab_kernel(where_ref, got_ref, out_ref, square_ref):
    for a in range(2):
        for x in range(2):
            for s in range(32):
                square_ref[pl.ds(4 * s, 4), :] = got_ref[s, pl.ds(8 * a + 4 * x, 4), :]
            out_ref[a, x] = square_ref[...].T[:WIN, :]


def slab_unpack(where, got):
    return run(slab_kernel, "slab", shaped(2, 2, WIN, ROWS), (where, got), [pltpu.VMEM((ROWS, ROWS), F32)])


def close_kernel(where_ref, got_ref, out_ref, wide_ref):
    for s in range(32):
        part = got_ref[s]
        wide_ref[:, pl.ds(CHUNK * chunk_parts(s), CHUNK)] = part[:, HALO : HALO + CHUNK]
    for row in range(4):
        for x in range(2):
            out_ref[row, x, :] = wide_ref[4 * x + row, :]


def close(where, got):
    return run(close_kernel, "close", shaped(4, 2, PTS), (where, got), [pltpu.VMEM((8, PTS), F32)])


def fib_of(y, z, core):
    return (y * 4 + z) * 2 + core


def shift(x, axis, by=1):
    if axis == "pool":
        return lax.ppermute(x, "pool", [(i, (i + by) % 4) for i in range(4)])
    pairs = []
    for y in range(4):
        for z in range(4):
            for core in range(2):
                to = {
                    "y": ((y + by) % 4, z, core),
                    "z": (y, (z + by) % 4, core),
                    "core": (y, z, 1 - core),
                }[axis]
                pairs.append((fib_of(y, z, core), fib_of(*to)))
    return lax.ppermute(x, "fib", pairs)


def to_three(parts, axis):
    got = {k: shift(parts[k - 1], axis, k) for k in (1, 3, 2)}
    return [got[1], got[2], got[3]]


def on_device(vm_state, recovery, spikes, owner, junction, column_index, cable_inverse, reaction, potential):
    fib = lax.axis_index("fib")
    pool = lax.axis_index("pool")
    core, z, y = fib % 2, (fib // 2) % 4, fib // 8
    where = jnp.stack([core, y, z, pool]).astype(jnp.int32)

    near = spikes.astype(F32)
    near = jnp.stack([near] + to_three([near] * 3, "y"))
    near = jnp.stack([near] + to_three([near] * 3, "z")).reshape(32, STEPS)
    far = shift(near, "core")
    unit_core, unit_z, unit_y = (owner // 2) % 2, (owner // 4) % 4, owner // 16
    away = jnp.where(unit_core == core, 0, 32)
    slot = away + (((z - unit_z) % 4) * 4 + (y - unit_y) % 4) * 2 + owner % 2
    table = jnp.concatenate([column_index, slot[:, None], junction[:, None]], axis=1)

    base, following, hot, look, fire, keep, send = first_call(where, vm_state, recovery, table, near, far)

    rounded = lax.reduce_precision(cable_inverse, 8, 7)
    high = rounded.astype(BF16)
    low = (cable_inverse - rounded).astype(BF16)

    slab = slab_unpack(where, lax.all_to_all(open_pack(where, potential, reaction), "fib", 0, 0, tiled=True))
    extra = [slab] + to_three([slab] * 3, "pool")
    piece = potential.reshape(8, PTS // TILE, TILE).transpose(1, 0, 2).reshape(CHUNK, COLS)

    for step in range(STEPS):
        last = step == STEPS - 1
        mine, *loads = y_pack(where, keep, shift(send, "core"), piece)
        gots = to_three(loads, "y")
        own, group, *loads = z_pack(not last, where, mine, piece, gots)
        gots = to_three(loads, "z")
        if last:
            source = own + gots[0] + gots[2] + gots[1]
            held = jnp.concatenate([group] + to_three([group] * 3, "z"))
        else:
            source, held = z_join(where, own, group, gots)
        other = shift(held, "core")
        note = message(where, source, held, other)
        msgs = [note] + to_three([note] * 3, "pool")
        out = step_call(
            step, where, held, other, base, following, look if step == 0 else hot, hot, table, fire, high, low
        )
        relaxed = relax(step, where, msgs, extra)
        if last:
            membrane, recovering = out[0], following
        else:
            base, following, keep, send = out
            piece = relaxed[1]
            if step == 0:
                gain = relaxed[2]
            extra = [relaxed[0], gain]
    extracell = close(where, lax.all_to_all(relaxed[0], "fib", 0, 0, tiled=True))
    return membrane, recovering, extracell


def solution(mesh):
    split_rows = P(("pool", "fib"), None)
    grid = P("fib", "pool", None)
    flat = P(("pool", "fib"))
    in_specs = (split_rows, split_rows, split_rows, flat, flat, split_rows, P(), grid, grid)
    return jax.shard_map(
        on_device, mesh=mesh, in_specs=in_specs, out_specs=(split_rows, split_rows, grid), check_vma=False
    )
```

```python
import functools

import jax
import jax.numpy as jnp
from jax import lax
from jax.experimental import pallas as pl
from jax.experimental.pallas import tpu as pltpu
from jax.sharding import PartitionSpec as P

STEPS = 4
SWEEPS = 4
TIME_STEP = 0.05
RECOVERY_RATE = 0.5
RECOVERY_SHIFT = 0.7
RECOVERY_SLOPE = 0.8
STIMULUS_GAIN = 4.0
JUNCTION_SPREAD = 8.0
SOURCE_GAIN = 0.25
RELAX_WEIGHT = 0.8

PTS = 1536
NBLK = 12
BLK = 128
FIB = 256
COLS = 256
ROWS = 128
CHUNK = 48
HALO = 4
WIN = CHUNK + 2 * HALO
YPART = 4 * CHUNK
CPART = 16 * CHUNK
YWIN = YPART + 2 * HALO
HALF = CPART + 2 * HALO
LOAD = YWIN + CHUNK
TILE = 256
TABLE = NBLK + 2
UNROLL = 3
PRODUCTS = 2
F32 = jnp.float32
BF16 = jnp.bfloat16
VMEM = pl.BlockSpec(memory_space=pltpu.VMEM)
SMEM = pl.BlockSpec(memory_space=pltpu.SMEM)


def shaped(*dims, dtype=F32):
    return jax.ShapeDtypeStruct(dims, dtype)


def run(kernel, name, out_shape, operands, scratch=(), flops=1 << 20, moved=1 << 20, megabytes=4):
    return pl.pallas_call(
        kernel,
        name=name,
        out_shape=out_shape,
        in_specs=[SMEM] + [VMEM] * (len(operands) - 1),
        out_specs=jax.tree.map(lambda _: VMEM, out_shape),
        scratch_shapes=scratch,
        cost_estimate=pl.CostEstimate(flops=flops, bytes_accessed=moved, transcendentals=0),
        compiler_params=pltpu.CompilerParams(vmem_limit_bytes=megabytes << 20),
    )(*operands)


def split(x):
    high = x.astype(BF16)
    return high, (x - high.astype(F32)).astype(BF16)


def dot(a, b, dims=((1,), (0,))):
    return lax.dot_general(a, b, (dims, ((), ())), preferred_element_type=F32)


def one_hot(column, width):
    lanes = lax.broadcasted_iota(jnp.int32, (column.shape[0], width), 1)
    return jnp.where(column == lanes, 1.0, 0.0).astype(BF16)


def advance(m, r, fire, place, start):
    width = m.shape[1]
    at = (lax.broadcasted_iota(jnp.int32, (1, width), 1) + start).astype(F32)
    offsets = (at - place) * (1.0 / JUNCTION_SPREAD)
    wave = jnp.exp(-offsets * offsets)
    current = m - m * m * m * (1.0 / 3.0) - r + (STIMULUS_GAIN * fire) * wave
    base = m + TIME_STEP * current
    following = r + TIME_STEP * RECOVERY_RATE * (m + RECOVERY_SHIFT - RECOVERY_SLOPE * r)
    return current, base, following


def deposit(current, hot):
    high, low = split(current.T)
    return dot(high, hot) + dot(low, hot)


def clear_ends(sums_ref):
    zero = jnp.zeros((8, COLS), F32)
    sums_ref[pl.ds(0, 8), :] = zero
    sums_ref[pl.ds(8 + PTS, 8), :] = zero


def put_halves(where_ref, sums_ref, keep_ref, send_ref):
    for core in range(2):

        @pl.when(where_ref[0] == core)
        def _():
            keep_ref[...] = sums_ref[pl.ds(8 - HALO + CPART * core, HALF), :]
            send_ref[...] = sums_ref[pl.ds(8 - HALO + CPART * (1 - core), HALF), :]


SUMS = pltpu.VMEM((PTS + 16, COLS), F32)


def column_of(table_ref, index):
    lanes = lax.broadcasted_iota(jnp.int32, (FIB, TABLE), 1)
    return jnp.sum(jnp.where(lanes == index, table_ref[...], 0.0), axis=1, keepdims=True).astype(jnp.int32)


def looped(count, inner, body):
    def several(i, carry):
        for k in range(inner):
            body(i * inner + k)
        return carry

    lax.fori_loop(0, count // inner, several, 0)


def block_at(b):
    return pl.ds(pl.multiple_of(b * BLK, BLK), BLK)


def slab_column(index):
    return (index & 1) * ROWS + (index >> 1)


def natural_column(index):
    return ((index >> 3) & 1) * 128 + (index >> 4) * 8 + (index & 7)


def first_kernel(
    where_ref, m_ref, r_ref, table_ref, got_ref, base_ref, next_ref, fire_ref, keep_ref, send_ref, sums_ref, trains_ref
):
    clear_ends(sums_ref)
    for s in range(32):
        trains_ref[pl.ds(2 * s, 2), :] = got_ref[s, pl.ds(0, 2), :]
    units = one_hot(table_ref[:, NBLK : NBLK + 1].astype(jnp.int32), 64)
    fires = dot(units, trains_ref[...].astype(BF16))[:, 64 : 64 + STEPS]
    fire_ref[...] = fires
    fire = fires[:, 0:1]
    place = table_ref[:, NBLK + 1 : NBLK + 2]

    def block(b):
        here = block_at(b)
        current, base, following = advance(m_ref[:, here], r_ref[:, here], fire, place, b * BLK)
        base_ref[:, here] = base
        next_ref[:, here] = following
        hot = one_hot(slab_column(column_of(table_ref, b)), COLS)
        sums_ref[pl.ds(pl.multiple_of(8 + b * BLK, 8), BLK), :] = deposit(current, hot)

    looped(NBLK, UNROLL, block)
    put_halves(where_ref, sums_ref, keep_ref, send_ref)


def first_call(where, m, r, table, got):
    state = shaped(FIB, PTS)
    return run(
        first_kernel,
        "first_deposit",
        (state, state, shaped(FIB, STEPS), shaped(HALF, COLS), shaped(HALF, COLS)),
        (where, m, r, table, got),
        [SUMS, pltpu.VMEM((64, 128), F32)],
        flops=6 << 30,
        moved=12 << 20,
        megabytes=6,
    )


def step_kernel(step, *refs):
    natural = step == 0
    last = step == STEPS - 1
    where_ref, own_ref, other_ref, base_ref, next_ref, table_ref, fire_ref, high_ref, low_ref = refs[:9]
    if last:
        m_out, field_ref, rhs_high, rhs_low, hot_ref = refs[9:]
    else:
        base_out, next_out, keep_ref, send_ref, field_ref, rhs_high, rhs_low, hot_ref, sums_ref, m_out = refs[9:]
    core, y, z = where_ref[0], where_ref[1], where_ref[2]

    def chunk(j):
        yy, zz = j >> 2, j & 3
        index = lax.rem(z - zz + 4, 4) * 4 + lax.rem(y - yy + 4, 4)
        first = pl.multiple_of(index * CHUNK, 8)
        for half, ref in ((core, own_ref), (1 - core, other_ref)):
            if natural:
                start = pl.multiple_of(half * 128 + j * 8, 8)
                for t in range(PTS // TILE):
                    field_ref[pl.ds(start, 8), t * TILE : (t + 1) * TILE] = ref[pl.ds(first + 8 * t, 8), :]
            else:
                start = pl.multiple_of(half * CPART + j * CHUNK, 8)
                field_ref[pl.ds(start, CHUNK), :] = ref[pl.ds(first, CHUNK), :]

    looped(16, 2, chunk)

    def sample(b):
        here = block_at(b)
        index = column_of(table_ref, b)
        hot = one_hot(natural_column(index) if natural else slab_column(index), COLS)
        if not last:
            hot_ref[b] = one_hot(slab_column(index), COLS) if natural else hot
        if natural:
            high, low = split(field_ref[:, here])
            sampled = dot(hot, high) + dot(hot, low)
        else:
            high, low = split(field_ref[here, :])
            sampled = dot(hot, high, ((1,), (1,))) + dot(hot, low, ((1,), (1,)))
        high, low = split(base_ref[:, here] + TIME_STEP * sampled)
        rhs_high[:, here] = high
        rhs_low[:, here] = low

    looped(NBLK, UNROLL, sample)

    def product(t):
        here = pl.ds(pl.multiple_of(t * TILE, TILE), TILE)
        m_out[:, here] = (
            dot(rhs_high[...], high_ref[:, here])
            + dot(rhs_low[...], high_ref[:, here])
            + dot(rhs_high[...], low_ref[:, here])
        )

    looped(PTS // TILE, PRODUCTS, product)
    if last:
        return
    clear_ends(sums_ref)
    place = table_ref[:, NBLK + 1 : NBLK + 2]
    fire = fire_ref[:, step + 1 : step + 2]

    def block(b):
        here = block_at(b)
        current, base, following = advance(m_out[:, here], next_ref[:, here], fire, place, b * BLK)
        base_out[:, here] = base
        next_out[:, here] = following
        sums_ref[pl.ds(pl.multiple_of(8 + b * BLK, 8), BLK), :] = deposit(current, hot_ref[b])

    looped(NBLK, UNROLL, block)
    put_halves(where_ref, sums_ref, keep_ref, send_ref)


def step_call(step, *operands):
    last = step == STEPS - 1
    state = shaped(FIB, PTS)
    field = (COLS, PTS) if step == 0 else (PTS, COLS)
    scratch = [pltpu.VMEM(field, F32), pltpu.VMEM((FIB, PTS), BF16), pltpu.VMEM((FIB, PTS), BF16)]
    scratch += [pltpu.VMEM((NBLK, FIB, COLS), BF16)]
    if last:
        out_shape = (state,)
    else:
        out_shape = (state, state, shaped(HALF, COLS), shaped(HALF, COLS))
        scratch += [SUMS, pltpu.VMEM((FIB, PTS), F32)]
    return run(
        functools.partial(step_kernel, step),
        "fibre_step",
        out_shape,
        operands,
        scratch,
        flops=2 * 3 * FIB * PTS * PTS,
        moved=20 << 20,
        megabytes=12,
    )


def parts_kernel(whole_ref, high_ref, low_ref):
    high, low = split(whole_ref[...])
    high_ref[...] = high
    low_ref[...] = low


def cable_parts(cable):
    rows = pl.BlockSpec((TILE, PTS), lambda i: (i, 0))
    return pl.pallas_call(
        parts_kernel,
        name="cable_parts",
        grid=(PTS // TILE,),
        out_shape=(shaped(PTS, PTS, dtype=BF16),) * 2,
        in_specs=[rows],
        out_specs=(rows, rows),
        cost_estimate=pl.CostEstimate(flops=1 << 23, bytes_accessed=18 << 20, transcendentals=0),
        compiler_params=pltpu.CompilerParams(vmem_limit_bytes=10 << 20),
    )(cable)


def y_pack_kernel(where_ref, keep_ref, got_ref, piece_ref, mine_ref, one_ref, two_ref, three_ref):
    y = where_ref[1]
    piece = piece_ref[...]
    for k, out in enumerate((mine_ref, one_ref, two_ref, three_ref)):
        here = pl.ds(pl.multiple_of(lax.rem(y + k, 4) * YPART, 8), YWIN)
        out[pl.ds(0, YWIN), :] = keep_ref[here, :] + got_ref[here, :]
        if k:
            out[pl.ds(YWIN, CHUNK), :] = piece


def y_pack(where, keep, got, piece):
    load = shaped(LOAD, COLS)
    return run(y_pack_kernel, "y_pack", (shaped(YWIN, COLS), load, load, load), (where, keep, got, piece))


def z_pack_kernel(where_ref, mine_ref, piece_ref, got1, got2, got3, own_ref, group_ref, *outs):
    z = where_ref[2]
    group = [piece_ref[...]] + [got[pl.ds(YWIN, CHUNK), :] for got in (got1, got2, got3)]
    for k, part in enumerate(group):
        group_ref[pl.ds(k * CHUNK, CHUNK), :] = part
    for k, out in enumerate((own_ref,) + outs):
        here = pl.ds(pl.multiple_of(lax.rem(z + k, 4) * CHUNK, 8), WIN)
        out[pl.ds(0, WIN), :] = mine_ref[here, :] + got1[here, :] + got3[here, :] + got2[here, :]
        if k:
            for i, part in enumerate(group):
                out[pl.ds(WIN + i * CHUNK, CHUNK), :] = part


def z_pack(where, mine, piece, gots):
    load = shaped(LOAD, COLS)
    return run(
        z_pack_kernel,
        "z_pack",
        (shaped(WIN, COLS), shaped(YPART, COLS), load, load, load),
        (where, mine, piece, *gots),
    )


def place_of(y, z, yy, zz):
    return lax.rem(z - zz + 4, 4) * 4 + lax.rem(y - yy + 4, 4)


def z_join_kernel(where_ref, own_ref, group_ref, got1, got2, got3, source_ref, held_ref, rim_ref):
    core, y, z = where_ref[0], where_ref[1], where_ref[2]
    here = pl.ds(0, WIN)
    source_ref[...] = own_ref[...] + got1[here, :] + got3[here, :] + got2[here, :]
    held_ref[pl.ds(0, YPART), :] = group_ref[...]
    for k, got in enumerate((got1, got2, got3)):
        held_ref[pl.ds((k + 1) * YPART, YPART), :] = got[pl.ds(WIN, YPART), :]
    top = pl.multiple_of(place_of(y, z, 3, 3) * CHUNK + CHUNK - 8, 8)
    bottom = pl.multiple_of(place_of(y, z, 0, 0) * CHUNK, 8)
    rim_ref[...] = jnp.where(core == 0, held_ref[pl.ds(top, 8), :], held_ref[pl.ds(bottom, 8), :])


def z_join(where, own, group, gots):
    out_shape = (shaped(WIN, COLS), shaped(CPART, COLS), shaped(8, COLS))
    return run(z_join_kernel, "z_join", out_shape, (where, own, group, *gots))


def message_kernel(where_ref, source_ref, held_ref, rim_ref, out_ref):
    core, y, z = where_ref[0], where_ref[1], where_ref[2]
    chunk = core * 16 + y * 4 + z
    out_ref[pl.ds(0, WIN), :] = source_ref[...]

    def rows(which, start):
        kept = jnp.clip(which, 0, 31)
        index = place_of(y, z, (kept >> 2) & 3, kept & 3)
        here = pl.ds(pl.multiple_of(index * CHUNK + start, 8), 8)
        found = jnp.where((kept >> 4) == core, held_ref[here, :], rim_ref[...])
        return pltpu.roll(jnp.where(which == kept, found, 0.0), 4, 0)

    below = rows(chunk - 1, CHUNK - 8)
    above = rows(chunk + 1, 0)
    level = lax.broadcasted_iota(jnp.int32, (8, COLS), 0)
    out_ref[pl.ds(WIN, 8), :] = jnp.where(level < HALO, below, above)


def message(where, source, held, rim):
    return run(message_kernel, "message", shaped(WIN + 8, COLS), (where, source, held, rim))


def relax_kernel(step, *refs):
    fresh = step == 0
    last = step == STEPS - 1
    refs = list(refs)
    where_ref = refs.pop(0)
    pool = where_ref[3]
    message_refs = [refs.pop(0) for _ in range(4)]
    if fresh:
        slab_refs = [refs.pop(0) for _ in range(4)]
    else:
        state_ref, gain_ref = refs.pop(0), refs.pop(0)
    if not last:
        state_out = refs.pop(0)
    own_out = refs.pop(0)
    if fresh:
        gain_ref = refs.pop(0)
    field_a, field_b, msgs, source = refs[:4]
    for k, ref in enumerate(message_refs):
        msgs[k] = ref[...]
    if fresh:
        state_ref = state_out
        for k, ref in enumerate(slab_refs):
            state_ref[k] = ref[0]
            gain_ref[k] = ref[1]
    lanes = lax.broadcasted_iota(jnp.int32, (WIN, ROWS), 1)
    zeros = jnp.zeros((WIN + 16, ROWS), F32)
    edge = jnp.zeros((8, ROWS), F32)
    for field in (field_a, field_b):
        field[0] = zeros
        field[9] = zeros
        for x in range(8):
            field[x + 1, pl.ds(0, 8), :] = edge
            field[x + 1, pl.ds(WIN + 8, 8), :] = edge
    for p in range(4):
        near = lax.rem(pool - p + 4, 4)
        for i in range(2):
            x = 2 * p + i
            lane = pl.ds(i * ROWS, ROWS)
            field_a[x + 1, pl.ds(8, WIN), :] = state_ref[near, i]
            if not fresh:
                field_a[x + 1, pl.ds(8, HALO), :] = msgs[near, pl.ds(WIN, HALO), lane]
                field_a[x + 1, pl.ds(8 + HALO + CHUNK, HALO), :] = msgs[near, pl.ds(WIN + HALO, HALO), lane]
            source[x] = SOURCE_GAIN * msgs[near, pl.ds(0, WIN), lane]
    def sweep(old, new):
        for p in range(4):
            near = lax.rem(pool - p + 4, 4)
            for i in range(2):
                x = 2 * p + i
                centre = old[x + 1, pl.ds(8, WIN), :]
                total = source[x] + old[x, pl.ds(8, WIN), :] + old[x + 2, pl.ds(8, WIN), :]
                total = total + old[x + 1, pl.ds(7, WIN), :] + old[x + 1, pl.ds(9, WIN), :]
                total = total + jnp.where(lanes == 0, 0.0, pltpu.roll(centre, 1, 1))
                total = total + jnp.where(lanes == ROWS - 1, 0.0, pltpu.roll(centre, ROWS - 1, 1))
                new[x + 1, pl.ds(8, WIN), :] = (1.0 - RELAX_WEIGHT) * centre + gain_ref[near, i] * total

    def both(_, carry):
        sweep(field_a, field_b)
        sweep(field_b, field_a)
        return carry

    lax.fori_loop(0, SWEEPS // 2, both, 0)
    old = field_a
    if last:
        for i in range(2):
            flat = old[2 * pool + i + 1, pl.ds(8, WIN), :]
            refs[4][...] = jnp.zeros((ROWS, ROWS), F32)
            refs[4][pl.ds(0, WIN), :] = flat
            turned = refs[4][...].T
            for s in range(32):
                own_out[s, pl.ds(4 * i, 4), :] = turned[4 * s : 4 * s + 4, :]
        return
    for p in range(4):
        near = lax.rem(pool - p + 4, 4)
        for i in range(2):
            state_out[near, i] = old[2 * p + i + 1, pl.ds(8, WIN), :]
    for i in range(2):
        own_out[:, i * ROWS : (i + 1) * ROWS] = old[2 * pool + i + 1, pl.ds(8 + HALO, CHUNK), :]


def relax(step, where, msgs, extra):
    state = shaped(4, 2, WIN, ROWS)
    own = shaped(CHUNK, COLS)
    out_shape = (state, own)
    if step == 0:
        out_shape = (state, own, state)
    if step == STEPS - 1:
        out_shape = (shaped(32, 8, ROWS),)
    scratch = [
        pltpu.VMEM((10, WIN + 16, ROWS), F32),
        pltpu.VMEM((10, WIN + 16, ROWS), F32),
        pltpu.VMEM((4, WIN + 8, COLS), F32),
        pltpu.VMEM((8, WIN, ROWS), F32),
        pltpu.VMEM((ROWS, ROWS), F32),
    ]
    return run(functools.partial(relax_kernel, step), "relax", out_shape, (where, *msgs, *extra), scratch)


def chunk_parts(s):
    core, z, y = s % 2, (s // 2) % 4, s // 8
    return core * 16 + y * 4 + z


def open_kernel(where_ref, potential_ref, reaction_ref, spikes_ref, out_ref, wide_ref, flags_ref):
    wide_ref[...] = jnp.zeros((16, PTS + 256), F32)
    flags_ref[...] = jnp.zeros((16, 128), F32)
    flags_ref[pl.ds(0, 2), 64 : 64 + STEPS] = spikes_ref[...].astype(F32)
    for row in range(4):
        for x in range(2):
            wide_ref[4 * x + row, pl.ds(128, PTS)] = potential_ref[row, x, :]
            wide_ref[8 + 4 * x + row, pl.ds(128, PTS)] = RELAX_WEIGHT / (6.0 + reaction_ref[row, x, :])
    lanes = lax.broadcasted_iota(jnp.int32, (16, 128), 1)
    for s in range(32):
        window = wide_ref[:, pl.ds(128 + CHUNK * chunk_parts(s) - HALO, 128)]
        out_ref[s] = jnp.where(lanes < 64, window, flags_ref[...])


def open_pack(where, potential, reaction, spikes):
    return run(
        open_kernel,
        "open_pack",
        shaped(32, 16, 128),
        (where, potential, reaction, spikes),
        [pltpu.VMEM((16, PTS + 256), F32), pltpu.VMEM((16, 128), F32)],
    )


def slab_kernel(where_ref, got_ref, out_ref, square_ref):
    for a in range(2):
        for x in range(2):
            for s in range(32):
                square_ref[pl.ds(4 * s, 4), :] = got_ref[s, pl.ds(8 * a + 4 * x, 4), :]
            out_ref[a, x] = square_ref[...].T[:WIN, :]


def slab_unpack(where, got):
    return run(slab_kernel, "slab", shaped(2, 2, WIN, ROWS), (where, got), [pltpu.VMEM((ROWS, ROWS), F32)])


def close_kernel(where_ref, got_ref, out_ref, wide_ref):
    for s in range(32):
        part = got_ref[s]
        wide_ref[:, pl.ds(CHUNK * chunk_parts(s), CHUNK)] = part[:, HALO : HALO + CHUNK]
    for row in range(4):
        for x in range(2):
            out_ref[row, x, :] = wide_ref[4 * x + row, :]


def close(where, got):
    return run(close_kernel, "close", shaped(4, 2, PTS), (where, got), [pltpu.VMEM((8, PTS), F32)])


def fib_of(y, z, core):
    return (y * 4 + z) * 2 + core


def shift(x, axis, by=1):
    if axis == "pool":
        return lax.ppermute(x, "pool", [(i, (i + by) % 4) for i in range(4)])
    pairs = []
    for y in range(4):
        for z in range(4):
            for core in range(2):
                to = {
                    "y": ((y + by) % 4, z, core),
                    "z": (y, (z + by) % 4, core),
                    "core": (y, z, 1 - core),
                }[axis]
                pairs.append((fib_of(y, z, core), fib_of(*to)))
    return lax.ppermute(x, "fib", pairs)


def to_three(parts, axis):
    got = {k: shift(parts[k - 1], axis, k) for k in (2, 1, 3)}
    return [got[1], got[2], got[3]]


def on_device(vm_state, recovery, spikes, owner, junction, column_index, cable_inverse, reaction, potential):
    fib = lax.axis_index("fib")
    pool = lax.axis_index("pool")
    core, z, y = fib % 2, (fib // 2) % 4, fib // 8
    where = jnp.stack([core, y, z, pool]).astype(jnp.int32)

    got = lax.all_to_all(open_pack(where, potential, reaction, spikes), "fib", 0, 0, tiled=True)
    table = jnp.concatenate([column_index, owner[:, None], junction[:, None]], axis=1).astype(F32)
    base, following, fire, keep, send = first_call(where, vm_state, recovery, table, got)
    piece = potential.reshape(8, PTS // TILE, TILE).transpose(1, 0, 2).reshape(CHUNK, COLS)

    for step in range(STEPS):
        mine, *loads = y_pack(where, keep, shift(send, "core"), piece)
        gots = to_three(loads, "y")
        if step == 0:
            cable, got, mine = lax.optimization_barrier((cable_inverse, got, mine))
            slab = slab_unpack(where, got)
            high, low = cable_parts(cable)
            extra = [slab] + to_three([slab] * 3, "pool")
            mine, high, low, *extra = lax.optimization_barrier((mine, high, low, *extra))
        own, group, *loads = z_pack(where, mine, piece, gots)
        source, held, rim = z_join(where, own, group, to_three(loads, "z"))
        other = shift(held, "core")
        note = message(where, source, held, shift(rim, "core"))
        msgs = to_three([note] * 3, "pool")
        other, note = lax.optimization_barrier((other, note))
        out = step_call(step, where, held, other, base, following, table, fire, high, low)
        *out, one, two, three = lax.optimization_barrier((*out, *msgs))
        relaxed = relax(step, where, [note, one, two, three], extra)
        if step == STEPS - 1:
            membrane, recovering = out[0], following
        else:
            base, following, keep, send = out
            piece = relaxed[1]
            if step == 0:
                gain = relaxed[2]
            extra = [relaxed[0], gain]
    extracell = close(where, lax.all_to_all(relaxed[0], "fib", 0, 0, tiled=True))
    return membrane, recovering, extracell


def solution(mesh):
    split_rows = P(("pool", "fib"), None)
    grid = P("fib", "pool", None)
    flat = P(("pool", "fib"))
    in_specs = (split_rows, split_rows, split_rows, flat, flat, split_rows, P(), grid, grid)
    return jax.shard_map(
        on_device, mesh=mesh, in_specs=in_specs, out_specs=(split_rows, split_rows, grid), check_vma=False
    )
```

```python
import functools

import jax
import jax.numpy as jnp
from jax import lax
from jax.experimental import pallas as pl
from jax.experimental.pallas import tpu as pltpu
from jax.sharding import PartitionSpec as P

STEPS = 4
SWEEPS = 4
TIME_STEP = 0.05
RECOVERY_RATE = 0.5
RECOVERY_SHIFT = 0.7
RECOVERY_SLOPE = 0.8
STIMULUS_GAIN = 4.0
JUNCTION_SPREAD = 8.0
SOURCE_GAIN = 0.25
RELAX_WEIGHT = 0.8

PTS = 1536
NBLK = 12
BLK = 128
FIB = 256
COLS = 256
ROWS = 128
CHUNK = 48
HALO = 4
WIN = CHUNK + 2 * HALO
YPART = 4 * CHUNK
CPART = 16 * CHUNK
YWIN = YPART + 2 * HALO
HALF = CPART + 2 * HALO
LOAD = YWIN + CHUNK
TILE = 256
TABLE = NBLK + 2
UNROLL = 6
PRODUCTS = 3
F32 = jnp.float32
BF16 = jnp.bfloat16
VMEM = pl.BlockSpec(memory_space=pltpu.VMEM)
SMEM = pl.BlockSpec(memory_space=pltpu.SMEM)


def shaped(*dims, dtype=F32):
    return jax.ShapeDtypeStruct(dims, dtype)


def run(kernel, name, out_shape, operands, scratch=(), flops=1 << 20, moved=1 << 20, megabytes=4):
    return pl.pallas_call(
        kernel,
        name=name,
        out_shape=out_shape,
        in_specs=[SMEM] + [VMEM] * (len(operands) - 1),
        out_specs=jax.tree.map(lambda _: VMEM, out_shape),
        scratch_shapes=scratch,
        cost_estimate=pl.CostEstimate(flops=flops, bytes_accessed=moved, transcendentals=0),
        compiler_params=pltpu.CompilerParams(vmem_limit_bytes=megabytes << 20),
    )(*operands)


def split(x):
    high = x.astype(BF16)
    return high, (x - high.astype(F32)).astype(BF16)


def dot(a, b, dims=((1,), (0,))):
    return lax.dot_general(a, b, (dims, ((), ())), preferred_element_type=F32)


def one_hot(column, width):
    lanes = lax.broadcasted_iota(jnp.int32, (column.shape[0], width), 1)
    return jnp.where(column == lanes, 1.0, 0.0).astype(BF16)


def advance(m, r, fire, place, start):
    width = m.shape[1]
    at = (lax.broadcasted_iota(jnp.int32, (1, width), 1) + start).astype(F32)
    offsets = (at - place) * (1.0 / JUNCTION_SPREAD)
    wave = jnp.exp(-offsets * offsets)
    current = m - m * m * m * (1.0 / 3.0) - r + (STIMULUS_GAIN * fire) * wave
    base = m + TIME_STEP * current
    following = r + TIME_STEP * RECOVERY_RATE * (m + RECOVERY_SHIFT - RECOVERY_SLOPE * r)
    return current, base, following


def deposit(current, hot):
    high, low = split(current.T)
    return dot(high, hot) + dot(low, hot)


def clear_ends(sums_ref):
    zero = jnp.zeros((8, COLS), F32)
    sums_ref[pl.ds(0, 8), :] = zero
    sums_ref[pl.ds(8 + PTS, 8), :] = zero


def put_halves(where_ref, sums_ref, keep_ref, send_ref):
    for core in range(2):

        @pl.when(where_ref[0] == core)
        def _():
            keep_ref[...] = sums_ref[pl.ds(8 - HALO + CPART * core, HALF), :]
            send_ref[...] = sums_ref[pl.ds(8 - HALO + CPART * (1 - core), HALF), :]


SUMS = pltpu.VMEM((PTS + 16, COLS), F32)


def column_of(table_ref, index):
    lanes = lax.broadcasted_iota(jnp.int32, (FIB, TABLE), 1)
    return jnp.sum(jnp.where(lanes == index, table_ref[...], 0.0), axis=1, keepdims=True).astype(jnp.int32)


def looped(count, inner, body):
    def several(i, carry):
        for k in range(inner):
            body(i * inner + k)
        return carry

    lax.fori_loop(0, count // inner, several, 0)


def block_at(b):
    return pl.ds(pl.multiple_of(b * BLK, BLK), BLK)


def slab_column(index):
    return (index & 1) * ROWS + (index >> 1)


def natural_column(index):
    return ((index >> 3) & 1) * 128 + (index >> 4) * 8 + (index & 7)


def first_kernel(
    where_ref, m_ref, r_ref, table_ref, got_ref, base_ref, next_ref, fire_ref, keep_ref, send_ref, sums_ref, trains_ref
):
    clear_ends(sums_ref)
    for s in range(32):
        trains_ref[pl.ds(2 * s, 2), :] = got_ref[s, pl.ds(0, 2), :]
    units = one_hot(table_ref[:, NBLK : NBLK + 1].astype(jnp.int32), 64)
    fires = dot(units, trains_ref[...].astype(BF16))[:, 64 : 64 + STEPS]
    fire_ref[...] = fires
    fire = fires[:, 0:1]
    place = table_ref[:, NBLK + 1 : NBLK + 2]

    def block(b):
        here = block_at(b)
        current, base, following = advance(m_ref[:, here], r_ref[:, here], fire, place, b * BLK)
        base_ref[:, here] = base
        next_ref[:, here] = following
        hot = one_hot(slab_column(column_of(table_ref, b)), COLS)
        sums_ref[pl.ds(pl.multiple_of(8 + b * BLK, 8), BLK), :] = deposit(current, hot)

    looped(NBLK, UNROLL, block)
    put_halves(where_ref, sums_ref, keep_ref, send_ref)


def first_call(where, m, r, table, got):
    state = shaped(FIB, PTS)
    return run(
        first_kernel,
        "first_deposit",
        (state, state, shaped(FIB, STEPS), shaped(HALF, COLS), shaped(HALF, COLS)),
        (where, m, r, table, got),
        [SUMS, pltpu.VMEM((64, 128), F32)],
        flops=6 << 30,
        moved=12 << 20,
        megabytes=6,
    )


def step_kernel(step, *refs):
    natural = step == 0
    last = step == STEPS - 1
    where_ref, own_ref, other_ref, base_ref, next_ref, table_ref, fire_ref, high_ref, low_ref = refs[:9]
    if last:
        m_out, field_ref, rhs_high, rhs_low, hot_ref = refs[9:]
    else:
        base_out, next_out, keep_ref, send_ref, field_ref, rhs_high, rhs_low, hot_ref, sums_ref, m_out = refs[9:]
    core, y, z = where_ref[0], where_ref[1], where_ref[2]

    def chunk(j):
        yy, zz = j >> 2, j & 3
        index = lax.rem(z - zz + 4, 4) * 4 + lax.rem(y - yy + 4, 4)
        first = pl.multiple_of(index * CHUNK, 8)
        for half, ref in ((core, own_ref), (1 - core, other_ref)):
            if natural:
                start = pl.multiple_of(half * 128 + j * 8, 8)
                for t in range(PTS // TILE):
                    field_ref[pl.ds(start, 8), t * TILE : (t + 1) * TILE] = ref[pl.ds(first + 8 * t, 8), :]
            else:
                start = pl.multiple_of(half * CPART + j * CHUNK, 8)
                field_ref[pl.ds(start, CHUNK), :] = ref[pl.ds(first, CHUNK), :]

    looped(16, 2, chunk)

    def sample(b):
        here = block_at(b)
        index = column_of(table_ref, b)
        hot = one_hot(natural_column(index) if natural else slab_column(index), COLS)
        if not last:
            hot_ref[b] = one_hot(slab_column(index), COLS) if natural else hot
        if natural:
            high, low = split(field_ref[:, here])
            sampled = dot(hot, high) + dot(hot, low)
        else:
            high, low = split(field_ref[here, :])
            sampled = dot(hot, high, ((1,), (1,))) + dot(hot, low, ((1,), (1,)))
        high, low = split(base_ref[:, here] + TIME_STEP * sampled)
        rhs_high[:, here] = high
        rhs_low[:, here] = low

    looped(NBLK, UNROLL, sample)

    def product(t):
        here = pl.ds(pl.multiple_of(t * TILE, TILE), TILE)
        m_out[:, here] = (
            dot(rhs_high[...], high_ref[:, here])
            + dot(rhs_low[...], high_ref[:, here])
            + dot(rhs_high[...], low_ref[:, here])
        )

    looped(PTS // TILE, PRODUCTS, product)
    if last:
        return
    clear_ends(sums_ref)
    place = table_ref[:, NBLK + 1 : NBLK + 2]
    fire = fire_ref[:, step + 1 : step + 2]

    def block(b):
        here = block_at(b)
        current, base, following = advance(m_out[:, here], next_ref[:, here], fire, place, b * BLK)
        base_out[:, here] = base
        next_out[:, here] = following
        sums_ref[pl.ds(pl.multiple_of(8 + b * BLK, 8), BLK), :] = deposit(current, hot_ref[b])

    looped(NBLK, UNROLL, block)
    put_halves(where_ref, sums_ref, keep_ref, send_ref)


def step_call(step, *operands):
    last = step == STEPS - 1
    state = shaped(FIB, PTS)
    field = (COLS, PTS) if step == 0 else (PTS, COLS)
    scratch = [pltpu.VMEM(field, F32), pltpu.VMEM((FIB, PTS), BF16), pltpu.VMEM((FIB, PTS), BF16)]
    scratch += [pltpu.VMEM((NBLK, FIB, COLS), BF16)]
    if last:
        out_shape = (state,)
    else:
        out_shape = (state, state, shaped(HALF, COLS), shaped(HALF, COLS))
        scratch += [SUMS, pltpu.VMEM((FIB, PTS), F32)]
    return run(
        functools.partial(step_kernel, step),
        "fibre_step",
        out_shape,
        operands,
        scratch,
        flops=2 * 3 * FIB * PTS * PTS,
        moved=20 << 20,
        megabytes=12,
    )


def parts_kernel(whole_ref, high_ref, low_ref):
    high, low = split(whole_ref[...])
    high_ref[...] = high
    low_ref[...] = low


def cable_parts(cable):
    rows = pl.BlockSpec((TILE, PTS), lambda i: (i, 0))
    return pl.pallas_call(
        parts_kernel,
        name="cable_parts",
        grid=(PTS // TILE,),
        out_shape=(shaped(PTS, PTS, dtype=BF16),) * 2,
        in_specs=[rows],
        out_specs=(rows, rows),
        cost_estimate=pl.CostEstimate(flops=1 << 23, bytes_accessed=18 << 20, transcendentals=0),
        compiler_params=pltpu.CompilerParams(vmem_limit_bytes=10 << 20),
    )(cable)


def place_of(y, z, yy, zz):
    return lax.rem(z - zz + 4, 4) * 4 + lax.rem(y - yy + 4, 4)


LEFT = slice(0, ROWS)
RIGHT = slice(ROWS, COLS)
FOUR = 4 * WIN


def rows_at(start, size):
    return pl.ds(pl.multiple_of(start, 8), size)


def first_pack_kernel(where_ref, keep_ref, got_ref, piece_ref, mine_l, mine_r, *outs):
    y, z = where_ref[1], where_ref[2]
    for k, out in enumerate((mine_l,) + outs[:3]):
        here = rows_at(lax.rem(y + k, 4) * YPART, YWIN)
        out[pl.ds(0, YWIN), :] = keep_ref[here, LEFT] + got_ref[here, LEFT]
        if k:
            out[pl.ds(YWIN, CHUNK), :] = piece_ref[:, LEFT]
    for k, out in enumerate((mine_r,) + outs[3:]):
        for yy in range(4):
            here = rows_at(yy * YPART + lax.rem(z + k, 4) * CHUNK, WIN)
            out[pl.ds(yy * WIN, WIN), :] = keep_ref[here, RIGHT] + got_ref[here, RIGHT]
        if k:
            out[pl.ds(FOUR, CHUNK), :] = piece_ref[:, RIGHT]


def first_pack(where, keep, got, piece):
    out = (shaped(YWIN, ROWS), shaped(FOUR, ROWS)) + (shaped(YWIN + CHUNK, ROWS),) * 3 + (shaped(FOUR + CHUNK, ROWS),) * 3
    mine_l, mine_r, *loads = run(first_pack_kernel, "first_pack", out, (where, keep, got, piece))
    return mine_l, mine_r, loads[:3], loads[3:]


def second_pack_kernel(where_ref, mine_l, mine_r, piece_ref, l1, l2, l3, r1, r2, r3, own_ref, group_l, group_r, *outs):
    y, z = where_ref[1], where_ref[2]
    for side, group, size, gots in ((LEFT, group_l, YWIN, (l1, l2, l3)), (RIGHT, group_r, FOUR, (r1, r2, r3))):
        parts = [piece_ref[:, side]] + [got[pl.ds(size, CHUNK), :] for got in gots]
        for i, part in enumerate(parts):
            group[pl.ds(i * CHUNK, CHUNK), :] = part
    for k in range(4):
        here = rows_at(lax.rem(z + k, 4) * CHUNK, WIN)
        left = mine_l[here, :] + l1[here, :] + l3[here, :] + l2[here, :]
        here = rows_at(lax.rem(y + k, 4) * WIN, WIN)
        right = mine_r[here, :] + r1[here, :] + r3[here, :] + r2[here, :]
        if k == 0:
            own_ref[:, LEFT] = left
            own_ref[:, RIGHT] = right
        else:
            outs[k - 1][pl.ds(0, WIN), :] = left
            outs[k - 1][pl.ds(WIN, YPART), :] = group_l[...]
            outs[k + 2][pl.ds(0, WIN), :] = right
            outs[k + 2][pl.ds(WIN, YPART), :] = group_r[...]


def second_pack(where, mine_l, mine_r, piece, gots_l, gots_r):
    group = shaped(YPART, ROWS)
    out = (shaped(WIN, COLS), group, group) + (shaped(WIN + YPART, ROWS),) * 6
    own, group_l, group_r, *loads = run(
        second_pack_kernel, "second_pack", out, (where, mine_l, mine_r, piece, *gots_l, *gots_r)
    )
    return own, group_l, group_r, loads[:3], loads[3:]


def join_kernel(where_ref, own_ref, group_l, group_r, l1, l2, l3, r1, r2, r3, source_ref, held_ref, rim_ref):
    core, y, z = where_ref[0], where_ref[1], where_ref[2]
    here = pl.ds(0, WIN)
    source_ref[:, LEFT] = own_ref[:, LEFT] + l1[here, :] + l3[here, :] + l2[here, :]
    source_ref[:, RIGHT] = own_ref[:, RIGHT] + r1[here, :] + r3[here, :] + r2[here, :]
    held_ref[pl.ds(0, YPART), LEFT] = group_l[...]
    for k, got in enumerate((l1, l2, l3)):
        held_ref[pl.ds((k + 1) * YPART, YPART), LEFT] = got[pl.ds(WIN, YPART), :]
    for i in range(4):
        held_ref[pl.ds(i * YPART, CHUNK), RIGHT] = group_r[pl.ds(i * CHUNK, CHUNK), :]
        for k, got in enumerate((r1, r2, r3)):
            held_ref[pl.ds(i * YPART + (k + 1) * CHUNK, CHUNK), RIGHT] = got[pl.ds(WIN + i * CHUNK, CHUNK), :]
    top = rows_at(place_of(y, z, 3, 3) * CHUNK + CHUNK - 8, 8)
    bottom = rows_at(place_of(y, z, 0, 0) * CHUNK, 8)
    rim_ref[...] = jnp.where(core == 0, held_ref[top, :], held_ref[bottom, :])


def join(where, own, group_l, group_r, gots_l, gots_r):
    out_shape = (shaped(WIN, COLS), shaped(CPART, COLS), shaped(8, COLS))
    return run(join_kernel, "join", out_shape, (where, own, group_l, group_r, *gots_l, *gots_r))


def message_kernel(where_ref, source_ref, held_ref, rim_ref, out_ref):
    core, y, z = where_ref[0], where_ref[1], where_ref[2]
    chunk = core * 16 + y * 4 + z
    out_ref[pl.ds(0, WIN), :] = source_ref[...]

    def rows(which, start):
        kept = jnp.clip(which, 0, 31)
        index = place_of(y, z, (kept >> 2) & 3, kept & 3)
        here = pl.ds(pl.multiple_of(index * CHUNK + start, 8), 8)
        found = jnp.where((kept >> 4) == core, held_ref[here, :], rim_ref[...])
        return pltpu.roll(jnp.where(which == kept, found, 0.0), 4, 0)

    below = rows(chunk - 1, CHUNK - 8)
    above = rows(chunk + 1, 0)
    level = lax.broadcasted_iota(jnp.int32, (8, COLS), 0)
    out_ref[pl.ds(WIN, 8), :] = jnp.where(level < HALO, below, above)


def message(where, source, held, rim):
    return run(message_kernel, "message", shaped(WIN + 8, COLS), (where, source, held, rim))


def relax_kernel(step, *refs):
    fresh = step == 0
    last = step == STEPS - 1
    refs = list(refs)
    where_ref = refs.pop(0)
    pool = where_ref[3]
    message_refs = [refs.pop(0) for _ in range(4)]
    if fresh:
        slab_refs = [refs.pop(0) for _ in range(4)]
    else:
        state_ref, gain_ref = refs.pop(0), refs.pop(0)
    if not last:
        state_out = refs.pop(0)
    own_out = refs.pop(0)
    if fresh:
        gain_ref = refs.pop(0)
    field_a, field_b, msgs, source = refs[:4]
    for k, ref in enumerate(message_refs):
        msgs[k] = ref[...]
    if fresh:
        state_ref = state_out
        for k, ref in enumerate(slab_refs):
            state_ref[k] = ref[0]
            gain_ref[k] = ref[1]
    lanes = lax.broadcasted_iota(jnp.int32, (WIN, ROWS), 1)
    zeros = jnp.zeros((WIN + 16, ROWS), F32)
    edge = jnp.zeros((8, ROWS), F32)
    for field in (field_a, field_b):
        field[0] = zeros
        field[9] = zeros
        for x in range(8):
            field[x + 1, pl.ds(0, 8), :] = edge
            field[x + 1, pl.ds(WIN + 8, 8), :] = edge
    for p in range(4):
        near = lax.rem(pool - p + 4, 4)
        for i in range(2):
            x = 2 * p + i
            lane = pl.ds(i * ROWS, ROWS)
            field_a[x + 1, pl.ds(8, WIN), :] = state_ref[near, i]
            if not fresh:
                field_a[x + 1, pl.ds(8, HALO), :] = msgs[near, pl.ds(WIN, HALO), lane]
                field_a[x + 1, pl.ds(8 + HALO + CHUNK, HALO), :] = msgs[near, pl.ds(WIN + HALO, HALO), lane]
            source[x] = SOURCE_GAIN * msgs[near, pl.ds(0, WIN), lane]
    def sweep(old, new):
        for p in range(4):
            near = lax.rem(pool - p + 4, 4)
            for i in range(2):
                x = 2 * p + i
                centre = old[x + 1, pl.ds(8, WIN), :]
                total = source[x] + old[x, pl.ds(8, WIN), :] + old[x + 2, pl.ds(8, WIN), :]
                total = total + old[x + 1, pl.ds(7, WIN), :] + old[x + 1, pl.ds(9, WIN), :]
                total = total + jnp.where(lanes == 0, 0.0, pltpu.roll(centre, 1, 1))
                total = total + jnp.where(lanes == ROWS - 1, 0.0, pltpu.roll(centre, ROWS - 1, 1))
                new[x + 1, pl.ds(8, WIN), :] = (1.0 - RELAX_WEIGHT) * centre + gain_ref[near, i] * total

    def both(_, carry):
        sweep(field_a, field_b)
        sweep(field_b, field_a)
        return carry

    lax.fori_loop(0, SWEEPS // 2, both, 0)
    old = field_a
    if last:
        for i in range(2):
            flat = old[2 * pool + i + 1, pl.ds(8, WIN), :]
            refs[4][...] = jnp.zeros((ROWS, ROWS), F32)
            refs[4][pl.ds(0, WIN), :] = flat
            turned = refs[4][...].T
            for s in range(32):
                own_out[s, pl.ds(4 * i, 4), :] = turned[4 * s : 4 * s + 4, :]
        return
    for p in range(4):
        near = lax.rem(pool - p + 4, 4)
        for i in range(2):
            state_out[near, i] = old[2 * p + i + 1, pl.ds(8, WIN), :]
    for i in range(2):
        own_out[:, i * ROWS : (i + 1) * ROWS] = old[2 * pool + i + 1, pl.ds(8 + HALO, CHUNK), :]


def relax(step, where, msgs, extra):
    state = shaped(4, 2, WIN, ROWS)
    own = shaped(CHUNK, COLS)
    out_shape = (state, own)
    if step == 0:
        out_shape = (state, own, state)
    if step == STEPS - 1:
        out_shape = (shaped(32, 8, ROWS),)
    scratch = [
        pltpu.VMEM((10, WIN + 16, ROWS), F32),
        pltpu.VMEM((10, WIN + 16, ROWS), F32),
        pltpu.VMEM((4, WIN + 8, COLS), F32),
        pltpu.VMEM((8, WIN, ROWS), F32),
        pltpu.VMEM((ROWS, ROWS), F32),
    ]
    return run(functools.partial(relax_kernel, step), "relax", out_shape, (where, *msgs, *extra), scratch)


def chunk_parts(s):
    core, z, y = s % 2, (s // 2) % 4, s // 8
    return core * 16 + y * 4 + z


def open_kernel(where_ref, potential_ref, reaction_ref, spikes_ref, out_ref, piece_ref, wide_ref, flags_ref):
    wide_ref[...] = jnp.zeros((16, PTS + 256), F32)
    flags_ref[...] = jnp.zeros((16, 128), F32)
    flags_ref[pl.ds(0, 2), 64 : 64 + STEPS] = spikes_ref[...].astype(F32)
    for row in range(4):
        for x in range(2):
            wide_ref[4 * x + row, pl.ds(128, PTS)] = potential_ref[row, x, :]
            for t in range(PTS // TILE):
                piece_ref[8 * t + 2 * row + x, :] = potential_ref[row, x, t * TILE : (t + 1) * TILE]
            wide_ref[8 + 4 * x + row, pl.ds(128, PTS)] = RELAX_WEIGHT / (6.0 + reaction_ref[row, x, :])
    lanes = lax.broadcasted_iota(jnp.int32, (16, 128), 1)
    for s in range(32):
        window = wide_ref[:, pl.ds(128 + CHUNK * chunk_parts(s) - HALO, 128)]
        out_ref[s] = jnp.where(lanes < 64, window, flags_ref[...])


def open_pack(where, potential, reaction, spikes):
    return run(
        open_kernel,
        "open_pack",
        (shaped(32, 16, 128), shaped(CHUNK, COLS)),
        (where, potential, reaction, spikes),
        [pltpu.VMEM((16, PTS + 256), F32), pltpu.VMEM((16, 128), F32)],
    )


def slab_kernel(where_ref, got_ref, out_ref, square_ref):
    for a in range(2):
        for x in range(2):
            for s in range(32):
                square_ref[pl.ds(4 * s, 4), :] = got_ref[s, pl.ds(8 * a + 4 * x, 4), :]
            out_ref[a, x] = square_ref[...].T[:WIN, :]


def slab_unpack(where, got):
    return run(slab_kernel, "slab", shaped(2, 2, WIN, ROWS), (where, got), [pltpu.VMEM((ROWS, ROWS), F32)])


def close_kernel(where_ref, got_ref, out_ref, wide_ref):
    for s in range(32):
        part = got_ref[s]
        wide_ref[:, pl.ds(CHUNK * chunk_parts(s), CHUNK)] = part[:, HALO : HALO + CHUNK]
    for row in range(4):
        for x in range(2):
            out_ref[row, x, :] = wide_ref[4 * x + row, :]


def close(where, got):
    return run(close_kernel, "close", shaped(4, 2, PTS), (where, got), [pltpu.VMEM((8, PTS), F32)])


def fib_of(y, z, core):
    return (y * 4 + z) * 2 + core


def shift(x, axis, by=1):
    if axis == "pool":
        return lax.ppermute(x, "pool", [(i, (i + by) % 4) for i in range(4)])
    pairs = []
    for y in range(4):
        for z in range(4):
            for core in range(2):
                to = {
                    "y": ((y + by) % 4, z, core),
                    "z": (y, (z + by) % 4, core),
                    "core": (y, z, 1 - core),
                }[axis]
                pairs.append((fib_of(y, z, core), fib_of(*to)))
    return lax.ppermute(x, "fib", pairs)


def to_three(parts, axis, more=(), other=None):
    both = {}
    for k in (2, 1, 3):
        both[k] = shift(parts[k - 1], axis, k)
        if other:
            both[-k] = shift(more[k - 1], other, k)
    first = [both[k] for k in (1, 2, 3)]
    return (first, [both[-k] for k in (1, 2, 3)]) if other else first


def on_device(vm_state, recovery, spikes, owner, junction, column_index, cable_inverse, reaction, potential):
    fib = lax.axis_index("fib")
    pool = lax.axis_index("pool")
    core, z, y = fib % 2, (fib // 2) % 4, fib // 8
    where = jnp.stack([core, y, z, pool]).astype(jnp.int32)

    windows, piece = open_pack(where, potential, reaction, spikes)
    got = lax.all_to_all(windows, "fib", 0, 0, tiled=True)
    table = jnp.concatenate([column_index, owner[:, None], junction[:, None]], axis=1).astype(F32)
    slab = slab_unpack(where, got)
    base, following, fire, keep, send = first_call(where, vm_state, recovery, table, got)

    for step in range(STEPS):
        mine_l, mine_r, loads_l, loads_r = first_pack(where, keep, shift(send, "core"), piece)
        gots_l, gots_r = to_three(loads_l, "y", loads_r, "z")
        if step == 0:
            cable, slab, mine_l = lax.optimization_barrier((cable_inverse, slab, mine_l))
            high, low = cable_parts(cable)
            extra = [slab] + to_three([slab] * 3, "pool")
            mine_l, high, low, *extra = lax.optimization_barrier((mine_l, high, low, *extra))
        own, group_l, group_r, loads_l, loads_r = second_pack(where, mine_l, mine_r, piece, gots_l, gots_r)
        gots_l, gots_r = to_three(loads_l, "z", loads_r, "y")
        source, held, rim = join(where, own, group_l, group_r, gots_l, gots_r)
        rim, sent = lax.optimization_barrier((shift(rim, "core"), held))
        other = shift(sent, "core")
        note = message(where, source, held, rim)
        msgs = to_three([note] * 3, "pool")
        other, note = lax.optimization_barrier((other, note))
        out = step_call(step, where, held, other, base, following, table, fire, high, low)
        *out, one, two, three = lax.optimization_barrier((*out, *msgs))
        relaxed = relax(step, where, [note, one, two, three], extra)
        if step == STEPS - 1:
            membrane, recovering = out[0], following
        else:
            base, following, keep, send = out
            piece = relaxed[1]
            if step == 0:
                gain = relaxed[2]
            extra = [relaxed[0], gain]
    extracell = close(where, lax.all_to_all(relaxed[0], "fib", 0, 0, tiled=True))
    return membrane, recovering, extracell


def solution(mesh):
    split_rows = P(("pool", "fib"), None)
    grid = P("fib", "pool", None)
    flat = P(("pool", "fib"))
    in_specs = (split_rows, split_rows, split_rows, flat, flat, split_rows, P(), grid, grid)
    return jax.shard_map(
        on_device, mesh=mesh, in_specs=in_specs, out_specs=(split_rows, split_rows, grid), check_vma=False
    )
```

```python
import functools

import jax
import jax.numpy as jnp
from jax import lax
from jax.experimental import pallas as pl
from jax.experimental.pallas import tpu as pltpu
from jax.sharding import PartitionSpec as P

STEPS = 4
SWEEPS = 4
TIME_STEP = 0.05
RECOVERY_RATE = 0.5
RECOVERY_SHIFT = 0.7
RECOVERY_SLOPE = 0.8
STIMULUS_GAIN = 4.0
JUNCTION_SPREAD = 8.0
SOURCE_GAIN = 0.25
RELAX_WEIGHT = 0.8

PTS = 1536
NBLK = 12
BLK = 128
FIB = 256
COLS = 256
ROWS = 128
CHUNK = 48
HALO = 4
WIN = CHUNK + 2 * HALO
YPART = 4 * CHUNK
CPART = 16 * CHUNK
YWIN = YPART + 2 * HALO
HALF = CPART + 2 * HALO
LOAD = YWIN + CHUNK
TILE = 256
TABLE = NBLK + 2
UNROLL = 12
PRODUCTS = 6
F32 = jnp.float32
BF16 = jnp.bfloat16
VMEM = pl.BlockSpec(memory_space=pltpu.VMEM)
SMEM = pl.BlockSpec(memory_space=pltpu.SMEM)
FAR = pl.BlockSpec(memory_space=pltpu.HBM)


def in_hbm(x):
    return pltpu.with_memory_space_constraint(x, pltpu.HBM)


def shaped(*dims, dtype=F32):
    return jax.ShapeDtypeStruct(dims, dtype)


def run(kernel, name, out_shape, operands, scratch=(), flops=1 << 20, moved=1 << 20, megabytes=4, outside=()):
    return pl.pallas_call(
        kernel,
        name=name,
        out_shape=out_shape,
        in_specs=[SMEM] + [FAR if i in outside else VMEM for i in range(1, len(operands))],
        out_specs=jax.tree.map(lambda _: VMEM, out_shape),
        scratch_shapes=scratch,
        cost_estimate=pl.CostEstimate(flops=flops, bytes_accessed=moved, transcendentals=0),
        compiler_params=pltpu.CompilerParams(vmem_limit_bytes=megabytes << 20),
    )(*operands)


def split(x):
    high = x.astype(BF16)
    return high, (x - high.astype(F32)).astype(BF16)


def dot(a, b, dims=((1,), (0,))):
    return lax.dot_general(a, b, (dims, ((), ())), preferred_element_type=F32)


def one_hot(column, width):
    lanes = lax.broadcasted_iota(jnp.int32, (column.shape[0], width), 1)
    return jnp.where(column == lanes, 1.0, 0.0).astype(BF16)


def advance(m, r, fire, place, start):
    width = m.shape[1]
    at = (lax.broadcasted_iota(jnp.int32, (1, width), 1) + start).astype(F32)
    offsets = (at - place) * (1.0 / JUNCTION_SPREAD)
    wave = jnp.exp(-offsets * offsets)
    current = m - m * m * m * (1.0 / 3.0) - r + (STIMULUS_GAIN * fire) * wave
    base = m + TIME_STEP * current
    following = r + TIME_STEP * RECOVERY_RATE * (m + RECOVERY_SHIFT - RECOVERY_SLOPE * r)
    return current, base, following


def deposit(current, hot):
    high, low = split(current.T)
    return dot(high, hot) + dot(low, hot)


def clear_ends(sums_ref):
    zero = jnp.zeros((8, COLS), F32)
    sums_ref[pl.ds(0, 8), :] = zero
    sums_ref[pl.ds(8 + PTS, 8), :] = zero


def put_halves(where_ref, sums_ref, keep_ref, send_ref):
    for core in range(2):

        @pl.when(where_ref[0] == core)
        def _():
            keep_ref[...] = sums_ref[pl.ds(8 - HALO + CPART * core, HALF), :]
            send_ref[...] = sums_ref[pl.ds(8 - HALO + CPART * (1 - core), HALF), :]


SUMS = pltpu.VMEM((PTS + 16, COLS), F32)


def rows_at(start, size):
    return pl.ds(start if isinstance(start, int) else pl.multiple_of(start, 8), size)


def column_of(table_ref, index):
    if isinstance(index, int):
        return table_ref[:, index : index + 1].astype(jnp.int32)
    lanes = lax.broadcasted_iota(jnp.int32, (FIB, TABLE), 1)
    return jnp.sum(jnp.where(lanes == index, table_ref[...], 0.0), axis=1, keepdims=True).astype(jnp.int32)


def looped(count, inner, body):
    if inner == count:
        for k in range(count):
            body(k)
        return

    def several(i, carry):
        for k in range(inner):
            body(i * inner + k)
        return carry

    lax.fori_loop(0, count // inner, several, 0)


def block_at(b):
    if isinstance(b, int):
        return pl.ds(b * BLK, BLK)
    return pl.ds(pl.multiple_of(b * BLK, BLK), BLK)


def slab_column(index):
    return (index & 1) * ROWS + (index >> 1)


def first_kernel(
    where_ref, m_hbm, r_hbm, table_ref, got_ref, base_ref, next_ref, fire_ref, keep_ref, send_ref,
    sums_ref, trains_ref, m_ref, r_ref, sems,
):
    copies = []
    for t in range(PTS // TILE):
        here = pl.ds(t * TILE, TILE)
        for i, (source, target) in enumerate(((m_hbm, m_ref), (r_hbm, r_ref))):
            copy = pltpu.make_async_copy(source.at[:, here], target.at[:, here], sems.at[2 * t + i])
            copy.start()
            copies.append(copy)
    clear_ends(sums_ref)
    for s in range(32):
        trains_ref[pl.ds(2 * s, 2), :] = got_ref[s, pl.ds(0, 2), :]
    units = one_hot(table_ref[:, NBLK : NBLK + 1].astype(jnp.int32), 64)
    fires = dot(units, trains_ref[...].astype(BF16))[:, 64 : 64 + STEPS]
    fire_ref[...] = fires
    fire = fires[:, 0:1]
    place = table_ref[:, NBLK + 1 : NBLK + 2]

    for b in range(NBLK):
        if b % 2 == 0:
            copies[b].wait()
            copies[b + 1].wait()
        here = block_at(b)
        current, base, following = advance(m_ref[:, here], r_ref[:, here], fire, place, b * BLK)
        base_ref[:, here] = base
        next_ref[:, here] = following
        hot = one_hot(slab_column(column_of(table_ref, b)), COLS)
        sums_ref[rows_at(8 + b * BLK, BLK), :] = deposit(current, hot)
    put_halves(where_ref, sums_ref, keep_ref, send_ref)


def first_call(where, m, r, table, got):
    state = shaped(FIB, PTS)
    return run(
        first_kernel,
        "first_deposit",
        (state, state, shaped(FIB, STEPS), shaped(HALF, COLS), shaped(HALF, COLS)),
        (where, in_hbm(m), in_hbm(r), table, got),
        [
            SUMS,
            pltpu.VMEM((64, 128), F32),
            pltpu.VMEM((FIB, PTS), F32),
            pltpu.VMEM((FIB, PTS), F32),
            pltpu.SemaphoreType.DMA((NBLK,)),
        ],
        outside=(1, 2),
        flops=6 << 30,
        moved=12 << 20,
        megabytes=12,
    )


def step_kernel(last, *refs):
    where_ref, own_ref, other_ref, base_ref, next_ref, table_ref, fire_ref, high_ref, low_ref = refs[:9]
    if last:
        m_out, field_ref, rhs_high, rhs_low, hot_ref = refs[9:]
    else:
        base_out, next_out, fire_out, keep_ref, send_ref, field_ref, rhs_high, rhs_low, hot_ref, sums_ref, m_out = refs[9:]
    core, y, z = where_ref[0], where_ref[1], where_ref[2]

    for yy in range(4):
        for zz in range(4):
            first = rows_at(place_of(y, z, yy, zz) * CHUNK, CHUNK)
            for half, ref in ((core, own_ref), (1 - core, other_ref)):
                field_ref[rows_at(half * CPART + (4 * yy + zz) * CHUNK, CHUNK), :] = ref[first, :]

    def sample(b):
        here = block_at(b)
        hot = one_hot(slab_column(column_of(table_ref, b)), COLS)
        if not last:
            hot_ref[b] = hot
        high, low = split(field_ref[here, :])
        sampled = dot(hot, high, ((1,), (1,))) + dot(hot, low, ((1,), (1,)))
        high, low = split(base_ref[:, here] + TIME_STEP * sampled)
        rhs_high[:, here] = high
        rhs_low[:, here] = low

    looped(NBLK, UNROLL, sample)

    def product(t):
        here = pl.ds(t * TILE if isinstance(t, int) else pl.multiple_of(t * TILE, TILE), TILE)
        m_out[:, here] = (
            dot(rhs_high[...], high_ref[:, here])
            + dot(rhs_low[...], high_ref[:, here])
            + dot(rhs_high[...], low_ref[:, here])
        )

    looped(PTS // TILE, PRODUCTS, product)
    if last:
        return
    clear_ends(sums_ref)
    place = table_ref[:, NBLK + 1 : NBLK + 2]
    fire = fire_ref[:, 1:2]
    fire_out[:, : STEPS - 1] = fire_ref[:, 1:]
    fire_out[:, STEPS - 1 :] = fire_ref[:, :1]

    def block(b):
        here = block_at(b)
        current, base, following = advance(m_out[:, here], next_ref[:, here], fire, place, b * BLK)
        base_out[:, here] = base
        next_out[:, here] = following
        sums_ref[rows_at(8 + b * BLK, BLK), :] = deposit(current, hot_ref[b])

    looped(NBLK, UNROLL, block)
    put_halves(where_ref, sums_ref, keep_ref, send_ref)


def step_call(last, *operands):
    state = shaped(FIB, PTS)
    field = (PTS, COLS)
    scratch = [pltpu.VMEM(field, F32), pltpu.VMEM((FIB, PTS), BF16), pltpu.VMEM((FIB, PTS), BF16)]
    scratch += [pltpu.VMEM((NBLK, FIB, COLS), BF16)]
    if last:
        out_shape = (state,)
    else:
        out_shape = (state, state, shaped(FIB, STEPS), shaped(HALF, COLS), shaped(HALF, COLS))
        scratch += [SUMS, pltpu.VMEM((FIB, PTS), F32)]
    return run(
        functools.partial(step_kernel, last),
        "fibre_step",
        out_shape,
        operands,
        scratch,
        flops=2 * 3 * FIB * PTS * PTS,
        moved=20 << 20,
        megabytes=12,
    )


def parts_kernel(whole_ref, high_ref, low_ref):
    high, low = split(whole_ref[...])
    high_ref[...] = high
    low_ref[...] = low


def cable_parts(cable):
    rows = pl.BlockSpec((TILE, PTS), lambda i: (i, 0))
    return pl.pallas_call(
        parts_kernel,
        name="cable_parts",
        grid=(PTS // TILE,),
        out_shape=(shaped(PTS, PTS, dtype=BF16),) * 2,
        in_specs=[rows],
        out_specs=(rows, rows),
        cost_estimate=pl.CostEstimate(flops=1 << 23, bytes_accessed=18 << 20, transcendentals=0),
        compiler_params=pltpu.CompilerParams(vmem_limit_bytes=10 << 20),
    )(in_hbm(cable))


def place_of(y, z, yy, zz):
    return lax.rem(z - zz + 4, 4) * 4 + lax.rem(y - yy + 4, 4)


LEFT = slice(0, ROWS)
RIGHT = slice(ROWS, COLS)
FOUR = 4 * WIN


def first_pack_kernel(where_ref, keep_ref, got_ref, piece_ref, mine_l, mine_r, *outs):
    y, z = where_ref[1], where_ref[2]
    for k, out in enumerate((mine_l,) + outs[:3]):
        here = rows_at(lax.rem(y + k, 4) * YPART, YWIN)
        out[pl.ds(0, YWIN), :] = keep_ref[here, LEFT] + got_ref[here, LEFT]
        if k:
            out[pl.ds(YWIN, CHUNK), :] = piece_ref[:, LEFT]
    for k, out in enumerate((mine_r,) + outs[3:]):
        for yy in range(4):
            here = rows_at(yy * YPART + lax.rem(z + k, 4) * CHUNK, WIN)
            out[pl.ds(yy * WIN, WIN), :] = keep_ref[here, RIGHT] + got_ref[here, RIGHT]
        if k:
            out[pl.ds(FOUR, CHUNK), :] = piece_ref[:, RIGHT]


def first_pack(where, keep, got, piece):
    out = (shaped(YWIN, ROWS), shaped(FOUR, ROWS)) + (shaped(YWIN + CHUNK, ROWS),) * 3 + (shaped(FOUR + CHUNK, ROWS),) * 3
    mine_l, mine_r, *loads = run(first_pack_kernel, "first_pack", out, (where, keep, got, piece))
    return mine_l, mine_r, loads[:3], loads[3:]


def second_pack_kernel(where_ref, mine_l, mine_r, piece_ref, l1, l2, l3, r1, r2, r3, own_ref, group_l, group_r, *outs):
    y, z = where_ref[1], where_ref[2]
    for side, group, size, gots in ((LEFT, group_l, YWIN, (l1, l2, l3)), (RIGHT, group_r, FOUR, (r1, r2, r3))):
        parts = [piece_ref[:, side]] + [got[pl.ds(size, CHUNK), :] for got in gots]
        for i, part in enumerate(parts):
            group[pl.ds(i * CHUNK, CHUNK), :] = part
    for k in range(4):
        here = rows_at(lax.rem(z + k, 4) * CHUNK, WIN)
        left = mine_l[here, :] + l1[here, :] + l3[here, :] + l2[here, :]
        here = rows_at(lax.rem(y + k, 4) * WIN, WIN)
        right = mine_r[here, :] + r1[here, :] + r3[here, :] + r2[here, :]
        if k == 0:
            own_ref[:, LEFT] = left
            own_ref[:, RIGHT] = right
        else:
            outs[k - 1][pl.ds(0, WIN), :] = left
            outs[k - 1][pl.ds(WIN, YPART), :] = group_l[...]
            outs[k + 2][pl.ds(0, WIN), :] = right
            outs[k + 2][pl.ds(WIN, YPART), :] = group_r[...]


def second_pack(where, mine_l, mine_r, piece, gots_l, gots_r):
    group = shaped(YPART, ROWS)
    out = (shaped(WIN, COLS), group, group) + (shaped(WIN + YPART, ROWS),) * 6
    own, group_l, group_r, *loads = run(
        second_pack_kernel, "second_pack", out, (where, mine_l, mine_r, piece, *gots_l, *gots_r)
    )
    return own, group_l, group_r, loads[:3], loads[3:]


def join_kernel(where_ref, own_ref, group_l, group_r, l1, l2, l3, r1, r2, r3, source_ref, held_ref, rim_ref):
    core, y, z = where_ref[0], where_ref[1], where_ref[2]
    here = pl.ds(0, WIN)
    source_ref[:, LEFT] = own_ref[:, LEFT] + l1[here, :] + l3[here, :] + l2[here, :]
    source_ref[:, RIGHT] = own_ref[:, RIGHT] + r1[here, :] + r3[here, :] + r2[here, :]
    held_ref[pl.ds(0, YPART), LEFT] = group_l[...]
    for k, got in enumerate((l1, l2, l3)):
        held_ref[pl.ds((k + 1) * YPART, YPART), LEFT] = got[pl.ds(WIN, YPART), :]
    for i in range(4):
        held_ref[pl.ds(i * YPART, CHUNK), RIGHT] = group_r[pl.ds(i * CHUNK, CHUNK), :]
        for k, got in enumerate((r1, r2, r3)):
            held_ref[pl.ds(i * YPART + (k + 1) * CHUNK, CHUNK), RIGHT] = got[pl.ds(WIN + i * CHUNK, CHUNK), :]
    top = rows_at(place_of(y, z, 3, 3) * CHUNK + CHUNK - 8, 8)
    bottom = rows_at(place_of(y, z, 0, 0) * CHUNK, 8)
    rim_ref[...] = jnp.where(core == 0, held_ref[top, :], held_ref[bottom, :])


def join(where, own, group_l, group_r, gots_l, gots_r):
    out_shape = (shaped(WIN, COLS), shaped(CPART, COLS), shaped(8, COLS))
    return run(join_kernel, "join", out_shape, (where, own, group_l, group_r, *gots_l, *gots_r))


def message_kernel(where_ref, source_ref, held_ref, rim_ref, *refs):
    out_ref = refs[-1]
    if len(refs) == 2:
        for a in range(2):
            for x in range(2):
                out_ref[pl.ds(WIN + 8 + a * WIN, WIN), x * ROWS : (x + 1) * ROWS] = refs[0][a, x]
    core, y, z = where_ref[0], where_ref[1], where_ref[2]
    chunk = core * 16 + y * 4 + z
    out_ref[pl.ds(0, WIN), :] = source_ref[...]

    def rows(which, start):
        kept = jnp.clip(which, 0, 31)
        index = place_of(y, z, (kept >> 2) & 3, kept & 3)
        here = pl.ds(pl.multiple_of(index * CHUNK + start, 8), 8)
        found = jnp.where((kept >> 4) == core, held_ref[here, :], rim_ref[...])
        return pltpu.roll(jnp.where(which == kept, found, 0.0), 4, 0)

    below = rows(chunk - 1, CHUNK - 8)
    above = rows(chunk + 1, 0)
    level = lax.broadcasted_iota(jnp.int32, (8, COLS), 0)
    out_ref[pl.ds(WIN, 8), :] = jnp.where(level < HALO, below, above)


def message(where, source, held, rim, *slab):
    size = (WIN + 8) + 2 * WIN * len(slab)
    return run(message_kernel, "message", shaped(size, COLS), (where, source, held, rim, *slab))


def relax_kernel(fresh, last, *refs):
    refs = list(refs)
    where_ref = refs.pop(0)
    pool = where_ref[3]
    message_refs = [refs.pop(0) for _ in range(4)]
    if not fresh:
        state_ref, gain_ref = refs.pop(0), refs.pop(0)
    if not last:
        state_out = refs.pop(0)
    own_out = refs.pop(0)
    if fresh:
        gain_ref = refs.pop(0)
    field_a, field_b, msgs, source = refs[:4]
    for k, ref in enumerate(message_refs):
        msgs[k] = ref[...]
    lanes = lax.broadcasted_iota(jnp.int32, (WIN, ROWS), 1)
    zeros = jnp.zeros((WIN + 16, ROWS), F32)
    edge = jnp.zeros((8, ROWS), F32)
    for field in (field_a, field_b):
        field[0] = zeros
        field[9] = zeros
        for x in range(8):
            field[x + 1, pl.ds(0, 8), :] = edge
            field[x + 1, pl.ds(WIN + 8, 8), :] = edge
    for p in range(4):
        near = lax.rem(pool - p + 4, 4)
        for i in range(2):
            x = 2 * p + i
            lane = pl.ds(i * ROWS, ROWS)
            if fresh:
                field_a[x + 1, pl.ds(8, WIN), :] = msgs[near, pl.ds(WIN + 8, WIN), lane]
                gain_ref[near, i] = msgs[near, pl.ds(2 * WIN + 8, WIN), lane]
            else:
                field_a[x + 1, pl.ds(8, WIN), :] = state_ref[near, i]
            field_a[x + 1, pl.ds(8, HALO), :] = msgs[near, pl.ds(WIN, HALO), lane]
            field_a[x + 1, pl.ds(8 + HALO + CHUNK, HALO), :] = msgs[near, pl.ds(WIN + HALO, HALO), lane]
            source[x] = SOURCE_GAIN * msgs[near, pl.ds(0, WIN), lane]
    def sweep(old, new):
        for p in range(4):
            near = lax.rem(pool - p + 4, 4)
            for i in range(2):
                x = 2 * p + i
                centre = old[x + 1, pl.ds(8, WIN), :]
                total = source[x] + old[x, pl.ds(8, WIN), :] + old[x + 2, pl.ds(8, WIN), :]
                total = total + old[x + 1, pl.ds(7, WIN), :] + old[x + 1, pl.ds(9, WIN), :]
                total = total + jnp.where(lanes == 0, 0.0, pltpu.roll(centre, 1, 1))
                total = total + jnp.where(lanes == ROWS - 1, 0.0, pltpu.roll(centre, ROWS - 1, 1))
                new[x + 1, pl.ds(8, WIN), :] = (1.0 - RELAX_WEIGHT) * centre + gain_ref[near, i] * total

    def both(_, carry):
        sweep(field_a, field_b)
        sweep(field_b, field_a)
        return carry

    lax.fori_loop(0, SWEEPS // 2, both, 0)
    old = field_a
    if last:
        for i in range(2):
            flat = old[2 * pool + i + 1, pl.ds(8, WIN), :]
            refs[4][...] = jnp.zeros((ROWS, ROWS), F32)
            refs[4][pl.ds(0, WIN), :] = flat
            turned = refs[4][...].T
            for s in range(32):
                own_out[s, pl.ds(4 * i, 4), :] = turned[4 * s : 4 * s + 4, :]
        return
    for p in range(4):
        near = lax.rem(pool - p + 4, 4)
        for i in range(2):
            state_out[near, i] = old[2 * p + i + 1, pl.ds(8, WIN), :]
    for i in range(2):
        own_out[:, i * ROWS : (i + 1) * ROWS] = old[2 * pool + i + 1, pl.ds(8 + HALO, CHUNK), :]


def relax(last, where, msgs, *fields):
    fresh = not fields
    state = shaped(4, 2, WIN, ROWS)
    out_shape = (state, shaped(CHUNK, COLS)) + ((state,) if fresh else ())
    if last:
        out_shape = (shaped(32, 8, ROWS),)
    scratch = [
        pltpu.VMEM((10, WIN + 16, ROWS), F32),
        pltpu.VMEM((10, WIN + 16, ROWS), F32),
        pltpu.VMEM((4,) + msgs[0].shape, F32),
        pltpu.VMEM((8, WIN, ROWS), F32),
        pltpu.VMEM((ROWS, ROWS), F32),
    ]
    return run(functools.partial(relax_kernel, fresh, last), "relax", out_shape, (where, *msgs, *fields), scratch)


def chunk_parts(s):
    core, z, y = s % 2, (s // 2) % 4, s // 8
    return core * 16 + y * 4 + z


def open_kernel(where_ref, potential_ref, reaction_ref, spikes_ref, out_ref, wide_ref, flags_ref):
    wide_ref[...] = jnp.zeros((16, PTS + 256), F32)
    flags_ref[...] = jnp.zeros((16, 128), F32)
    flags_ref[pl.ds(0, 2), 64 : 64 + STEPS] = spikes_ref[...].astype(F32)
    for row in range(4):
        for x in range(2):
            wide_ref[4 * x + row, pl.ds(128, PTS)] = potential_ref[row, x, :]
            wide_ref[8 + 4 * x + row, pl.ds(128, PTS)] = RELAX_WEIGHT / (6.0 + reaction_ref[row, x, :])
    lanes = lax.broadcasted_iota(jnp.int32, (16, 128), 1)
    for s in range(32):
        window = wide_ref[:, pl.ds(128 + CHUNK * chunk_parts(s) - HALO, 128)]
        out_ref[s] = jnp.where(lanes < 64, window, flags_ref[...])


def open_pack(where, potential, reaction, spikes):
    return run(
        open_kernel,
        "open_pack",
        shaped(32, 16, 128),
        (where, potential, reaction, spikes),
        [pltpu.VMEM((16, PTS + 256), F32), pltpu.VMEM((16, 128), F32)],
    )


def slab_kernel(where_ref, got_ref, out_ref, piece_ref, square_ref):
    for a in range(2):
        for x in range(2):
            for s in range(32):
                square_ref[pl.ds(4 * s, 4), :] = got_ref[s, pl.ds(8 * a + 4 * x, 4), :]
            turned = square_ref[...].T
            out_ref[a, x] = turned[:WIN, :]
            if a == 0:
                piece_ref[:, x * ROWS : (x + 1) * ROWS] = turned[HALO : HALO + CHUNK, :]


def slab_unpack(where, got):
    out_shape = (shaped(2, 2, WIN, ROWS), shaped(CHUNK, COLS))
    return run(slab_kernel, "slab", out_shape, (where, got), [pltpu.VMEM((ROWS, ROWS), F32)])


def close_kernel(where_ref, got_ref, out_ref, wide_ref):
    for s in range(32):
        part = got_ref[s]
        wide_ref[:, pl.ds(CHUNK * chunk_parts(s), CHUNK)] = part[:, HALO : HALO + CHUNK]
    for row in range(4):
        for x in range(2):
            out_ref[row, x, :] = wide_ref[4 * x + row, :]


def close(where, got):
    return run(close_kernel, "close", shaped(4, 2, PTS), (where, got), [pltpu.VMEM((8, PTS), F32)])


def fib_of(y, z, core):
    return (y * 4 + z) * 2 + core


def shift(x, axis, by=1):
    if axis == "pool":
        return lax.ppermute(x, "pool", [(i, (i + by) % 4) for i in range(4)])
    pairs = []
    for y in range(4):
        for z in range(4):
            for core in range(2):
                to = {
                    "y": ((y + by) % 4, z, core),
                    "z": (y, (z + by) % 4, core),
                    "core": (y, z, 1 - core),
                }[axis]
                pairs.append((fib_of(y, z, core), fib_of(*to)))
    return lax.ppermute(x, "fib", pairs)


def to_three(parts, axis, more=(), other=None):
    both = {}
    for k in (2, 1, 3):
        both[k] = shift(parts[k - 1], axis, k)
        if other:
            both[-k] = shift(more[k - 1], other, k)
    first = [both[k] for k in (1, 2, 3)]
    return (first, [both[-k] for k in (1, 2, 3)]) if other else first


def on_device(vm_state, recovery, spikes, owner, junction, column_index, cable_inverse, reaction, potential):
    fib = lax.axis_index("fib")
    pool = lax.axis_index("pool")
    core, z, y = fib % 2, (fib // 2) % 4, fib // 8
    where = jnp.stack([core, y, z, pool]).astype(jnp.int32)

    got = lax.all_to_all(open_pack(where, potential, reaction, spikes), "fib", 0, 0, tiled=True)
    table = jnp.concatenate([column_index, owner[:, None], junction[:, None]], axis=1).astype(F32)
    slab, piece = slab_unpack(where, got)
    base, following, fire, keep, send = first_call(where, vm_state, recovery, table, got)
    parts = {}

    def step(number, base, following, fire, keep, send, piece, state):
        mine_l, mine_r, loads_l, loads_r = first_pack(where, keep, shift(send, "core"), piece)
        gots_l, gots_r = to_three(loads_l, "y", loads_r, "z")
        last = number == STEPS - 1
        if number == 0:
            cable, mine_l = lax.optimization_barrier((cable_inverse, mine_l))
            high, low = cable_parts(cable)
            mine_l, high, low = lax.optimization_barrier((mine_l, high, low))
            parts.update(high=high, low=low)
        high, low = parts["high"], parts["low"]
        own, group_l, group_r, loads_l, loads_r = second_pack(where, mine_l, mine_r, piece, gots_l, gots_r)
        gots_l, gots_r = to_three(loads_l, "z", loads_r, "y")
        source, held, rim = join(where, own, group_l, group_r, gots_l, gots_r)
        rim, sent = lax.optimization_barrier((shift(rim, "core"), held))
        other = shift(sent, "core")
        note = message(where, source, held, rim, *([] if number else [slab]))
        msgs = to_three([note] * 3, "pool")
        other, note = lax.optimization_barrier((other, note))
        out = step_call(last, where, held, other, base, following, table, fire, high, low)
        *out, one, two, three = lax.optimization_barrier((*out, *msgs))
        relaxed = relax(last, where, [note, one, two, three], *([state, parts["gain"]] if number else []))
        if number == 0:
            parts.update(gain=relaxed[2])
        if last:
            return out[0], relaxed[0]
        return (*out, relaxed[1], relaxed[0])

    carry = (base, following, fire, keep, send, piece, None)
    for number in range(STEPS - 1):
        carry = step(number, *carry)
    membrane, closing = step(STEPS - 1, *carry)
    recovering = carry[1]
    extracell = close(where, lax.all_to_all(closing, "fib", 0, 0, tiled=True))
    return membrane, recovering, extracell


def solution(mesh):
    split_rows = P(("pool", "fib"), None)
    grid = P("fib", "pool", None)
    flat = P(("pool", "fib"))
    in_specs = (split_rows, split_rows, split_rows, flat, flat, split_rows, P(), grid, grid)
    return jax.shard_map(
        on_device, mesh=mesh, in_specs=in_specs, out_specs=(split_rows, split_rows, grid), check_vma=False
    )
```

```python
import functools

import jax
import jax.numpy as jnp
from jax import lax
from jax.experimental import pallas as pl
from jax.experimental.pallas import tpu as pltpu
from jax.sharding import PartitionSpec as P

STEPS = 4
SWEEPS = 4
TIME_STEP = 0.05
RECOVERY_RATE = 0.5
RECOVERY_SHIFT = 0.7
RECOVERY_SLOPE = 0.8
STIMULUS_GAIN = 4.0
JUNCTION_SPREAD = 8.0
SOURCE_GAIN = 0.25
RELAX_WEIGHT = 0.8

PTS = 1536
NBLK = 12
BLK = 128
FIB = 256
COLS = 256
ROWS = 128
CHUNK = 48
HALO = 4
WIN = CHUNK + 2 * HALO
YPART = 4 * CHUNK
CPART = 16 * CHUNK
YWIN = YPART + 2 * HALO
HALF = CPART + 2 * HALO
LOAD = YWIN + CHUNK
TILE = 256
TABLE = NBLK + 2
UNROLL = 12
PRODUCTS = 6
F32 = jnp.float32
BF16 = jnp.bfloat16
VMEM = pl.BlockSpec(memory_space=pltpu.VMEM)
SMEM = pl.BlockSpec(memory_space=pltpu.SMEM)
FAR = pl.BlockSpec(memory_space=pltpu.HBM)


def in_hbm(x):
    return pltpu.with_memory_space_constraint(x, pltpu.HBM)


def shaped(*dims, dtype=F32):
    return jax.ShapeDtypeStruct(dims, dtype)


def run(kernel, name, out_shape, operands, scratch=(), flops=1 << 20, moved=1 << 20, megabytes=4, outside=()):
    return pl.pallas_call(
        kernel,
        name=name,
        out_shape=out_shape,
        in_specs=[SMEM] + [FAR if i in outside else VMEM for i in range(1, len(operands))],
        out_specs=jax.tree.map(lambda _: VMEM, out_shape),
        scratch_shapes=scratch,
        cost_estimate=pl.CostEstimate(flops=flops, bytes_accessed=moved, transcendentals=0),
        compiler_params=pltpu.CompilerParams(vmem_limit_bytes=megabytes << 20),
    )(*operands)


def split(x):
    high = x.astype(BF16)
    return high, (x - high.astype(F32)).astype(BF16)


def dot(a, b, dims=((1,), (0,))):
    return lax.dot_general(a, b, (dims, ((), ())), preferred_element_type=F32)


def one_hot(column, width):
    lanes = lax.broadcasted_iota(jnp.int32, (column.shape[0], width), 1)
    return jnp.where(column == lanes, 1.0, 0.0).astype(BF16)


def advance(m, r, fire, place, start):
    width = m.shape[1]
    at = (lax.broadcasted_iota(jnp.int32, (1, width), 1) + start).astype(F32)
    offsets = (at - place) * (1.0 / JUNCTION_SPREAD)
    wave = jnp.exp(-offsets * offsets)
    current = m - m * m * m * (1.0 / 3.0) - r + (STIMULUS_GAIN * fire) * wave
    base = m + TIME_STEP * current
    following = r + TIME_STEP * RECOVERY_RATE * (m + RECOVERY_SHIFT - RECOVERY_SLOPE * r)
    return current, base, following


def deposit(current, hot):
    high, low = split(current.T)
    return dot(high, hot) + dot(low, hot)


def clear_ends(sums_ref):
    zero = jnp.zeros((8, COLS), F32)
    sums_ref[pl.ds(0, 8), :] = zero
    sums_ref[pl.ds(8 + PTS, 8), :] = zero


def put_halves(where_ref, sums_ref, keep_ref, send_ref):
    for core in range(2):

        @pl.when(where_ref[0] == core)
        def _():
            keep_ref[...] = sums_ref[pl.ds(8 - HALO + CPART * core, HALF), :]
            send_ref[...] = sums_ref[pl.ds(8 - HALO + CPART * (1 - core), HALF), :]


SUMS = pltpu.VMEM((PTS + 16, COLS), F32)


def rows_at(start, size):
    return pl.ds(start if isinstance(start, int) else pl.multiple_of(start, 8), size)


def column_of(table_ref, index):
    if isinstance(index, int):
        return table_ref[:, index : index + 1].astype(jnp.int32)
    lanes = lax.broadcasted_iota(jnp.int32, (FIB, TABLE), 1)
    return jnp.sum(jnp.where(lanes == index, table_ref[...], 0.0), axis=1, keepdims=True).astype(jnp.int32)


def looped(count, inner, body):
    if inner == count:
        for k in range(count):
            body(k)
        return

    def several(i, carry):
        for k in range(inner):
            body(i * inner + k)
        return carry

    lax.fori_loop(0, count // inner, several, 0)


def block_at(b):
    if isinstance(b, int):
        return pl.ds(b * BLK, BLK)
    return pl.ds(pl.multiple_of(b * BLK, BLK), BLK)


def slab_column(index):
    return (index & 1) * ROWS + (index >> 1)


def first_kernel(
    where_ref, m_hbm, r_hbm, table_ref, got_ref, base_ref, next_ref, fire_ref, keep_ref, send_ref,
    sums_ref, trains_ref, m_ref, r_ref, sems,
):
    copies = []
    for t in range(PTS // TILE):
        here = pl.ds(t * TILE, TILE)
        for i, (source, target) in enumerate(((m_hbm, m_ref), (r_hbm, r_ref))):
            copy = pltpu.make_async_copy(source.at[:, here], target.at[:, here], sems.at[2 * t + i])
            copy.start()
            copies.append(copy)
    clear_ends(sums_ref)
    for s in range(32):
        trains_ref[pl.ds(2 * s, 2), :] = got_ref[s, pl.ds(0, 2), :]
    units = one_hot(table_ref[:, NBLK : NBLK + 1].astype(jnp.int32), 64)
    fires = dot(units, trains_ref[...].astype(BF16))[:, 64 : 64 + STEPS]
    fire_ref[...] = fires
    fire = fires[:, 0:1]
    place = table_ref[:, NBLK + 1 : NBLK + 2]

    for b in range(NBLK):
        if b % 2 == 0:
            copies[b].wait()
            copies[b + 1].wait()
        here = block_at(b)
        current, base, following = advance(m_ref[:, here], r_ref[:, here], fire, place, b * BLK)
        base_ref[:, here] = base
        next_ref[:, here] = following
        hot = one_hot(slab_column(column_of(table_ref, b)), COLS)
        sums_ref[rows_at(8 + b * BLK, BLK), :] = deposit(current, hot)
    put_halves(where_ref, sums_ref, keep_ref, send_ref)


def first_call(where, m, r, table, got):
    state = shaped(FIB, PTS)
    return run(
        first_kernel,
        "first_deposit",
        (state, state, shaped(FIB, STEPS), shaped(HALF, COLS), shaped(HALF, COLS)),
        (where, in_hbm(m), in_hbm(r), table, got),
        [
            SUMS,
            pltpu.VMEM((64, 128), F32),
            pltpu.VMEM((FIB, PTS), F32),
            pltpu.VMEM((FIB, PTS), F32),
            pltpu.SemaphoreType.DMA((NBLK,)),
        ],
        outside=(1, 2),
        flops=6 << 30,
        moved=12 << 20,
        megabytes=12,
    )


def step_kernel(last, *refs):
    where_ref, own_ref, other_ref, base_ref, next_ref, table_ref, fire_ref, high_ref, low_ref = refs[:9]
    if last:
        m_out, field_ref, rhs_high, rhs_low, hot_ref = refs[9:]
    else:
        base_out, next_out, fire_out, keep_ref, send_ref, field_ref, rhs_high, rhs_low, hot_ref, sums_ref, m_out = refs[9:]
    core, y, z = where_ref[0], where_ref[1], where_ref[2]

    for yy in range(4):
        for zz in range(4):
            first = rows_at(place_of(y, z, yy, zz) * CHUNK, CHUNK)
            for half, ref in ((core, own_ref), (1 - core, other_ref)):
                field_ref[rows_at(half * CPART + (4 * yy + zz) * CHUNK, CHUNK), :] = ref[first, :]

    def sample(b):
        here = block_at(b)
        hot = one_hot(slab_column(column_of(table_ref, b)), COLS)
        if not last:
            hot_ref[b] = hot
        high, low = split(field_ref[here, :])
        sampled = dot(hot, high, ((1,), (1,))) + dot(hot, low, ((1,), (1,)))
        high, low = split(base_ref[:, here] + TIME_STEP * sampled)
        rhs_high[:, here] = high
        rhs_low[:, here] = low

    looped(NBLK, UNROLL, sample)

    def product(t):
        here = pl.ds(t * TILE if isinstance(t, int) else pl.multiple_of(t * TILE, TILE), TILE)
        m_out[:, here] = (
            dot(rhs_high[...], high_ref[:, here])
            + dot(rhs_low[...], high_ref[:, here])
            + dot(rhs_high[...], low_ref[:, here])
        )

    looped(PTS // TILE, PRODUCTS, product)
    if last:
        return
    clear_ends(sums_ref)
    place = table_ref[:, NBLK + 1 : NBLK + 2]
    fire = fire_ref[:, 1:2]
    fire_out[:, : STEPS - 1] = fire_ref[:, 1:]
    fire_out[:, STEPS - 1 :] = fire_ref[:, :1]

    def block(b):
        here = block_at(b)
        current, base, following = advance(m_out[:, here], next_ref[:, here], fire, place, b * BLK)
        base_out[:, here] = base
        next_out[:, here] = following
        sums_ref[rows_at(8 + b * BLK, BLK), :] = deposit(current, hot_ref[b])

    looped(NBLK, UNROLL, block)
    put_halves(where_ref, sums_ref, keep_ref, send_ref)


def step_call(last, *operands):
    state = shaped(FIB, PTS)
    field = (PTS, COLS)
    scratch = [pltpu.VMEM(field, F32), pltpu.VMEM((FIB, PTS), BF16), pltpu.VMEM((FIB, PTS), BF16)]
    scratch += [pltpu.VMEM((NBLK, FIB, COLS), BF16)]
    if last:
        out_shape = (state,)
    else:
        out_shape = (state, state, shaped(FIB, STEPS), shaped(HALF, COLS), shaped(HALF, COLS))
        scratch += [SUMS, pltpu.VMEM((FIB, PTS), F32)]
    return run(
        functools.partial(step_kernel, last),
        "fibre_step",
        out_shape,
        operands,
        scratch,
        flops=2 * 3 * FIB * PTS * PTS,
        moved=20 << 20,
        megabytes=12,
    )


def parts_kernel(whole_ref, high_ref, low_ref):
    high, low = split(whole_ref[...])
    high_ref[...] = high
    low_ref[...] = low


def cable_parts(cable):
    rows = pl.BlockSpec((TILE, PTS), lambda i: (i, 0))
    return pl.pallas_call(
        parts_kernel,
        name="cable_parts",
        grid=(PTS // TILE,),
        out_shape=(shaped(PTS, PTS, dtype=BF16),) * 2,
        in_specs=[rows],
        out_specs=(rows, rows),
        cost_estimate=pl.CostEstimate(flops=1 << 23, bytes_accessed=18 << 20, transcendentals=0),
        compiler_params=pltpu.CompilerParams(vmem_limit_bytes=10 << 20),
    )(in_hbm(cable))


def place_of(y, z, yy, zz):
    return lax.rem(z - zz + 4, 4) * 4 + lax.rem(y - yy + 4, 4)


LEFT = slice(0, ROWS)
RIGHT = slice(ROWS, COLS)
FOUR = 4 * WIN


def first_pack_kernel(where_ref, keep_ref, got_ref, piece_ref, mine_l, mine_r, *outs):
    y, z = where_ref[1], where_ref[2]
    for k, out in enumerate((mine_l,) + outs[:3]):
        here = rows_at(lax.rem(y + k, 4) * YPART, YWIN)
        out[pl.ds(0, YWIN), :] = keep_ref[here, LEFT] + got_ref[here, LEFT]
        if k:
            out[pl.ds(YWIN, CHUNK), :] = piece_ref[:, LEFT]
    for k, out in enumerate((mine_r,) + outs[3:]):
        for yy in range(4):
            here = rows_at(yy * YPART + lax.rem(z + k, 4) * CHUNK, WIN)
            out[pl.ds(yy * WIN, WIN), :] = keep_ref[here, RIGHT] + got_ref[here, RIGHT]
        if k:
            out[pl.ds(FOUR, CHUNK), :] = piece_ref[:, RIGHT]


def first_pack(where, keep, got, piece):
    out = (shaped(YWIN, ROWS), shaped(FOUR, ROWS)) + (shaped(YWIN + CHUNK, ROWS),) * 3 + (shaped(FOUR + CHUNK, ROWS),) * 3
    mine_l, mine_r, *loads = run(first_pack_kernel, "first_pack", out, (where, keep, got, piece))
    return mine_l, mine_r, loads[:3], loads[3:]


def second_pack_kernel(where_ref, mine_l, mine_r, piece_ref, l2, r2, l1, r1, l3, r3, own_ref, group_l, group_r, *outs):
    y, z = where_ref[1], where_ref[2]
    for side, group, size, gots in ((LEFT, group_l, YWIN, (l1, l2, l3)), (RIGHT, group_r, FOUR, (r1, r2, r3))):
        parts = [piece_ref[:, side]] + [got[pl.ds(size, CHUNK), :] for got in gots]
        for i, part in enumerate(parts):
            group[pl.ds(i * CHUNK, CHUNK), :] = part
    for k in range(4):
        here = rows_at(lax.rem(z + k, 4) * CHUNK, WIN)
        left = mine_l[here, :] + l1[here, :] + l3[here, :] + l2[here, :]
        here = rows_at(lax.rem(y + k, 4) * WIN, WIN)
        right = mine_r[here, :] + r1[here, :] + r3[here, :] + r2[here, :]
        if k == 0:
            own_ref[:, LEFT] = left
            own_ref[:, RIGHT] = right
        else:
            outs[k - 1][pl.ds(0, WIN), :] = left
            outs[k - 1][pl.ds(WIN, YPART), :] = group_l[...]
            outs[k + 2][pl.ds(0, WIN), :] = right
            outs[k + 2][pl.ds(WIN, YPART), :] = group_r[...]


def second_pack(where, mine_l, mine_r, piece, gots_l, gots_r):
    group = shaped(YPART, ROWS)
    out = (shaped(WIN, COLS), group, group) + (shaped(WIN + YPART, ROWS),) * 6
    own, group_l, group_r, *loads = run(
        second_pack_kernel, "second_pack", out, (where, mine_l, mine_r, piece, gots_l[1], gots_r[1], gots_l[0], gots_r[0], gots_l[2], gots_r[2])
    )
    return own, group_l, group_r, loads[:3], loads[3:]


def join_kernel(where_ref, own_ref, group_l, group_r, l2, r2, l1, r1, l3, r3, source_ref, held_ref, rim_ref):
    core, y, z = where_ref[0], where_ref[1], where_ref[2]
    here = pl.ds(0, WIN)
    source_ref[:, LEFT] = own_ref[:, LEFT] + l1[here, :] + l3[here, :] + l2[here, :]
    source_ref[:, RIGHT] = own_ref[:, RIGHT] + r1[here, :] + r3[here, :] + r2[here, :]
    held_ref[pl.ds(0, YPART), LEFT] = group_l[...]
    for k, got in enumerate((l1, l2, l3)):
        held_ref[pl.ds((k + 1) * YPART, YPART), LEFT] = got[pl.ds(WIN, YPART), :]
    for i in range(4):
        held_ref[pl.ds(i * YPART, CHUNK), RIGHT] = group_r[pl.ds(i * CHUNK, CHUNK), :]
        for k, got in enumerate((r1, r2, r3)):
            held_ref[pl.ds(i * YPART + (k + 1) * CHUNK, CHUNK), RIGHT] = got[pl.ds(WIN + i * CHUNK, CHUNK), :]
    top = rows_at(place_of(y, z, 3, 3) * CHUNK + CHUNK - 8, 8)
    bottom = rows_at(place_of(y, z, 0, 0) * CHUNK, 8)
    rim_ref[...] = jnp.where(core == 0, held_ref[top, :], held_ref[bottom, :])


def join(where, own, group_l, group_r, gots_l, gots_r):
    out_shape = (shaped(WIN, COLS), shaped(CPART, COLS), shaped(8, COLS))
    return run(join_kernel, "join", out_shape, (where, own, group_l, group_r, gots_l[1], gots_r[1], gots_l[0], gots_r[0], gots_l[2], gots_r[2]))


def message_kernel(where_ref, source_ref, held_ref, rim_ref, *refs):
    out_ref = refs[-1]
    if len(refs) == 2:
        for a in range(2):
            for x in range(2):
                out_ref[pl.ds(WIN + 8 + a * WIN, WIN), x * ROWS : (x + 1) * ROWS] = refs[0][a, x]
    core, y, z = where_ref[0], where_ref[1], where_ref[2]
    chunk = core * 16 + y * 4 + z
    out_ref[pl.ds(0, WIN), :] = source_ref[...]

    def rows(which, start):
        kept = jnp.clip(which, 0, 31)
        index = place_of(y, z, (kept >> 2) & 3, kept & 3)
        here = pl.ds(pl.multiple_of(index * CHUNK + start, 8), 8)
        found = jnp.where((kept >> 4) == core, held_ref[here, :], rim_ref[...])
        return pltpu.roll(jnp.where(which == kept, found, 0.0), 4, 0)

    below = rows(chunk - 1, CHUNK - 8)
    above = rows(chunk + 1, 0)
    level = lax.broadcasted_iota(jnp.int32, (8, COLS), 0)
    out_ref[pl.ds(WIN, 8), :] = jnp.where(level < HALO, below, above)


def message(where, source, held, rim, *slab):
    size = (WIN + 8) + 2 * WIN * len(slab)
    return run(message_kernel, "message", shaped(size, COLS), (where, source, held, rim, *slab))


def relax_kernel(fresh, last, *refs):
    refs = list(refs)
    where_ref = refs.pop(0)
    pool = where_ref[3]
    message_refs = [refs.pop(0) for _ in range(4)]
    if not fresh:
        state_ref, gain_ref = refs.pop(0), refs.pop(0)
    if not last:
        state_out = refs.pop(0)
    own_out = refs.pop(0)
    if fresh:
        gain_ref = refs.pop(0)
    field_a, field_b, msgs, source = refs[:4]
    for k, ref in enumerate(message_refs):
        msgs[k] = ref[...]
    lanes = lax.broadcasted_iota(jnp.int32, (WIN, ROWS), 1)
    zeros = jnp.zeros((WIN + 16, ROWS), F32)
    edge = jnp.zeros((8, ROWS), F32)
    for field in (field_a, field_b):
        field[0] = zeros
        field[9] = zeros
        for x in range(8):
            field[x + 1, pl.ds(0, 8), :] = edge
            field[x + 1, pl.ds(WIN + 8, 8), :] = edge
    for p in range(4):
        near = lax.rem(pool - p + 4, 4)
        for i in range(2):
            x = 2 * p + i
            lane = pl.ds(i * ROWS, ROWS)
            if fresh:
                field_a[x + 1, pl.ds(8, WIN), :] = msgs[near, pl.ds(WIN + 8, WIN), lane]
                gain_ref[near, i] = msgs[near, pl.ds(2 * WIN + 8, WIN), lane]
            else:
                field_a[x + 1, pl.ds(8, WIN), :] = state_ref[near, i]
            field_a[x + 1, pl.ds(8, HALO), :] = msgs[near, pl.ds(WIN, HALO), lane]
            field_a[x + 1, pl.ds(8 + HALO + CHUNK, HALO), :] = msgs[near, pl.ds(WIN + HALO, HALO), lane]
            source[x] = SOURCE_GAIN * msgs[near, pl.ds(0, WIN), lane]
    def sweep(old, new):
        for p in range(4):
            near = lax.rem(pool - p + 4, 4)
            for i in range(2):
                x = 2 * p + i
                centre = old[x + 1, pl.ds(8, WIN), :]
                total = source[x] + old[x, pl.ds(8, WIN), :] + old[x + 2, pl.ds(8, WIN), :]
                total = total + old[x + 1, pl.ds(7, WIN), :] + old[x + 1, pl.ds(9, WIN), :]
                total = total + jnp.where(lanes == 0, 0.0, pltpu.roll(centre, 1, 1))
                total = total + jnp.where(lanes == ROWS - 1, 0.0, pltpu.roll(centre, ROWS - 1, 1))
                new[x + 1, pl.ds(8, WIN), :] = (1.0 - RELAX_WEIGHT) * centre + gain_ref[near, i] * total

    def both(_, carry):
        sweep(field_a, field_b)
        sweep(field_b, field_a)
        return carry

    lax.fori_loop(0, SWEEPS // 2, both, 0)
    old = field_a
    if last:
        for i in range(2):
            flat = old[2 * pool + i + 1, pl.ds(8, WIN), :]
            refs[4][...] = jnp.zeros((ROWS, ROWS), F32)
            refs[4][pl.ds(0, WIN), :] = flat
            turned = refs[4][...].T
            for s in range(32):
                own_out[s, pl.ds(4 * i, 4), :] = turned[4 * s : 4 * s + 4, :]
        return
    for p in range(4):
        near = lax.rem(pool - p + 4, 4)
        for i in range(2):
            state_out[near, i] = old[2 * p + i + 1, pl.ds(8, WIN), :]
    for i in range(2):
        own_out[:, i * ROWS : (i + 1) * ROWS] = old[2 * pool + i + 1, pl.ds(8 + HALO, CHUNK), :]


def relax(last, where, msgs, *fields):
    fresh = not fields
    state = shaped(4, 2, WIN, ROWS)
    out_shape = (state, shaped(CHUNK, COLS)) + ((state,) if fresh else ())
    if last:
        out_shape = (shaped(32, 8, ROWS),)
    scratch = [
        pltpu.VMEM((10, WIN + 16, ROWS), F32),
        pltpu.VMEM((10, WIN + 16, ROWS), F32),
        pltpu.VMEM((4,) + msgs[0].shape, F32),
        pltpu.VMEM((8, WIN, ROWS), F32),
        pltpu.VMEM((ROWS, ROWS), F32),
    ]
    return run(functools.partial(relax_kernel, fresh, last), "relax", out_shape, (where, *msgs, *fields), scratch)


def chunk_parts(s):
    core, z, y = s % 2, (s // 2) % 4, s // 8
    return core * 16 + y * 4 + z


def open_kernel(where_ref, potential_ref, reaction_ref, spikes_ref, out_ref, wide_ref, flags_ref):
    wide_ref[...] = jnp.zeros((16, PTS + 256), F32)
    flags_ref[...] = jnp.zeros((16, 128), F32)
    flags_ref[pl.ds(0, 2), 64 : 64 + STEPS] = spikes_ref[...].astype(F32)
    for row in range(4):
        for x in range(2):
            wide_ref[4 * x + row, pl.ds(128, PTS)] = potential_ref[row, x, :]
            wide_ref[8 + 4 * x + row, pl.ds(128, PTS)] = RELAX_WEIGHT / (6.0 + reaction_ref[row, x, :])
    lanes = lax.broadcasted_iota(jnp.int32, (16, 128), 1)
    for s in range(32):
        window = wide_ref[:, pl.ds(128 + CHUNK * chunk_parts(s) - HALO, 128)]
        out_ref[s] = jnp.where(lanes < 64, window, flags_ref[...])


def open_pack(where, potential, reaction, spikes):
    return run(
        open_kernel,
        "open_pack",
        shaped(32, 16, 128),
        (where, potential, reaction, spikes),
        [pltpu.VMEM((16, PTS + 256), F32), pltpu.VMEM((16, 128), F32)],
    )


def slab_kernel(where_ref, got_ref, out_ref, piece_ref, square_ref):
    for a in range(2):
        for x in range(2):
            for s in range(32):
                square_ref[pl.ds(4 * s, 4), :] = got_ref[s, pl.ds(8 * a + 4 * x, 4), :]
            turned = square_ref[...].T
            out_ref[a, x] = turned[:WIN, :]
            if a == 0:
                piece_ref[:, x * ROWS : (x + 1) * ROWS] = turned[HALO : HALO + CHUNK, :]


def slab_unpack(where, got):
    out_shape = (shaped(2, 2, WIN, ROWS), shaped(CHUNK, COLS))
    return run(slab_kernel, "slab", out_shape, (where, got), [pltpu.VMEM((ROWS, ROWS), F32)])


def close_kernel(where_ref, got_ref, out_ref, wide_ref):
    for s in range(32):
        part = got_ref[s]
        wide_ref[:, pl.ds(CHUNK * chunk_parts(s), CHUNK)] = part[:, HALO : HALO + CHUNK]
    for row in range(4):
        for x in range(2):
            out_ref[row, x, :] = wide_ref[4 * x + row, :]


def close(where, got):
    return run(close_kernel, "close", shaped(4, 2, PTS), (where, got), [pltpu.VMEM((8, PTS), F32)])


def fib_of(y, z, core):
    return (y * 4 + z) * 2 + core


def shift(x, axis, by=1):
    if axis == "pool":
        return lax.ppermute(x, "pool", [(i, (i + by) % 4) for i in range(4)])
    pairs = []
    for y in range(4):
        for z in range(4):
            for core in range(2):
                to = {
                    "y": ((y + by) % 4, z, core),
                    "z": (y, (z + by) % 4, core),
                    "core": (y, z, 1 - core),
                }[axis]
                pairs.append((fib_of(y, z, core), fib_of(*to)))
    return lax.ppermute(x, "fib", pairs)


def to_three(parts, axis, more=(), other=None):
    both = {}
    for k in (2, 1, 3):
        both[k] = shift(parts[k - 1], axis, k)
        if other:
            both[-k] = shift(more[k - 1], other, k)
    first = [both[k] for k in (1, 2, 3)]
    return (first, [both[-k] for k in (1, 2, 3)]) if other else first


def on_device(vm_state, recovery, spikes, owner, junction, column_index, cable_inverse, reaction, potential):
    fib = lax.axis_index("fib")
    pool = lax.axis_index("pool")
    core, z, y = fib % 2, (fib // 2) % 4, fib // 8
    where = jnp.stack([core, y, z, pool]).astype(jnp.int32)

    got = lax.all_to_all(open_pack(where, potential, reaction, spikes), "fib", 0, 0, tiled=True)
    table = jnp.concatenate([column_index, owner[:, None], junction[:, None]], axis=1).astype(F32)
    slab, piece = slab_unpack(where, got)
    base, following, fire, keep, send = first_call(where, vm_state, recovery, table, got)
    parts = {}

    def step(number, base, following, fire, keep, send, piece, state):
        mine_l, mine_r, loads_l, loads_r = first_pack(where, keep, shift(send, "core"), piece)
        gots_l, gots_r = to_three(loads_l, "y", loads_r, "z")
        last = number == STEPS - 1
        if number == 0:
            cable, mine_l = lax.optimization_barrier((cable_inverse, mine_l))
            high, low = cable_parts(cable)
            mine_l, high, low = lax.optimization_barrier((mine_l, high, low))
            parts.update(high=high, low=low)
        high, low = parts["high"], parts["low"]
        own, group_l, group_r, loads_l, loads_r = second_pack(where, mine_l, mine_r, piece, gots_l, gots_r)
        gots_l, gots_r = to_three(loads_l, "z", loads_r, "y")
        source, held, rim = join(where, own, group_l, group_r, gots_l, gots_r)
        rim, sent = lax.optimization_barrier((shift(rim, "core"), held))
        other = shift(sent, "core")
        note = message(where, source, held, rim, *([] if number else [slab]))
        msgs = to_three([note] * 3, "pool")
        other, note = lax.optimization_barrier((other, note))
        out = step_call(last, where, held, other, base, following, table, fire, high, low)
        *out, one, two, three = lax.optimization_barrier((*out, *msgs))
        relaxed = relax(last, where, [note, one, two, three], *([state, parts["gain"]] if number else []))
        if number == 0:
            parts.update(gain=relaxed[2])
        if last:
            return out[0], relaxed[0]
        return (*out, relaxed[1], relaxed[0])

    carry = (base, following, fire, keep, send, piece, None)
    for number in range(STEPS - 1):
        carry = step(number, *carry)
    membrane, closing = step(STEPS - 1, *carry)
    recovering = carry[1]
    extracell = close(where, lax.all_to_all(closing, "fib", 0, 0, tiled=True))
    return membrane, recovering, extracell


def solution(mesh):
    split_rows = P(("pool", "fib"), None)
    grid = P("fib", "pool", None)
    flat = P(("pool", "fib"))
    in_specs = (split_rows, split_rows, split_rows, flat, flat, split_rows, P(), grid, grid)
    return jax.shard_map(
        on_device, mesh=mesh, in_specs=in_specs, out_specs=(split_rows, split_rows, grid), check_vma=False
    )
```

```python
import functools

import jax
import jax.numpy as jnp
from jax import lax
from jax.experimental import pallas as pl
from jax.experimental.pallas import tpu as pltpu
from jax.sharding import PartitionSpec as P

STEPS = 4
SWEEPS = 4
TIME_STEP = 0.05
RECOVERY_RATE = 0.5
RECOVERY_SHIFT = 0.7
RECOVERY_SLOPE = 0.8
STIMULUS_GAIN = 4.0
JUNCTION_SPREAD = 8.0
SOURCE_GAIN = 0.25
RELAX_WEIGHT = 0.8

PTS = 1536
NBLK = 12
BLK = 128
FIB = 256
COLS = 256
ROWS = 128
CHUNK = 48
HALO = 4
WIN = CHUNK + 2 * HALO
YPART = 4 * CHUNK
CPART = 16 * CHUNK
YWIN = YPART + 2 * HALO
HALF = CPART + 2 * HALO
LOAD = YWIN + CHUNK
TILE = 256
TABLE = NBLK + 2
UNROLL = 12
PRODUCTS = 6
F32 = jnp.float32
BF16 = jnp.bfloat16
VMEM = pl.BlockSpec(memory_space=pltpu.VMEM)
SMEM = pl.BlockSpec(memory_space=pltpu.SMEM)
FAR = pl.BlockSpec(memory_space=pltpu.HBM)


def in_hbm(x):
    return pltpu.with_memory_space_constraint(x, pltpu.HBM)


def shaped(*dims, dtype=F32):
    return jax.ShapeDtypeStruct(dims, dtype)


def run(kernel, name, out_shape, operands, scratch=(), flops=1 << 20, moved=1 << 20, megabytes=4, outside=()):
    return pl.pallas_call(
        kernel,
        name=name,
        out_shape=out_shape,
        in_specs=[SMEM] + [FAR if i in outside else VMEM for i in range(1, len(operands))],
        out_specs=jax.tree.map(lambda _: VMEM, out_shape),
        scratch_shapes=scratch,
        cost_estimate=pl.CostEstimate(flops=flops, bytes_accessed=moved, transcendentals=0),
        compiler_params=pltpu.CompilerParams(vmem_limit_bytes=megabytes << 20),
    )(*operands)


def split(x):
    high = x.astype(BF16)
    return high, (x - high.astype(F32)).astype(BF16)


def dot(a, b, dims=((1,), (0,))):
    return lax.dot_general(a, b, (dims, ((), ())), preferred_element_type=F32)


def one_hot(column, width):
    lanes = lax.broadcasted_iota(jnp.int32, (column.shape[0], width), 1)
    return jnp.where(column == lanes, 1.0, 0.0).astype(BF16)


def advance(m, r, fire, place, start):
    width = m.shape[1]
    at = (lax.broadcasted_iota(jnp.int32, (1, width), 1) + start).astype(F32)
    offsets = (at - place) * (1.0 / JUNCTION_SPREAD)
    wave = jnp.exp(-offsets * offsets)
    current = m - m * m * m * (1.0 / 3.0) - r + (STIMULUS_GAIN * fire) * wave
    base = m + TIME_STEP * current
    following = r + TIME_STEP * RECOVERY_RATE * (m + RECOVERY_SHIFT - RECOVERY_SLOPE * r)
    return current, base, following


def deposit(current, hot):
    high, low = split(current.T)
    return dot(high, hot) + dot(low, hot)


def clear_ends(sums_ref):
    zero = jnp.zeros((8, COLS), F32)
    sums_ref[pl.ds(0, 8), :] = zero
    sums_ref[pl.ds(8 + PTS, 8), :] = zero


def put_halves(where_ref, sums_ref, keep_ref, send_ref):
    for core in range(2):

        @pl.when(where_ref[0] == core)
        def _():
            keep_ref[...] = sums_ref[pl.ds(8 - HALO + CPART * core, HALF), :]
            send_ref[...] = sums_ref[pl.ds(8 - HALO + CPART * (1 - core), HALF), :]


SUMS = pltpu.VMEM((PTS + 16, COLS), F32)


def rows_at(start, size):
    return pl.ds(start if isinstance(start, int) else pl.multiple_of(start, 8), size)


def column_of(table_ref, index):
    if isinstance(index, int):
        return table_ref[:, index : index + 1].astype(jnp.int32)
    lanes = lax.broadcasted_iota(jnp.int32, (FIB, TABLE), 1)
    return jnp.sum(jnp.where(lanes == index, table_ref[...], 0.0), axis=1, keepdims=True).astype(jnp.int32)


def looped(count, inner, body):
    if inner == count:
        for k in range(count):
            body(k)
        return

    def several(i, carry):
        for k in range(inner):
            body(i * inner + k)
        return carry

    lax.fori_loop(0, count // inner, several, 0)


def block_at(b):
    if isinstance(b, int):
        return pl.ds(b * BLK, BLK)
    return pl.ds(pl.multiple_of(b * BLK, BLK), BLK)


def slab_column(index):
    return (index & 1) * ROWS + (index >> 1)


def first_kernel(
    where_ref, m_hbm, r_hbm, table_ref, got_ref, base_ref, next_ref, fire_ref, keep_ref, send_ref,
    sums_ref, trains_ref, m_ref, r_ref, sems,
):
    copies = []
    for t in range(PTS // TILE):
        here = pl.ds(t * TILE, TILE)
        for i, (source, target) in enumerate(((m_hbm, m_ref), (r_hbm, r_ref))):
            copy = pltpu.make_async_copy(source.at[:, here], target.at[:, here], sems.at[2 * t + i])
            copy.start()
            copies.append(copy)
    clear_ends(sums_ref)
    for s in range(32):
        trains_ref[pl.ds(2 * s, 2), :] = got_ref[s, pl.ds(0, 2), :]
    units = one_hot(table_ref[:, NBLK : NBLK + 1].astype(jnp.int32), 64)
    fires = dot(units, trains_ref[...].astype(BF16))[:, 64 : 64 + STEPS]
    fire_ref[...] = fires
    fire = fires[:, 0:1]
    place = table_ref[:, NBLK + 1 : NBLK + 2]

    for b in range(NBLK):
        if b % 2 == 0:
            copies[b].wait()
            copies[b + 1].wait()
        here = block_at(b)
        current, base, following = advance(m_ref[:, here], r_ref[:, here], fire, place, b * BLK)
        base_ref[:, here] = base
        next_ref[:, here] = following
        hot = one_hot(slab_column(column_of(table_ref, b)), COLS)
        sums_ref[rows_at(8 + b * BLK, BLK), :] = deposit(current, hot)
    put_halves(where_ref, sums_ref, keep_ref, send_ref)


def first_call(where, m, r, table, got):
    state = shaped(FIB, PTS)
    return run(
        first_kernel,
        "first_deposit",
        (state, state, shaped(FIB, STEPS), shaped(HALF, COLS), shaped(HALF, COLS)),
        (where, in_hbm(m), in_hbm(r), table, got),
        [
            SUMS,
            pltpu.VMEM((64, 128), F32),
            pltpu.VMEM((FIB, PTS), F32),
            pltpu.VMEM((FIB, PTS), F32),
            pltpu.SemaphoreType.DMA((NBLK,)),
        ],
        outside=(1, 2),
        flops=6 << 30,
        moved=12 << 20,
        megabytes=12,
    )


def step_kernel(last, *refs):
    where_ref, own_ref, other_ref, base_ref, next_ref, table_ref, fire_ref, high_ref, low_ref = refs[:9]
    if last:
        m_out, field_ref, rhs_high, rhs_low, hot_ref = refs[9:]
    else:
        base_out, next_out, fire_out, keep_ref, send_ref, field_ref, rhs_high, rhs_low, hot_ref, sums_ref, m_out = refs[9:]
    core, y, z = where_ref[0], where_ref[1], where_ref[2]

    for yy in range(4):
        for zz in range(4):
            first = rows_at(place_of(y, z, yy, zz) * CHUNK, CHUNK)
            for half, ref in ((core, own_ref), (1 - core, other_ref)):
                field_ref[rows_at(half * CPART + (4 * yy + zz) * CHUNK, CHUNK), :] = ref[first, :]

    def sample(b):
        here = block_at(b)
        hot = one_hot(slab_column(column_of(table_ref, b)), COLS)
        if not last:
            hot_ref[b] = hot
        high, low = split(field_ref[here, :])
        sampled = dot(hot, high, ((1,), (1,))) + dot(hot, low, ((1,), (1,)))
        high, low = split(base_ref[:, here] + TIME_STEP * sampled)
        rhs_high[:, here] = high
        rhs_low[:, here] = low

    looped(NBLK, UNROLL, sample)

    def product(t):
        here = pl.ds(t * TILE if isinstance(t, int) else pl.multiple_of(t * TILE, TILE), TILE)
        m_out[:, here] = (
            dot(rhs_high[...], high_ref[:, here])
            + dot(rhs_low[...], high_ref[:, here])
            + dot(rhs_high[...], low_ref[:, here])
        )

    looped(PTS // TILE, PRODUCTS, product)
    if last:
        return
    clear_ends(sums_ref)
    place = table_ref[:, NBLK + 1 : NBLK + 2]
    fire = fire_ref[:, 1:2]
    fire_out[:, : STEPS - 1] = fire_ref[:, 1:]
    fire_out[:, STEPS - 1 :] = fire_ref[:, :1]

    def block(b):
        here = block_at(b)
        current, base, following = advance(m_out[:, here], next_ref[:, here], fire, place, b * BLK)
        base_out[:, here] = base
        next_out[:, here] = following
        sums_ref[rows_at(8 + b * BLK, BLK), :] = deposit(current, hot_ref[b])

    looped(NBLK, UNROLL, block)
    put_halves(where_ref, sums_ref, keep_ref, send_ref)


def step_call(last, *operands):
    state = shaped(FIB, PTS)
    field = (PTS, COLS)
    scratch = [pltpu.VMEM(field, F32), pltpu.VMEM((FIB, PTS), BF16), pltpu.VMEM((FIB, PTS), BF16)]
    scratch += [pltpu.VMEM((NBLK, FIB, COLS), BF16)]
    if last:
        out_shape = (state,)
    else:
        out_shape = (state, state, shaped(FIB, STEPS), shaped(HALF, COLS), shaped(HALF, COLS))
        scratch += [SUMS, pltpu.VMEM((FIB, PTS), F32)]
    return run(
        functools.partial(step_kernel, last),
        "fibre_step",
        out_shape,
        operands,
        scratch,
        flops=2 * 3 * FIB * PTS * PTS,
        moved=20 << 20,
        megabytes=12,
    )


def parts_kernel(whole_ref, high_ref, low_ref):
    high, low = split(whole_ref[...])
    high_ref[...] = high
    low_ref[...] = low


def cable_parts(cable):
    rows = pl.BlockSpec((TILE, PTS), lambda i: (i, 0))
    return pl.pallas_call(
        parts_kernel,
        name="cable_parts",
        grid=(PTS // TILE,),
        out_shape=(shaped(PTS, PTS, dtype=BF16),) * 2,
        in_specs=[rows],
        out_specs=(rows, rows),
        cost_estimate=pl.CostEstimate(flops=1 << 23, bytes_accessed=18 << 20, transcendentals=0),
        compiler_params=pltpu.CompilerParams(vmem_limit_bytes=10 << 20),
    )(in_hbm(cable))


def place_of(y, z, yy, zz):
    return lax.rem(z - zz + 4, 4) * 4 + lax.rem(y - yy + 4, 4)


LEFT = slice(0, ROWS)
RIGHT = slice(ROWS, COLS)
FOUR = 4 * WIN


def first_pack_kernel(where_ref, keep_ref, got_ref, piece_ref, mine_l, mine_r, *outs):
    y, z = where_ref[1], where_ref[2]
    for k, out in enumerate((mine_l,) + outs[:3]):
        here = rows_at(lax.rem(y + k, 4) * YPART, YWIN)
        out[pl.ds(0, YWIN), :] = keep_ref[here, LEFT] + got_ref[here, LEFT]
        if k:
            out[pl.ds(YWIN, CHUNK), :] = piece_ref[:, LEFT]
    for k, out in enumerate((mine_r,) + outs[3:]):
        for yy in range(4):
            here = rows_at(yy * YPART + lax.rem(z + k, 4) * CHUNK, WIN)
            out[pl.ds(yy * WIN, WIN), :] = keep_ref[here, RIGHT] + got_ref[here, RIGHT]
        if k:
            out[pl.ds(FOUR, CHUNK), :] = piece_ref[:, RIGHT]


def first_pack(where, keep, got, piece):
    out = (shaped(YWIN, ROWS), shaped(FOUR, ROWS)) + (shaped(YWIN + CHUNK, ROWS),) * 3 + (shaped(FOUR + CHUNK, ROWS),) * 3
    mine_l, mine_r, *loads = run(first_pack_kernel, "first_pack", out, (where, keep, got, piece))
    return mine_l, mine_r, loads[:3], loads[3:]


def second_pack_kernel(where_ref, mine_l, mine_r, piece_ref, r2, l2, r1, l1, r3, l3, own_ref, group_l, group_r, *outs):
    y, z = where_ref[1], where_ref[2]
    for side, group, size, gots in ((LEFT, group_l, YWIN, (l1, l2, l3)), (RIGHT, group_r, FOUR, (r1, r2, r3))):
        parts = [piece_ref[:, side]] + [got[pl.ds(size, CHUNK), :] for got in gots]
        for i, part in enumerate(parts):
            group[pl.ds(i * CHUNK, CHUNK), :] = part
    for k in range(4):
        here = rows_at(lax.rem(z + k, 4) * CHUNK, WIN)
        left = mine_l[here, :] + l1[here, :] + l3[here, :] + l2[here, :]
        here = rows_at(lax.rem(y + k, 4) * WIN, WIN)
        right = mine_r[here, :] + r1[here, :] + r3[here, :] + r2[here, :]
        if k == 0:
            own_ref[:, LEFT] = left
            own_ref[:, RIGHT] = right
        else:
            outs[k - 1][pl.ds(0, WIN), :] = left
            outs[k - 1][pl.ds(WIN, YPART), :] = group_l[...]
            outs[k + 2][pl.ds(0, WIN), :] = right
            outs[k + 2][pl.ds(WIN, YPART), :] = group_r[...]


def second_pack(where, mine_l, mine_r, piece, gots_l, gots_r):
    group = shaped(YPART, ROWS)
    out = (shaped(WIN, COLS), group, group) + (shaped(WIN + YPART, ROWS),) * 6
    own, group_l, group_r, *loads = run(
        second_pack_kernel, "second_pack", out, (where, mine_l, mine_r, piece, gots_r[1], gots_l[1], gots_r[0], gots_l[0], gots_r[2], gots_l[2])
    )
    return own, group_l, group_r, loads[:3], loads[3:]


def join_kernel(where_ref, own_ref, group_l, group_r, r2, l2, r1, l1, r3, l3, source_ref, held_ref, rim_ref):
    core, y, z = where_ref[0], where_ref[1], where_ref[2]
    here = pl.ds(0, WIN)
    source_ref[:, LEFT] = own_ref[:, LEFT] + l1[here, :] + l3[here, :] + l2[here, :]
    source_ref[:, RIGHT] = own_ref[:, RIGHT] + r1[here, :] + r3[here, :] + r2[here, :]
    held_ref[pl.ds(0, YPART), LEFT] = group_l[...]
    for k, got in enumerate((l1, l2, l3)):
        held_ref[pl.ds((k + 1) * YPART, YPART), LEFT] = got[pl.ds(WIN, YPART), :]
    for i in range(4):
        held_ref[pl.ds(i * YPART, CHUNK), RIGHT] = group_r[pl.ds(i * CHUNK, CHUNK), :]
        for k, got in enumerate((r1, r2, r3)):
            held_ref[pl.ds(i * YPART + (k + 1) * CHUNK, CHUNK), RIGHT] = got[pl.ds(WIN + i * CHUNK, CHUNK), :]
    top = rows_at(place_of(y, z, 3, 3) * CHUNK + CHUNK - 8, 8)
    bottom = rows_at(place_of(y, z, 0, 0) * CHUNK, 8)
    rim_ref[...] = jnp.where(core == 0, held_ref[top, :], held_ref[bottom, :])


def join(where, own, group_l, group_r, gots_l, gots_r):
    out_shape = (shaped(WIN, COLS), shaped(CPART, COLS), shaped(8, COLS))
    return run(join_kernel, "join", out_shape, (where, own, group_l, group_r, gots_r[1], gots_l[1], gots_r[0], gots_l[0], gots_r[2], gots_l[2]))


def message_kernel(where_ref, source_ref, held_ref, rim_ref, *refs):
    out_ref = refs[-1]
    if len(refs) == 2:
        for a in range(2):
            for x in range(2):
                out_ref[pl.ds(WIN + 8 + a * WIN, WIN), x * ROWS : (x + 1) * ROWS] = refs[0][a, x]
    core, y, z = where_ref[0], where_ref[1], where_ref[2]
    chunk = core * 16 + y * 4 + z
    out_ref[pl.ds(0, WIN), :] = source_ref[...]

    def rows(which, start):
        kept = jnp.clip(which, 0, 31)
        index = place_of(y, z, (kept >> 2) & 3, kept & 3)
        here = pl.ds(pl.multiple_of(index * CHUNK + start, 8), 8)
        found = jnp.where((kept >> 4) == core, held_ref[here, :], rim_ref[...])
        return pltpu.roll(jnp.where(which == kept, found, 0.0), 4, 0)

    below = rows(chunk - 1, CHUNK - 8)
    above = rows(chunk + 1, 0)
    level = lax.broadcasted_iota(jnp.int32, (8, COLS), 0)
    out_ref[pl.ds(WIN, 8), :] = jnp.where(level < HALO, below, above)


def message(where, source, held, rim, *slab):
    size = (WIN + 8) + 2 * WIN * len(slab)
    return run(message_kernel, "message", shaped(size, COLS), (where, source, held, rim, *slab))


def relax_kernel(fresh, last, *refs):
    refs = list(refs)
    where_ref = refs.pop(0)
    pool = where_ref[3]
    message_refs = [refs.pop(0) for _ in range(4)]
    if not fresh:
        state_ref, gain_ref = refs.pop(0), refs.pop(0)
    if not last:
        state_out = refs.pop(0)
    own_out = refs.pop(0)
    if fresh:
        gain_ref = refs.pop(0)
    field_a, field_b, msgs, source = refs[:4]
    for k, ref in enumerate(message_refs):
        msgs[k] = ref[...]
    lanes = lax.broadcasted_iota(jnp.int32, (WIN, ROWS), 1)
    zeros = jnp.zeros((WIN + 16, ROWS), F32)
    edge = jnp.zeros((8, ROWS), F32)
    for field in (field_a, field_b):
        field[0] = zeros
        field[9] = zeros
        for x in range(8):
            field[x + 1, pl.ds(0, 8), :] = edge
            field[x + 1, pl.ds(WIN + 8, 8), :] = edge
    for p in range(4):
        near = lax.rem(pool - p + 4, 4)
        for i in range(2):
            x = 2 * p + i
            lane = pl.ds(i * ROWS, ROWS)
            if fresh:
                field_a[x + 1, pl.ds(8, WIN), :] = msgs[near, pl.ds(WIN + 8, WIN), lane]
                gain_ref[near, i] = msgs[near, pl.ds(2 * WIN + 8, WIN), lane]
            else:
                field_a[x + 1, pl.ds(8, WIN), :] = state_ref[near, i]
            field_a[x + 1, pl.ds(8, HALO), :] = msgs[near, pl.ds(WIN, HALO), lane]
            field_a[x + 1, pl.ds(8 + HALO + CHUNK, HALO), :] = msgs[near, pl.ds(WIN + HALO, HALO), lane]
            source[x] = SOURCE_GAIN * msgs[near, pl.ds(0, WIN), lane]
    def sweep(old, new):
        for p in range(4):
            near = lax.rem(pool - p + 4, 4)
            for i in range(2):
                x = 2 * p + i
                centre = old[x + 1, pl.ds(8, WIN), :]
                total = source[x] + old[x, pl.ds(8, WIN), :] + old[x + 2, pl.ds(8, WIN), :]
                total = total + old[x + 1, pl.ds(7, WIN), :] + old[x + 1, pl.ds(9, WIN), :]
                total = total + jnp.where(lanes == 0, 0.0, pltpu.roll(centre, 1, 1))
                total = total + jnp.where(lanes == ROWS - 1, 0.0, pltpu.roll(centre, ROWS - 1, 1))
                new[x + 1, pl.ds(8, WIN), :] = (1.0 - RELAX_WEIGHT) * centre + gain_ref[near, i] * total

    def both(_, carry):
        sweep(field_a, field_b)
        sweep(field_b, field_a)
        return carry

    lax.fori_loop(0, SWEEPS // 2, both, 0)
    old = field_a
    if last:
        for i in range(2):
            flat = old[2 * pool + i + 1, pl.ds(8, WIN), :]
            refs[4][...] = jnp.zeros((ROWS, ROWS), F32)
            refs[4][pl.ds(0, WIN), :] = flat
            turned = refs[4][...].T
            for s in range(32):
                own_out[s, pl.ds(4 * i, 4), :] = turned[4 * s : 4 * s + 4, :]
        return
    for p in range(4):
        near = lax.rem(pool - p + 4, 4)
        for i in range(2):
            state_out[near, i] = old[2 * p + i + 1, pl.ds(8, WIN), :]
    for i in range(2):
        own_out[:, i * ROWS : (i + 1) * ROWS] = old[2 * pool + i + 1, pl.ds(8 + HALO, CHUNK), :]


def relax(last, where, msgs, *fields):
    fresh = not fields
    state = shaped(4, 2, WIN, ROWS)
    out_shape = (state, shaped(CHUNK, COLS)) + ((state,) if fresh else ())
    if last:
        out_shape = (shaped(32, 8, ROWS),)
    scratch = [
        pltpu.VMEM((10, WIN + 16, ROWS), F32),
        pltpu.VMEM((10, WIN + 16, ROWS), F32),
        pltpu.VMEM((4,) + msgs[0].shape, F32),
        pltpu.VMEM((8, WIN, ROWS), F32),
        pltpu.VMEM((ROWS, ROWS), F32),
    ]
    return run(functools.partial(relax_kernel, fresh, last), "relax", out_shape, (where, *msgs, *fields), scratch)


def chunk_parts(s):
    core, z, y = s % 2, (s // 2) % 4, s // 8
    return core * 16 + y * 4 + z


def open_kernel(
    where_ref, potential_hbm, reaction_hbm, spikes_hbm, out_ref,
    wide_ref, flags_ref, potential_ref, reaction_ref, spikes_ref, sems,
):
    pairs = ((potential_hbm, potential_ref), (reaction_hbm, reaction_ref), (spikes_hbm, spikes_ref))
    copies = [pltpu.make_async_copy(source, target, sems.at[i]) for i, (source, target) in enumerate(pairs)]
    for copy in copies:
        copy.start()
    wide_ref[...] = jnp.zeros((16, PTS + 256), F32)
    flags_ref[...] = jnp.zeros((16, 128), F32)
    for copy in copies:
        copy.wait()
    flags_ref[pl.ds(0, 2), 64 : 64 + STEPS] = spikes_ref[...].astype(F32)
    for row in range(4):
        for x in range(2):
            wide_ref[4 * x + row, pl.ds(128, PTS)] = potential_ref[row, x, :]
            wide_ref[8 + 4 * x + row, pl.ds(128, PTS)] = RELAX_WEIGHT / (6.0 + reaction_ref[row, x, :])
    lanes = lax.broadcasted_iota(jnp.int32, (16, 128), 1)
    for s in range(32):
        window = wide_ref[:, pl.ds(128 + CHUNK * chunk_parts(s) - HALO, 128)]
        out_ref[s] = jnp.where(lanes < 64, window, flags_ref[...])


def open_pack(where, potential, reaction, spikes):
    return run(
        open_kernel,
        "open_pack",
        shaped(32, 16, 128),
        (where, in_hbm(potential), in_hbm(reaction), in_hbm(spikes)),
        [
            pltpu.VMEM((16, PTS + 256), F32),
            pltpu.VMEM((16, 128), F32),
            pltpu.VMEM((4, 2, PTS), F32),
            pltpu.VMEM((4, 2, PTS), F32),
            pltpu.VMEM((2, STEPS), jnp.int32),
            pltpu.SemaphoreType.DMA((3,)),
        ],
        outside=(1, 2, 3),
    )


def slab_kernel(where_ref, got_ref, out_ref, piece_ref, square_ref):
    for a in range(2):
        for x in range(2):
            for s in range(32):
                square_ref[pl.ds(4 * s, 4), :] = got_ref[s, pl.ds(8 * a + 4 * x, 4), :]
            turned = square_ref[...].T
            out_ref[a, x] = turned[:WIN, :]
            if a == 0:
                piece_ref[:, x * ROWS : (x + 1) * ROWS] = turned[HALO : HALO + CHUNK, :]


def slab_unpack(where, got):
    out_shape = (shaped(2, 2, WIN, ROWS), shaped(CHUNK, COLS))
    return run(slab_kernel, "slab", out_shape, (where, got), [pltpu.VMEM((ROWS, ROWS), F32)])


def close_kernel(where_ref, got_ref, out_ref, wide_ref):
    for s in range(32):
        part = got_ref[s]
        wide_ref[:, pl.ds(CHUNK * chunk_parts(s), CHUNK)] = part[:, HALO : HALO + CHUNK]
    for row in range(4):
        for x in range(2):
            out_ref[row, x, :] = wide_ref[4 * x + row, :]


def close(where, got):
    return run(close_kernel, "close", shaped(4, 2, PTS), (where, got), [pltpu.VMEM((8, PTS), F32)])


def fib_of(y, z, core):
    return (y * 4 + z) * 2 + core


def shift(x, axis, by=1):
    if axis == "pool":
        return lax.ppermute(x, "pool", [(i, (i + by) % 4) for i in range(4)])
    pairs = []
    for y in range(4):
        for z in range(4):
            for core in range(2):
                to = {
                    "y": ((y + by) % 4, z, core),
                    "z": (y, (z + by) % 4, core),
                    "core": (y, z, 1 - core),
                }[axis]
                pairs.append((fib_of(y, z, core), fib_of(*to)))
    return lax.ppermute(x, "fib", pairs)


def to_three(parts, axis, more=(), other=None):
    both = {}
    for k in (2, 1, 3):
        both[k] = shift(parts[k - 1], axis, k)
        if other:
            both[-k] = shift(more[k - 1], other, k)
    first = [both[k] for k in (1, 2, 3)]
    return (first, [both[-k] for k in (1, 2, 3)]) if other else first


def on_device(vm_state, recovery, spikes, owner, junction, column_index, cable_inverse, reaction, potential):
    fib = lax.axis_index("fib")
    pool = lax.axis_index("pool")
    core, z, y = fib % 2, (fib // 2) % 4, fib // 8
    where = jnp.stack([core, y, z, pool]).astype(jnp.int32)

    got = lax.all_to_all(open_pack(where, potential, reaction, spikes), "fib", 0, 0, tiled=True)
    table = jnp.concatenate([column_index, owner[:, None], junction[:, None]], axis=1).astype(F32)
    slab, piece = slab_unpack(where, got)
    base, following, fire, keep, send = first_call(where, vm_state, recovery, table, got)
    parts = {}

    def step(number, base, following, fire, keep, send, piece, state):
        mine_l, mine_r, loads_l, loads_r = first_pack(where, keep, shift(send, "core"), piece)
        gots_l, gots_r = to_three(loads_l, "y", loads_r, "z")
        last = number == STEPS - 1
        if number == 0:
            cable, mine_l = lax.optimization_barrier((cable_inverse, mine_l))
            high, low = cable_parts(cable)
            mine_l, high, low = lax.optimization_barrier((mine_l, high, low))
            parts.update(high=high, low=low)
        high, low = parts["high"], parts["low"]
        own, group_l, group_r, loads_l, loads_r = second_pack(where, mine_l, mine_r, piece, gots_l, gots_r)
        gots_l, gots_r = to_three(loads_l, "z", loads_r, "y")
        source, held, rim = join(where, own, group_l, group_r, gots_l, gots_r)
        rim, sent = lax.optimization_barrier((shift(rim, "core"), held))
        other = shift(sent, "core")
        note = message(where, source, held, rim, *([] if number else [slab]))
        msgs = to_three([note] * 3, "pool")
        other, note = lax.optimization_barrier((other, note))
        out = step_call(last, where, held, other, base, following, table, fire, high, low)
        *out, one, two, three = lax.optimization_barrier((*out, *msgs))
        relaxed = relax(last, where, [note, one, two, three], *([state, parts["gain"]] if number else []))
        if number == 0:
            parts.update(gain=relaxed[2])
        if last:
            return out[0], relaxed[0]
        return (*out, relaxed[1], relaxed[0])

    carry = (base, following, fire, keep, send, piece, None)
    for number in range(STEPS - 1):
        carry = step(number, *carry)
    membrane, closing = step(STEPS - 1, *carry)
    recovering = carry[1]
    extracell = close(where, lax.all_to_all(closing, "fib", 0, 0, tiled=True))
    return membrane, recovering, extracell


def solution(mesh):
    split_rows = P(("pool", "fib"), None)
    grid = P("fib", "pool", None)
    flat = P(("pool", "fib"))
    in_specs = (split_rows, split_rows, split_rows, flat, flat, split_rows, P(), grid, grid)
    return jax.shard_map(
        on_device, mesh=mesh, in_specs=in_specs, out_specs=(split_rows, split_rows, grid), check_vma=False
    )
```

```python
import functools

import jax
import jax.numpy as jnp
from jax import lax
from jax.experimental import pallas as pl
from jax.experimental.pallas import tpu as pltpu
from jax.sharding import PartitionSpec as P

STEPS = 4
SWEEPS = 4
TIME_STEP = 0.05
RECOVERY_RATE = 0.5
RECOVERY_SHIFT = 0.7
RECOVERY_SLOPE = 0.8
STIMULUS_GAIN = 4.0
JUNCTION_SPREAD = 8.0
SOURCE_GAIN = 0.25
RELAX_WEIGHT = 0.8

PTS = 1536
NBLK = 12
BLK = 128
FIB = 256
COLS = 256
ROWS = 128
CHUNK = 48
HALO = 4
WIN = CHUNK + 2 * HALO
YPART = 4 * CHUNK
CPART = 16 * CHUNK
YWIN = YPART + 2 * HALO
HALF = CPART + 2 * HALO
LOAD = YWIN + CHUNK
TILE = 256
TABLE = NBLK + 2
UNROLL = 12
PRODUCTS = 6
F32 = jnp.float32
BF16 = jnp.bfloat16
VMEM = pl.BlockSpec(memory_space=pltpu.VMEM)
SMEM = pl.BlockSpec(memory_space=pltpu.SMEM)
FAR = pl.BlockSpec(memory_space=pltpu.HBM)


def in_hbm(x):
    return pltpu.with_memory_space_constraint(x, pltpu.HBM)


def shaped(*dims, dtype=F32):
    return jax.ShapeDtypeStruct(dims, dtype)


def run(kernel, name, out_shape, operands, scratch=(), flops=1 << 20, moved=1 << 20, megabytes=4, outside=()):
    return pl.pallas_call(
        kernel,
        name=name,
        out_shape=out_shape,
        in_specs=[SMEM] + [FAR if i in outside else VMEM for i in range(1, len(operands))],
        out_specs=jax.tree.map(lambda _: VMEM, out_shape),
        scratch_shapes=scratch,
        cost_estimate=pl.CostEstimate(flops=flops, bytes_accessed=moved, transcendentals=0),
        compiler_params=pltpu.CompilerParams(vmem_limit_bytes=megabytes << 20),
    )(*operands)


def split(x):
    high = x.astype(BF16)
    return high, (x - high.astype(F32)).astype(BF16)


def dot(a, b, dims=((1,), (0,))):
    return lax.dot_general(a, b, (dims, ((), ())), preferred_element_type=F32)


def one_hot(column, width):
    lanes = lax.broadcasted_iota(jnp.int32, (column.shape[0], width), 1)
    return jnp.where(column == lanes, 1.0, 0.0).astype(BF16)


def advance(m, r, fire, place, start):
    width = m.shape[1]
    at = (lax.broadcasted_iota(jnp.int32, (1, width), 1) + start).astype(F32)
    offsets = (at - place) * (1.0 / JUNCTION_SPREAD)
    wave = jnp.exp(-offsets * offsets)
    current = m - m * m * m * (1.0 / 3.0) - r + (STIMULUS_GAIN * fire) * wave
    base = m + TIME_STEP * current
    following = r + TIME_STEP * RECOVERY_RATE * (m + RECOVERY_SHIFT - RECOVERY_SLOPE * r)
    return current, base, following


def deposit(current, hot):
    high, low = split(current.T)
    return dot(high, hot) + dot(low, hot)


def clear_ends(sums_ref):
    zero = jnp.zeros((8, COLS), F32)
    sums_ref[pl.ds(0, 8), :] = zero
    sums_ref[pl.ds(8 + PTS, 8), :] = zero


def put_halves(where_ref, sums_ref, keep_ref, send_ref):
    for core in range(2):

        @pl.when(where_ref[0] == core)
        def _():
            keep_ref[...] = sums_ref[pl.ds(8 - HALO + CPART * core, HALF), :]
            send_ref[...] = sums_ref[pl.ds(8 - HALO + CPART * (1 - core), HALF), :]


SUMS = pltpu.VMEM((PTS + 16, COLS), F32)


def rows_at(start, size):
    return pl.ds(start if isinstance(start, int) else pl.multiple_of(start, 8), size)


def column_of(table_ref, index):
    if isinstance(index, int):
        return table_ref[:, index : index + 1].astype(jnp.int32)
    lanes = lax.broadcasted_iota(jnp.int32, (FIB, TABLE), 1)
    return jnp.sum(jnp.where(lanes == index, table_ref[...], 0.0), axis=1, keepdims=True).astype(jnp.int32)


def looped(count, inner, body):
    if inner == count:
        for k in range(count):
            body(k)
        return

    def several(i, carry):
        for k in range(inner):
            body(i * inner + k)
        return carry

    lax.fori_loop(0, count // inner, several, 0)


def block_at(b):
    if isinstance(b, int):
        return pl.ds(b * BLK, BLK)
    return pl.ds(pl.multiple_of(b * BLK, BLK), BLK)


def slab_column(index):
    return (index & 1) * ROWS + (index >> 1)


def first_kernel(
    where_ref, m_hbm, r_hbm, table_ref, got_ref, base_ref, next_ref, fire_ref, keep_ref, send_ref,
    sums_ref, trains_ref, m_ref, r_ref, sems,
):
    copies = []
    for t in range(PTS // TILE):
        here = pl.ds(t * TILE, TILE)
        for i, (source, target) in enumerate(((m_hbm, m_ref), (r_hbm, r_ref))):
            copy = pltpu.make_async_copy(source.at[:, here], target.at[:, here], sems.at[2 * t + i])
            copy.start()
            copies.append(copy)
    clear_ends(sums_ref)
    for s in range(32):
        trains_ref[pl.ds(2 * s, 2), :] = got_ref[s, pl.ds(0, 2), :]
    units = one_hot(table_ref[:, NBLK : NBLK + 1].astype(jnp.int32), 64)
    fires = dot(units, trains_ref[...].astype(BF16))[:, 64 : 64 + STEPS]
    fire_ref[...] = fires
    fire = fires[:, 0:1]
    place = table_ref[:, NBLK + 1 : NBLK + 2]

    for b in range(NBLK):
        if b % 2 == 0:
            copies[b].wait()
            copies[b + 1].wait()
        here = block_at(b)
        current, base, following = advance(m_ref[:, here], r_ref[:, here], fire, place, b * BLK)
        base_ref[:, here] = base
        next_ref[:, here] = following
        hot = one_hot(slab_column(column_of(table_ref, b)), COLS)
        sums_ref[rows_at(8 + b * BLK, BLK), :] = deposit(current, hot)
    put_halves(where_ref, sums_ref, keep_ref, send_ref)


def first_call(where, m, r, table, got):
    state = shaped(FIB, PTS)
    return run(
        first_kernel,
        "first_deposit",
        (state, state, shaped(FIB, STEPS), shaped(HALF, COLS), shaped(HALF, COLS)),
        (where, in_hbm(m), in_hbm(r), table, got),
        [
            SUMS,
            pltpu.VMEM((64, 128), F32),
            pltpu.VMEM((FIB, PTS), F32),
            pltpu.VMEM((FIB, PTS), F32),
            pltpu.SemaphoreType.DMA((NBLK,)),
        ],
        outside=(1, 2),
        flops=6 << 30,
        moved=12 << 20,
        megabytes=12,
    )


def step_kernel(last, *refs):
    where_ref, own_ref, other_ref, base_ref, next_ref, table_ref, fire_ref, high_ref, low_ref = refs[:9]
    if last:
        m_out, field_ref, rhs_high, rhs_low, hot_ref = refs[9:]
    else:
        base_out, next_out, fire_out, keep_ref, send_ref, field_ref, rhs_high, rhs_low, hot_ref, sums_ref, m_out = refs[9:]
    core, y, z = where_ref[0], where_ref[1], where_ref[2]

    for yy in range(4):
        for zz in range(4):
            first = rows_at(place_of(y, z, yy, zz) * CHUNK, CHUNK)
            for half, ref in ((core, own_ref), (1 - core, other_ref)):
                field_ref[rows_at(half * CPART + (4 * yy + zz) * CHUNK, CHUNK), :] = ref[first, :]

    def sample(b):
        here = block_at(b)
        hot = one_hot(slab_column(column_of(table_ref, b)), COLS)
        if not last:
            hot_ref[b] = hot
        high, low = split(field_ref[here, :])
        sampled = dot(hot, high, ((1,), (1,))) + dot(hot, low, ((1,), (1,)))
        high, low = split(base_ref[:, here] + TIME_STEP * sampled)
        rhs_high[:, here] = high
        rhs_low[:, here] = low

    looped(NBLK, UNROLL, sample)

    def product(t):
        here = pl.ds(t * TILE if isinstance(t, int) else pl.multiple_of(t * TILE, TILE), TILE)
        m_out[:, here] = (
            dot(rhs_high[...], high_ref[:, here])
            + dot(rhs_low[...], high_ref[:, here])
            + dot(rhs_high[...], low_ref[:, here])
        )

    looped(PTS // TILE, PRODUCTS, product)
    if last:
        return
    clear_ends(sums_ref)
    place = table_ref[:, NBLK + 1 : NBLK + 2]
    fire = fire_ref[:, 1:2]
    fire_out[:, : STEPS - 1] = fire_ref[:, 1:]
    fire_out[:, STEPS - 1 :] = fire_ref[:, :1]

    def block(b):
        here = block_at(b)
        current, base, following = advance(m_out[:, here], next_ref[:, here], fire, place, b * BLK)
        base_out[:, here] = base
        next_out[:, here] = following
        sums_ref[rows_at(8 + b * BLK, BLK), :] = deposit(current, hot_ref[b])

    looped(NBLK, UNROLL, block)
    put_halves(where_ref, sums_ref, keep_ref, send_ref)


def step_call(last, *operands):
    state = shaped(FIB, PTS)
    field = (PTS, COLS)
    scratch = [pltpu.VMEM(field, F32), pltpu.VMEM((FIB, PTS), BF16), pltpu.VMEM((FIB, PTS), BF16)]
    scratch += [pltpu.VMEM((NBLK, FIB, COLS), BF16)]
    if last:
        out_shape = (state,)
    else:
        out_shape = (state, state, shaped(FIB, STEPS), shaped(HALF, COLS), shaped(HALF, COLS))
        scratch += [SUMS, pltpu.VMEM((FIB, PTS), F32)]
    return run(
        functools.partial(step_kernel, last),
        "fibre_step",
        out_shape,
        operands,
        scratch,
        flops=2 * 3 * FIB * PTS * PTS,
        moved=20 << 20,
        megabytes=12,
    )


def parts_kernel(whole_ref, high_ref, low_ref):
    high, low = split(whole_ref[...])
    high_ref[...] = high
    low_ref[...] = low


def cable_parts(cable):
    rows = pl.BlockSpec((TILE, PTS), lambda i: (i, 0))
    return pl.pallas_call(
        parts_kernel,
        name="cable_parts",
        grid=(PTS // TILE,),
        out_shape=(shaped(PTS, PTS, dtype=BF16),) * 2,
        in_specs=[rows],
        out_specs=(rows, rows),
        cost_estimate=pl.CostEstimate(flops=1 << 23, bytes_accessed=18 << 20, transcendentals=0),
        compiler_params=pltpu.CompilerParams(vmem_limit_bytes=10 << 20),
    )(in_hbm(cable))


def place_of(y, z, yy, zz):
    return lax.rem(z - zz + 4, 4) * 4 + lax.rem(y - yy + 4, 4)


LEFT = slice(0, ROWS)
RIGHT = slice(ROWS, COLS)
FOUR = 4 * WIN


def first_pack_kernel(where_ref, keep_ref, got_ref, piece_ref, mine_l, mine_r, *outs):
    y, z = where_ref[1], where_ref[2]
    for k, out in enumerate((mine_l,) + outs[:3]):
        here = rows_at(lax.rem(y + k, 4) * YPART, YWIN)
        out[pl.ds(0, YWIN), :] = keep_ref[here, LEFT] + got_ref[here, LEFT]
        if k:
            out[pl.ds(YWIN, CHUNK), :] = piece_ref[:, LEFT]
    for k, out in enumerate((mine_r,) + outs[3:]):
        for yy in range(4):
            here = rows_at(yy * YPART + lax.rem(z + k, 4) * CHUNK, WIN)
            out[pl.ds(yy * WIN, WIN), :] = keep_ref[here, RIGHT] + got_ref[here, RIGHT]
        if k:
            out[pl.ds(FOUR, CHUNK), :] = piece_ref[:, RIGHT]


def first_pack(where, keep, got, piece):
    out = (shaped(YWIN, ROWS), shaped(FOUR, ROWS)) + (shaped(YWIN + CHUNK, ROWS),) * 3 + (shaped(FOUR + CHUNK, ROWS),) * 3
    mine_l, mine_r, *loads = run(first_pack_kernel, "first_pack", out, (where, keep, got, piece))
    return mine_l, mine_r, loads[:3], loads[3:]


def second_pack_kernel(where_ref, mine_l, mine_r, piece_ref, r2, l2, r3, l3, r1, l1, own_ref, group_l, group_r, *outs):
    y, z = where_ref[1], where_ref[2]
    for side, group, size, gots in ((LEFT, group_l, YWIN, (l1, l2, l3)), (RIGHT, group_r, FOUR, (r1, r2, r3))):
        parts = [piece_ref[:, side]] + [got[pl.ds(size, CHUNK), :] for got in gots]
        for i, part in enumerate(parts):
            group[pl.ds(i * CHUNK, CHUNK), :] = part
    for k in range(4):
        here = rows_at(lax.rem(z + k, 4) * CHUNK, WIN)
        left = mine_l[here, :] + l1[here, :] + l3[here, :] + l2[here, :]
        here = rows_at(lax.rem(y + k, 4) * WIN, WIN)
        right = mine_r[here, :] + r1[here, :] + r3[here, :] + r2[here, :]
        if k == 0:
            own_ref[:, LEFT] = left
            own_ref[:, RIGHT] = right
        else:
            outs[k - 1][pl.ds(0, WIN), :] = left
            outs[k - 1][pl.ds(WIN, YPART), :] = group_l[...]
            outs[k + 2][pl.ds(0, WIN), :] = right
            outs[k + 2][pl.ds(WIN, YPART), :] = group_r[...]


def second_pack(where, mine_l, mine_r, piece, gots_l, gots_r):
    group = shaped(YPART, ROWS)
    out = (shaped(WIN, COLS), group, group) + (shaped(WIN + YPART, ROWS),) * 6
    own, group_l, group_r, *loads = run(
        second_pack_kernel, "second_pack", out, (where, mine_l, mine_r, piece, gots_r[1], gots_l[1], gots_r[2], gots_l[2], gots_r[0], gots_l[0])
    )
    return own, group_l, group_r, loads[:3], loads[3:]


def join_kernel(where_ref, own_ref, group_l, group_r, r2, l2, r3, l3, r1, l1, source_ref, held_ref, rim_ref):
    core, y, z = where_ref[0], where_ref[1], where_ref[2]
    here = pl.ds(0, WIN)
    source_ref[:, LEFT] = own_ref[:, LEFT] + l1[here, :] + l3[here, :] + l2[here, :]
    source_ref[:, RIGHT] = own_ref[:, RIGHT] + r1[here, :] + r3[here, :] + r2[here, :]
    held_ref[pl.ds(0, YPART), LEFT] = group_l[...]
    for k, got in enumerate((l1, l2, l3)):
        held_ref[pl.ds((k + 1) * YPART, YPART), LEFT] = got[pl.ds(WIN, YPART), :]
    for i in range(4):
        held_ref[pl.ds(i * YPART, CHUNK), RIGHT] = group_r[pl.ds(i * CHUNK, CHUNK), :]
        for k, got in enumerate((r1, r2, r3)):
            held_ref[pl.ds(i * YPART + (k + 1) * CHUNK, CHUNK), RIGHT] = got[pl.ds(WIN + i * CHUNK, CHUNK), :]
    top = rows_at(place_of(y, z, 3, 3) * CHUNK + CHUNK - 8, 8)
    bottom = rows_at(place_of(y, z, 0, 0) * CHUNK, 8)
    rim_ref[...] = jnp.where(core == 0, held_ref[top, :], held_ref[bottom, :])


def join(where, own, group_l, group_r, gots_l, gots_r):
    out_shape = (shaped(WIN, COLS), shaped(CPART, COLS), shaped(8, COLS))
    return run(join_kernel, "join", out_shape, (where, own, group_l, group_r, gots_r[1], gots_l[1], gots_r[2], gots_l[2], gots_r[0], gots_l[0]))


def message_kernel(where_ref, source_ref, held_ref, rim_ref, *refs):
    out_ref = refs[-1]
    if len(refs) == 2:
        for a in range(2):
            for x in range(2):
                out_ref[pl.ds(WIN + 8 + a * WIN, WIN), x * ROWS : (x + 1) * ROWS] = refs[0][a, x]
    core, y, z = where_ref[0], where_ref[1], where_ref[2]
    chunk = core * 16 + y * 4 + z
    out_ref[pl.ds(0, WIN), :] = source_ref[...]

    def rows(which, start):
        kept = jnp.clip(which, 0, 31)
        index = place_of(y, z, (kept >> 2) & 3, kept & 3)
        here = pl.ds(pl.multiple_of(index * CHUNK + start, 8), 8)
        found = jnp.where((kept >> 4) == core, held_ref[here, :], rim_ref[...])
        return pltpu.roll(jnp.where(which == kept, found, 0.0), 4, 0)

    below = rows(chunk - 1, CHUNK - 8)
    above = rows(chunk + 1, 0)
    level = lax.broadcasted_iota(jnp.int32, (8, COLS), 0)
    out_ref[pl.ds(WIN, 8), :] = jnp.where(level < HALO, below, above)


def message(where, source, held, rim, *slab):
    size = (WIN + 8) + 2 * WIN * len(slab)
    return run(message_kernel, "message", shaped(size, COLS), (where, source, held, rim, *slab))


def relax_kernel(fresh, last, *refs):
    refs = list(refs)
    where_ref = refs.pop(0)
    pool = where_ref[3]
    message_refs = [refs.pop(0) for _ in range(4)]
    if not fresh:
        state_ref, gain_ref = refs.pop(0), refs.pop(0)
    if not last:
        state_out = refs.pop(0)
    own_out = refs.pop(0)
    if fresh:
        gain_ref = refs.pop(0)
    field_a, field_b, msgs, source = refs[:4]
    for k, ref in enumerate(message_refs):
        msgs[k] = ref[...]
    lanes = lax.broadcasted_iota(jnp.int32, (WIN, ROWS), 1)
    zeros = jnp.zeros((WIN + 16, ROWS), F32)
    edge = jnp.zeros((8, ROWS), F32)
    for field in (field_a, field_b):
        field[0] = zeros
        field[9] = zeros
        for x in range(8):
            field[x + 1, pl.ds(0, 8), :] = edge
            field[x + 1, pl.ds(WIN + 8, 8), :] = edge
    for p in range(4):
        near = lax.rem(pool - p + 4, 4)
        for i in range(2):
            x = 2 * p + i
            lane = pl.ds(i * ROWS, ROWS)
            if fresh:
                field_a[x + 1, pl.ds(8, WIN), :] = msgs[near, pl.ds(WIN + 8, WIN), lane]
                gain_ref[near, i] = msgs[near, pl.ds(2 * WIN + 8, WIN), lane]
            else:
                field_a[x + 1, pl.ds(8, WIN), :] = state_ref[near, i]
            field_a[x + 1, pl.ds(8, HALO), :] = msgs[near, pl.ds(WIN, HALO), lane]
            field_a[x + 1, pl.ds(8 + HALO + CHUNK, HALO), :] = msgs[near, pl.ds(WIN + HALO, HALO), lane]
            source[x] = SOURCE_GAIN * msgs[near, pl.ds(0, WIN), lane]
    def sweep(old, new):
        for p in range(4):
            near = lax.rem(pool - p + 4, 4)
            for i in range(2):
                x = 2 * p + i
                centre = old[x + 1, pl.ds(8, WIN), :]
                total = source[x] + old[x, pl.ds(8, WIN), :] + old[x + 2, pl.ds(8, WIN), :]
                total = total + old[x + 1, pl.ds(7, WIN), :] + old[x + 1, pl.ds(9, WIN), :]
                total = total + jnp.where(lanes == 0, 0.0, pltpu.roll(centre, 1, 1))
                total = total + jnp.where(lanes == ROWS - 1, 0.0, pltpu.roll(centre, ROWS - 1, 1))
                new[x + 1, pl.ds(8, WIN), :] = (1.0 - RELAX_WEIGHT) * centre + gain_ref[near, i] * total

    def both(_, carry):
        sweep(field_a, field_b)
        sweep(field_b, field_a)
        return carry

    lax.fori_loop(0, SWEEPS // 2, both, 0)
    old = field_a
    if last:
        for i in range(2):
            flat = old[2 * pool + i + 1, pl.ds(8, WIN), :]
            refs[4][...] = jnp.zeros((ROWS, ROWS), F32)
            refs[4][pl.ds(0, WIN), :] = flat
            turned = refs[4][...].T
            for s in range(32):
                own_out[s, pl.ds(4 * i, 4), :] = turned[4 * s : 4 * s + 4, :]
        return
    for p in range(4):
        near = lax.rem(pool - p + 4, 4)
        for i in range(2):
            state_out[near, i] = old[2 * p + i + 1, pl.ds(8, WIN), :]
    for i in range(2):
        own_out[:, i * ROWS : (i + 1) * ROWS] = old[2 * pool + i + 1, pl.ds(8 + HALO, CHUNK), :]


def relax(last, where, msgs, *fields):
    fresh = not fields
    state = shaped(4, 2, WIN, ROWS)
    out_shape = (state, shaped(CHUNK, COLS)) + ((state,) if fresh else ())
    if last:
        out_shape = (shaped(32, 8, ROWS),)
    scratch = [
        pltpu.VMEM((10, WIN + 16, ROWS), F32),
        pltpu.VMEM((10, WIN + 16, ROWS), F32),
        pltpu.VMEM((4,) + msgs[0].shape, F32),
        pltpu.VMEM((8, WIN, ROWS), F32),
        pltpu.VMEM((ROWS, ROWS), F32),
    ]
    return run(functools.partial(relax_kernel, fresh, last), "relax", out_shape, (where, *msgs, *fields), scratch)


def chunk_parts(s):
    core, z, y = s % 2, (s // 2) % 4, s // 8
    return core * 16 + y * 4 + z


def open_kernel(
    where_ref, potential_hbm, reaction_hbm, spikes_hbm, out_ref,
    wide_ref, flags_ref, potential_ref, reaction_ref, spikes_ref, sems,
):
    pairs = ((potential_hbm, potential_ref), (reaction_hbm, reaction_ref), (spikes_hbm, spikes_ref))
    copies = [pltpu.make_async_copy(source, target, sems.at[i]) for i, (source, target) in enumerate(pairs)]
    for copy in copies:
        copy.start()
    wide_ref[...] = jnp.zeros((16, PTS + 256), F32)
    flags_ref[...] = jnp.zeros((16, 128), F32)
    for copy in copies:
        copy.wait()
    flags_ref[pl.ds(0, 2), 64 : 64 + STEPS] = spikes_ref[...].astype(F32)
    for row in range(4):
        for x in range(2):
            wide_ref[4 * x + row, pl.ds(128, PTS)] = potential_ref[row, x, :]
            wide_ref[8 + 4 * x + row, pl.ds(128, PTS)] = RELAX_WEIGHT / (6.0 + reaction_ref[row, x, :])
    lanes = lax.broadcasted_iota(jnp.int32, (16, 128), 1)
    for s in range(32):
        window = wide_ref[:, pl.ds(128 + CHUNK * chunk_parts(s) - HALO, 128)]
        out_ref[s] = jnp.where(lanes < 64, window, flags_ref[...])


def open_pack(where, potential, reaction, spikes):
    return run(
        open_kernel,
        "open_pack",
        shaped(32, 16, 128),
        (where, in_hbm(potential), in_hbm(reaction), in_hbm(spikes)),
        [
            pltpu.VMEM((16, PTS + 256), F32),
            pltpu.VMEM((16, 128), F32),
            pltpu.VMEM((4, 2, PTS), F32),
            pltpu.VMEM((4, 2, PTS), F32),
            pltpu.VMEM((2, STEPS), jnp.int32),
            pltpu.SemaphoreType.DMA((3,)),
        ],
        outside=(1, 2, 3),
    )


def slab_kernel(where_ref, got_ref, out_ref, piece_ref, square_ref):
    for a in range(2):
        for x in range(2):
            for s in range(32):
                square_ref[pl.ds(4 * s, 4), :] = got_ref[s, pl.ds(8 * a + 4 * x, 4), :]
            turned = square_ref[...].T
            out_ref[a, x] = turned[:WIN, :]
            if a == 0:
                piece_ref[:, x * ROWS : (x + 1) * ROWS] = turned[HALO : HALO + CHUNK, :]


def slab_unpack(where, got):
    out_shape = (shaped(2, 2, WIN, ROWS), shaped(CHUNK, COLS))
    return run(slab_kernel, "slab", out_shape, (where, got), [pltpu.VMEM((ROWS, ROWS), F32)])


def close_kernel(where_ref, got_ref, out_ref, wide_ref):
    for s in range(32):
        part = got_ref[s]
        wide_ref[:, pl.ds(CHUNK * chunk_parts(s), CHUNK)] = part[:, HALO : HALO + CHUNK]
    for row in range(4):
        for x in range(2):
            out_ref[row, x, :] = wide_ref[4 * x + row, :]


def close(where, got):
    return run(close_kernel, "close", shaped(4, 2, PTS), (where, got), [pltpu.VMEM((8, PTS), F32)])


def fib_of(y, z, core):
    return (y * 4 + z) * 2 + core


def shift(x, axis, by=1):
    if axis == "pool":
        return lax.ppermute(x, "pool", [(i, (i + by) % 4) for i in range(4)])
    pairs = []
    for y in range(4):
        for z in range(4):
            for core in range(2):
                to = {
                    "y": ((y + by) % 4, z, core),
                    "z": (y, (z + by) % 4, core),
                    "core": (y, z, 1 - core),
                }[axis]
                pairs.append((fib_of(y, z, core), fib_of(*to)))
    return lax.ppermute(x, "fib", pairs)


def to_three(parts, axis, more=(), other=None):
    both = {}
    for k in (2, 1, 3):
        both[k] = shift(parts[k - 1], axis, k)
        if other:
            both[-k] = shift(more[k - 1], other, k)
    first = [both[k] for k in (1, 2, 3)]
    return (first, [both[-k] for k in (1, 2, 3)]) if other else first


def on_device(vm_state, recovery, spikes, owner, junction, column_index, cable_inverse, reaction, potential):
    fib = lax.axis_index("fib")
    pool = lax.axis_index("pool")
    core, z, y = fib % 2, (fib // 2) % 4, fib // 8
    where = jnp.stack([core, y, z, pool]).astype(jnp.int32)

    got = lax.all_to_all(open_pack(where, potential, reaction, spikes), "fib", 0, 0, tiled=True)
    table = jnp.concatenate([column_index, owner[:, None], junction[:, None]], axis=1).astype(F32)
    slab, piece = slab_unpack(where, got)
    base, following, fire, keep, send = first_call(where, vm_state, recovery, table, got)
    parts = {}

    def step(number, base, following, fire, keep, send, piece, state):
        mine_l, mine_r, loads_l, loads_r = first_pack(where, keep, shift(send, "core"), piece)
        gots_l, gots_r = to_three(loads_l, "y", loads_r, "z")
        last = number == STEPS - 1
        if number == 0:
            cable, mine_l = lax.optimization_barrier((cable_inverse, mine_l))
            high, low = cable_parts(cable)
            mine_l, high, low = lax.optimization_barrier((mine_l, high, low))
            parts.update(high=high, low=low)
        high, low = parts["high"], parts["low"]
        own, group_l, group_r, loads_l, loads_r = second_pack(where, mine_l, mine_r, piece, gots_l, gots_r)
        gots_l, gots_r = to_three(loads_l, "z", loads_r, "y")
        source, held, rim = join(where, own, group_l, group_r, gots_l, gots_r)
        rim, sent = lax.optimization_barrier((shift(rim, "core"), held))
        other = shift(sent, "core")
        note = message(where, source, held, rim, *([] if number else [slab]))
        msgs = to_three([note] * 3, "pool")
        other, note = lax.optimization_barrier((other, note))
        out = step_call(last, where, held, other, base, following, table, fire, high, low)
        *out, one, two, three = lax.optimization_barrier((*out, *msgs))
        relaxed = relax(last, where, [note, one, two, three], *([state, parts["gain"]] if number else []))
        if number == 0:
            parts.update(gain=relaxed[2])
        if last:
            return out[0], relaxed[0]
        return (*out, relaxed[1], relaxed[0])

    carry = (base, following, fire, keep, send, piece, None)
    for number in range(STEPS - 1):
        carry = step(number, *carry)
    membrane, closing = step(STEPS - 1, *carry)
    recovering = carry[1]
    extracell = close(where, lax.all_to_all(closing, "fib", 0, 0, tiled=True))
    return membrane, recovering, extracell


def solution(mesh):
    split_rows = P(("pool", "fib"), None)
    grid = P("fib", "pool", None)
    flat = P(("pool", "fib"))
    in_specs = (split_rows, split_rows, split_rows, flat, flat, split_rows, P(), grid, grid)
    return jax.shard_map(
        on_device, mesh=mesh, in_specs=in_specs, out_specs=(split_rows, split_rows, grid), check_vma=False
    )
```
